32 devices in a mesh: loop: 4 (over y, core), inner: 8 (over z, x).
Axes of the slice: x: 2, y: 2, z: 4, core: 2. Of those that a mesh axis runs over, the one named last changes fastest.
Arguments:
- snapshots: bfloat16 [8192, 1024], P(('loop', 'inner')), may hold values from -6 to 6
- bins: int32 [8192], replicated, may hold values from 0 to 63, as said below
- pairs: int32 [256, 2], replicated, may hold values from 0 to 63, as said below
- start_weights: bfloat16 [1024, 32], replicated, may hold values from -0.1875 to 0.1875
Outputs:
- basis: float32 [8192, 96], P(('loop', 'inner'))
- coefficients: float32 [4, 32, 32], replicated
The draws below stay inside these ranges and needn't reach their ends.
Inputs may be any that keep to these rules, and one draw needn't show every extreme that they name: `bins`: the snapshot in row n has a bin in [r * 8, (r + 1) * 8), where r = (n // 256) mod (8). `pairs`: every row (a, b) has a <= b <= a + 8; every bin is paired with itself.
All inputs are finite; a program needn't handle non-finite values.
Results may differ from the reference program's by a relative error of at most 0.0003.
Values may be sent and summed in bfloat16 or wider, within the bound.
No kernel may reach another device: no remote copies, remote signals or barrier semaphores. Data moves between devices by JAX's collectives and lax.ppermute only.
A program may use at most 64 MiB of HBM per device.

```python
import jax
import jax.numpy as jnp
from jax import lax

FEATURES = 1024
BLOCK = 32
STEPS = 2
BINS_COL = 8
LINKS = 4
ROWS_DEV = 256
SNAPSHOTS = 8192
NBINS = 64
PAIRS = 256
N_LOOP = 4
N_INNER = 8


def draw_bins(key, part):
    index = jnp.arange(SNAPSHOTS, dtype=jnp.int32)
    column = index // ROWS_DEV % (NBINS // BINS_COL)
    within = index % ROWS_DEV
    first_key = jax.random.fold_in(key, 11)
    second_key = jax.random.fold_in(key, 12)
    first_pick = jax.random.randint(first_key, (SNAPSHOTS,), 0, BINS_COL, dtype=jnp.int32)
    second_pick = jax.random.randint(second_key, (SNAPSHOTS,), 0, BINS_COL, dtype=jnp.int32)
    offset = jnp.minimum(first_pick, second_pick)
    offset = jnp.where(within == 0, 0, jnp.where(within == ROWS_DEV - 1, BINS_COL - 1, offset))
    return (column * BINS_COL + offset).astype(jnp.int32)


def draw_pairs(key, part):
    index = jnp.arange(PAIRS, dtype=jnp.int32)
    anchor = index // LINKS
    link_index = index % LINKS
    offset = jax.random.randint(jax.random.fold_in(key, 21), (PAIRS,), 1, BINS_COL + 1, dtype=jnp.int32)
    offset = jnp.where(link_index == 0, 0, offset)
    target = jnp.minimum(anchor + offset, NBINS - 1)
    return jnp.stack([anchor, target], axis=1).astype(jnp.int32)


def block_levels(stream_key, extent, pieces, low, top_value):
    def one(dim, parts):
        draws = jax.random.uniform(jax.random.fold_in(jax.random.fold_in(stream_key, 6), dim), (parts,), jnp.float32, low / len(pieces), top_value / len(pieces))
        return jnp.repeat(jnp.exp(draws), extent[dim] // parts).reshape((-1,) + (1,) * (len(extent) - dim - 1))

    gain = one(*pieces[0])
    for cut in pieces[1:]:
        gain = gain * one(*cut)
    return gain


def normal_values(stream_key, shape, deviation, bound, shards=(), kind=jnp.bfloat16):
    entries = jax.random.normal(stream_key, shape, jnp.float32) * deviation
    if len(shards) > 0:
        entries = block_levels(stream_key, shape, shards, -0.22, 0.18) * entries
    return jnp.clip(entries, min=-bound, max=bound).astype(kind)


def setup_inputs(seed: int = 0) -> dict:
    key_of = jax.random.split(jax.random.key(seed), 5)
    snapshots = normal_values(key_of[0], (SNAPSHOTS, FEATURES), 1.0, 6.0, ((0, 32),))
    bins = draw_bins(jax.random.fold_in(key_of[4], 71), 0)
    pairs = draw_pairs(jax.random.fold_in(key_of[4], 71), 0)
    start_weights = normal_values(key_of[3], (FEATURES, BLOCK), FEATURES ** -0.5, 0.1875)
    return {"snapshots": snapshots, "bins": bins, "pairs": pairs, "start_weights": start_weights}


def gram_matrix(left, right):
    return jnp.dot(left.T, right, precision=lax.Precision.HIGHEST)

def orthonormal(matrix):
    lower_factor = jnp.linalg.cholesky(gram_matrix(matrix, matrix))
    result = lax.linalg.triangular_solve(lower_factor, matrix, left_side=False, lower=True, transpose_a=True)
    return (result, lower_factor.T)

def reference(snapshots, bins, pairs, start_weights):
    adjacency = jnp.zeros((NBINS, NBINS), jnp.float32)
    adjacency = adjacency.at[pairs[:, 0], pairs[:, 1]].set(1.0).at[pairs[:, 1], pairs[:, 0]].set(1.0)
    grid = snapshots.reshape(N_LOOP, N_INNER, ROWS_DEV, FEATURES)
    padded = jnp.pad(grid, ((0, 0), (1, 1), (0, 0), (0, 0)))
    bin_grid = jnp.pad(bins.reshape(N_LOOP, N_INNER, ROWS_DEV), ((0, 0), (1, 1), (0, 0)), constant_values=-1)
    epsilon = FEATURES / 3.0
    columns = jnp.arange(N_INNER, dtype=jnp.int32)

    def column_kernel(column):
        mine = lax.dynamic_index_in_dim(padded, column + 1, 1, keepdims=False).reshape(N_LOOP * ROWS_DEV, FEATURES)
        partner = lax.dynamic_slice_in_dim(padded, column, 3, 1).reshape(N_LOOP * 3 * ROWS_DEV, FEATURES)
        my_bins = lax.dynamic_index_in_dim(bin_grid, column + 1, 1, keepdims=False).reshape(-1)
        part_bins = lax.dynamic_slice_in_dim(bin_grid, column, 3, 1).reshape(-1)
        valid = (part_bins >= 0).astype(jnp.float32)
        linked = adjacency[my_bins][:, jnp.maximum(part_bins, 0)] * valid[None, :]
        mine_wide = mine.astype(jnp.float32)
        part_wide = partner.astype(jnp.float32)
        mine_norms = lax.optimization_barrier(jnp.sum(mine_wide * mine_wide, axis=1))
        part_norms = lax.optimization_barrier(jnp.sum(part_wide * part_wide, axis=1))
        products = jnp.dot(mine_wide, part_wide.T, precision=lax.Precision.HIGHEST)
        distance = mine_norms[:, None] + part_norms[None, :] - 2.0 * products
        return linked * jnp.exp(-distance / epsilon)

    def regroup(stacked):
        width = stacked.shape[-1]
        return stacked.reshape(N_INNER, N_LOOP, ROWS_DEV, width).transpose(1, 0, 2, 3).reshape(-1, width)

    def degree_column(column):
        return lax.optimization_barrier(jnp.sum(column_kernel(column), axis=1))[:, None]
    degree = regroup(lax.map(degree_column, columns))[:, 0]
    inv_root = lax.rsqrt(degree)

    def apply_kernel(vectors):
        width = vectors.shape[1]
        vec_pad = jnp.pad(vectors.reshape(N_LOOP, N_INNER, ROWS_DEV, width), ((0, 0), (1, 1), (0, 0), (0, 0)))

        def one_column(column):
            partner = lax.dynamic_slice_in_dim(vec_pad, column, 3, 1).reshape(N_LOOP * 3 * ROWS_DEV, width)
            return jnp.dot(column_kernel(column), partner, precision=lax.Precision.HIGHEST)
        return regroup(lax.map(one_column, columns))
    start_block = jnp.dot(snapshots.astype(jnp.float32), start_weights.astype(jnp.float32), preferred_element_type=jnp.float32)
    current, unused = orthonormal(start_block)
    basis_blocks = [current]
    coefficients = []
    previous = current
    prev_b = jnp.zeros((BLOCK, BLOCK), jnp.float32)
    for lanczos_step in range(STEPS):
        image = inv_root[:, None] * apply_kernel(inv_root[:, None] * current)
        projected = gram_matrix(current, image)
        image = image - jnp.dot(current, projected, precision=lax.Precision.HIGHEST)
        if lanczos_step > 0:
            image = image - jnp.dot(previous, prev_b.T, precision=lax.Precision.HIGHEST)
        following, factor = orthonormal(image)
        coefficients.append(projected)
        coefficients.append(factor)
        previous = current
        prev_b = factor
        current = following
        basis_blocks.append(current)
    return (jnp.concatenate(basis_blocks, axis=1), jnp.stack(coefficients))
```

```python
import jax
import jax.numpy as jnp
from jax import lax
from jax.sharding import PartitionSpec as P

BINS_COL = 8
BOTH = ("loop", "inner")
HI = lax.Precision.HIGHEST


def dot_nt(left, right, precision=HI):
    return lax.dot_general(
        left, right, (((1,), (1,)), ((), ())), precision=precision,
        preferred_element_type=jnp.float32,
    )


def dot(left, right):
    return jnp.dot(left, right, precision=HI, preferred_element_type=jnp.float32)


def matches(values, targets):
    return (values[:, None] == targets[None, :]).astype(jnp.float32)


def routes(n_loop, n_inner):
    def build(loop_of, inner_of):
        pairs = []
        for l in range(n_loop):
            for c in range(n_inner):
                target = inner_of(c)
                if 0 <= target < n_inner:
                    pairs.append((l * n_inner + c, loop_of(l) * n_inner + target))
        return pairs

    same = lambda v: v
    return {
        "core": build(lambda l: l ^ 1, same),
        "row": build(lambda l: l ^ 2, same),
        "near": build(same, lambda c: c ^ 1),
        "far": build(same, lambda c: c + 1 if c % 2 else c - 1),
        "relay": build(same, lambda c: c - 2 if c % 2 else c + 2),
    }


def local(snapshots, bins, pairs, start_weights):
    row_count, features = snapshots.shape
    n_loop = lax.axis_size("loop")
    n_inner = lax.axis_size("inner")
    column = lax.axis_index("inner")
    group = lax.axis_index("loop")
    route = routes(n_loop, n_inner)

    def move(value, name):
        return lax.ppermute(value, BOTH, route[name])

    near_rows = move(snapshots, "near")
    across_rows = move(snapshots, "row")
    far_rows = move(near_rows, "relay")
    mate_rows = move(snapshots, "core")
    across_mate = move(across_rows, "core")
    group_rows = jnp.concatenate([snapshots, mate_rows, across_rows, across_mate], axis=0)

    odd = column % 2
    near_column = jnp.where(odd == 1, column - 1, column + 1)
    far_column = jnp.where(odd == 1, column + 1, column - 1)
    bin_grid = bins.reshape(n_loop, n_inner, row_count)

    def bins_of(l, c):
        return lax.dynamic_slice(bin_grid, (l, c, 0), (1, 1, row_count)).reshape(-1)

    row_bins = jnp.concatenate([bins_of(group ^ r, column) for r in range(n_loop)])
    row_ids = column * BINS_COL + jnp.arange(BINS_COL, dtype=jnp.int32)
    left_bins = pairs[:, 0]
    right_bins = pairs[:, 1]
    row_hot = matches(row_bins, row_ids)
    masks = []
    for other in (column, near_column, far_column):
        ids = other * BINS_COL + jnp.arange(BINS_COL, dtype=jnp.int32)
        count = jnp.dot(matches(left_bins, ids).T, matches(right_bins, row_ids), precision=HI)
        count = count + jnp.dot(matches(right_bins, ids).T, matches(left_bins, row_ids), precision=HI)
        linked = jnp.where(count > 0.5, 1.0, 0.0).astype(jnp.float32)
        inside = jnp.logical_and(other >= 0, other < n_inner)
        their_bins = jnp.where(inside, bins_of(group, jnp.clip(other, 0, n_inner - 1)), -1)
        masks.append(jnp.dot(matches(their_bins, ids), jnp.dot(linked, row_hot.T)))

    epsilon = features / 3.0
    wide = group_rows.astype(jnp.float32)
    norms = jnp.sum(wide * wide, axis=1)

    def tile(other_rows, mask):
        other_wide = other_rows.astype(jnp.float32)
        other_norms = jnp.sum(other_wide * other_wide, axis=1)
        products = dot_nt(other_rows, group_rows, None)
        distance = other_norms[:, None] + norms[None, :] - 2.0 * products
        return mask * jnp.exp(-distance / epsilon)

    tiles = [
        tile(rows, mask) for rows, mask in zip((snapshots, near_rows, far_rows), masks)
    ]
    kernel = jnp.concatenate(tiles, axis=0)

    def group_sum(partial):
        block = [partial[:, r * row_count:(r + 1) * row_count] for r in range(4)]
        got = move(jnp.stack([block[1], block[3]]), "core")
        mine = block[0] + got[0]
        theirs = block[2] + got[1]
        return mine + move(theirs, "row")

    degree = group_sum(jnp.sum(kernel, axis=0)[None, :])
    inv_root = lax.rsqrt(degree)

    def apply(vectors):
        scaled = inv_root * vectors
        strip = jnp.concatenate([scaled, move(scaled, "near"), move(scaled, "far")], axis=1)
        return inv_root * group_sum(dot(strip, kernel))

    def total(value):
        copies = jnp.broadcast_to(value[None], (n_loop * n_inner,) + value.shape)
        return jnp.sum(lax.all_to_all(copies, BOTH, 0, 0), axis=0)

    def factor(gram):
        lower = jnp.linalg.cholesky(gram)
        eye = jnp.eye(gram.shape[0], dtype=jnp.float32)
        inverse = lax.linalg.triangular_solve(lower, eye, left_side=True, lower=True)
        return lower, inverse

    start = dot_nt(start_weights.T, snapshots, None)
    unused, inverse_s = factor(total(dot_nt(start, start)))
    basis_0 = dot(inverse_s, start)
    image_1 = apply(basis_0)
    image_2 = apply(image_1)
    sums = total(
        jnp.concatenate(
            [
                dot_nt(basis_0, image_1),
                dot_nt(image_1, image_1),
                dot_nt(image_1, image_2),
                dot_nt(image_2, image_2),
            ],
            axis=1,
        )
    )
    a_0, m_11, m_12, m_22 = jnp.split(sums, 4, axis=1)
    lower_1, inverse_1 = factor(m_11 - dot(a_0.T, a_0))
    basis_1 = dot(inverse_1, image_1 - dot(a_0.T, basis_0))
    mixed = m_12 - dot(m_11, a_0) - dot(a_0.T, m_11) + dot(a_0.T, dot(a_0, a_0))
    a_1 = dot_nt(dot(inverse_1, mixed), inverse_1)
    twice = m_22 - dot(m_12.T, a_0) - dot(a_0.T, m_12) + dot(a_0.T, dot(m_11, a_0))
    gram_2 = dot_nt(dot(inverse_1, twice), inverse_1)
    gram_2 = gram_2 - dot(a_1.T, a_1) - dot_nt(lower_1.T, lower_1.T)
    lower_2, inverse_2 = factor(gram_2)
    image = dot(inverse_1, image_2 - dot(a_0.T, image_1))
    image = image - dot(a_1.T, basis_1) - dot(lower_1.T, basis_0)
    basis_2 = dot(inverse_2, image)
    basis = jnp.concatenate([basis_0, basis_1, basis_2], axis=0).T
    return basis, jnp.stack([a_0, lower_1.T, a_1, lower_2.T])


def solution(mesh):
    in_specs = (P(BOTH, None), P(), P(), P())
    out_specs = (P(BOTH, None), P())
    return jax.shard_map(local, mesh=mesh, in_specs=in_specs, out_specs=out_specs, check_vma=False)
```

```python
import functools

import jax
import jax.numpy as jnp
from jax import lax
from jax.experimental import pallas as pl
from jax.experimental.pallas import tpu as pltpu
from jax.sharding import Mesh, PartitionSpec as P

BINS_COL = 8
LANES = 128
ALL = ("row", "core", "inner")
HI = lax.Precision.HIGHEST
F32 = jnp.float32
BF16 = jnp.bfloat16


def nt(left, right, precision=HI):
    return lax.dot_general(
        left, right, (((1,), (1,)), ((), ())), precision=precision, preferred_element_type=F32
    )


def nn(left, right, precision=HI):
    return lax.dot_general(
        left, right, (((1,), (0,)), ((), ())), precision=precision, preferred_element_type=F32
    )


def tn(left, right):
    return nn(left.T, right)


def matches(values, targets):
    return (values[:, None] == targets[None, :]).astype(F32)


def call(kernel, outs, *args, **extra):
    return pl.pallas_call(
        kernel,
        out_shape=[jax.ShapeDtypeStruct(shape, kind) for shape, kind in outs],
        **extra,
    )(*args)


def spread(value):
    return jnp.broadcast_to(value, (8, LANES))


def eliminate(groups, count):
    sub = lax.broadcasted_iota(jnp.int32, (8, LANES), 0)
    lane = lax.broadcasted_iota(jnp.int32, (8, LANES), 1)
    g = list(groups)
    for j in range(0, count, 2):
        q, s = divmod(j, 8)
        first = [spread(v[:, j:j + 1]) for v in g[q:]]
        second = [spread(v[:, j + 1:j + 2]) for v in g[q:]]
        row_a = spread(g[q][s:s + 1, :])
        row_b = spread(g[q][s + 1:s + 2, :])
        a = spread(first[0][s:s + 1, :])
        b = spread(first[0][s + 1:s + 2, :])
        d = spread(second[0][s + 1:s + 2, :])
        inverse = 1.0 / (a * d - b * b)
        left = (d * inverse) * row_a - (b * inverse) * row_b
        right = (a * inverse) * row_b - (b * inverse) * row_a
        for i in range(len(g) - q):
            change = first[i] * left + second[i] * right
            if i == 0:
                change = jnp.where(sub > s + 1, change, 0.0)
            g[q + i] = g[q + i] - change
    odd = sub % 2 == 1
    done = []
    for q, v in enumerate(g):
        above = pltpu.roll(v, 1, 0)
        at = lane == sub + (8 * q - 1)
        b = jnp.sum(jnp.where(at, v, 0.0), axis=1, keepdims=True)
        a = jnp.sum(jnp.where(at, above, 0.0), axis=1, keepdims=True)
        v = jnp.where(odd, v - (b / jnp.where(odd, a, 1.0)) * above, v)
        pivot = jnp.sum(jnp.where(lane == sub + 8 * q, v, 0.0), axis=1, keepdims=True)
        done.append(v * lax.rsqrt(pivot))
    return done


def eye_lanes(rows, start):
    row = lax.broadcasted_iota(jnp.int32, (rows, LANES), 0)
    lane = lax.broadcasted_iota(jnp.int32, (rows, LANES), 1)
    return jnp.where(lane == row + start, 1.0, 0.0)


def start_kernel(weights, rows, start, copies):
    value = nt(weights[...], rows[...], None)
    start[...] = value
    gram = nt(value, value)
    width = gram.shape[0]
    packed = jnp.concatenate([gram[8 * q:8 * q + 8, :] for q in range(width // 8)], axis=1)
    copies[...] = jnp.broadcast_to(packed[None], copies.shape)


def first_basis_kernel(parts, start, basis):
    packed = jnp.sum(parts[...], axis=0)
    width = start.shape[0]
    eye = eye_lanes(width, LANES // 2)
    groups = []
    for q in range(width // 8):
        piece = packed[:, width * q:width * (q + 1)]
        piece = jnp.concatenate([piece, jnp.zeros((8, LANES - width), F32)], axis=1)
        groups.append(piece + eye[8 * q:8 * q + 8, :])
    whole = jnp.concatenate(eliminate(groups, width), axis=0)
    inverse = whole[:, LANES // 2:LANES // 2 + width]
    basis[...] = nn(inverse, start[...])


def tile_kernel(scale, other, hot, links, norms, degree, r0, r1, r2, r3, high, low, out):
    x = other[...]
    wide = x.astype(F32)
    own = jnp.sum(wide * wide, axis=1, keepdims=True)
    span = r0.shape[0]
    mask = nn(hot[...], links[...], None)
    for i, rows in enumerate((r0, r1, r2, r3)):
        at = slice(i * span, (i + 1) * span)
        products = nt(x, rows[...], None)
        distance = own + norms[:, at] - 2.0 * products
        value = mask[:, at] * jnp.exp(distance * scale)
        top = value.astype(BF16)
        high[:, at] = top
        low[:, at] = (value - top.astype(F32)).astype(BF16)
        out[:, at] = degree[:, at] + jnp.sum(value, axis=0, keepdims=True)


def apply_kernel(*refs):
    vectors, tiles, (keep, send) = refs[:3], refs[3:-2], refs[-2:]
    width = vectors[0].shape[0]
    half = keep.shape[1]
    total = None
    parts = []
    count = len(tiles) // 2
    strip = jnp.concatenate([v[...] for v in vectors], axis=1)
    top = strip.astype(BF16)
    low = (strip - top.astype(F32)).astype(BF16)
    both = jnp.concatenate([top, low], axis=0)
    at = 0
    for i in range(count):
        high_tile, low_tile = tiles[2 * i][...], tiles[2 * i + 1][...]
        size = high_tile.shape[0]
        piece = nn(both[:, at:at + size], high_tile, None)
        piece = piece[:width] + piece[width:] + nn(top[:, at:at + size], low_tile, None)
        total = piece if total is None else total + piece
        at += size
    keep[...] = total[:, :half]
    send[...] = total[:, half:]


def gram_kernel(mine, got, inv_root, basis, image, image_next, packed):
    value = inv_root[...] * (mine[...] + got[...])
    image_next[...] = value
    first = image[...]
    packed[...] = jnp.concatenate(
        [nt(basis[...], first), nt(first, first), nt(first, value), nt(value, value)], axis=1
    )


def last_kernel(parts, q0, v1, v2, basis, coefficients):
    packed = jnp.sum(parts[...], axis=0)
    width = q0.shape[0]
    a_0, m_11, m_12, m_22 = [packed[:, width * i:width * (i + 1)] for i in range(4)]
    left_0 = jnp.concatenate([a_0, m_11], axis=1)
    cross = tn(left_0, left_0)
    top = jnp.concatenate([m_11, m_12], axis=1) - cross[:width]
    low = jnp.concatenate([m_12, m_22], axis=1) - cross[width:]
    gram = jnp.concatenate([top, low], axis=0)
    rows = 2 * width
    gram = jnp.concatenate([gram, jnp.zeros((rows, LANES - rows), F32)], axis=1)
    gram = gram + eye_lanes(rows, LANES // 2)
    groups = [gram[8 * q:8 * q + 8, :] for q in range(rows // 8)]
    whole = jnp.concatenate(eliminate(groups, rows), axis=0)
    inverse = whole[:, LANES // 2:LANES // 2 + rows]
    q = q0[...]
    rest = jnp.concatenate([v1[...], v2[...]], axis=0) - tn(left_0, q)
    basis[:width, :] = q
    basis[width:, :] = nn(inverse, rest)
    row = lax.broadcasted_iota(jnp.int32, (width, width), 0)
    col = lax.broadcasted_iota(jnp.int32, (width, width), 1)
    r_11 = jnp.where(col >= row, whole[:width, :width], 0.0)
    r_12 = whole[:width, width:rows]
    r_22 = jnp.where(col >= row, whole[width:, width:rows], 0.0)
    z_11 = inverse[:width, :width]
    coefficients[0] = a_0
    coefficients[1] = r_11
    coefficients[2] = nt(r_12 - nn(r_11, a_0), z_11)
    coefficients[3] = jnp.where(col >= row, nt(r_22, z_11), 0.0)


def routes(n_loop, n_inner):
    def build(loop_of, inner_of):
        pairs = []
        for l in range(n_loop):
            for c in range(n_inner):
                if 0 <= inner_of(c) < n_inner:
                    pairs.append((l * n_inner + c, loop_of(l) * n_inner + inner_of(c)))
        return pairs

    same = lambda v: v
    return {
        "core": build(lambda l: l ^ 1, same),
        "row": build(lambda l: l ^ 2, same),
        "near": build(same, lambda c: c ^ 1),
        "far": build(same, lambda c: c + 1 if c % 2 else c - 1),
        "relay": build(same, lambda c: c - 2 if c % 2 else c + 2),
    }


def local(snapshots, bins, pairs, start_weights):
    row_count, features = snapshots.shape
    width = start_weights.shape[1]
    n_row = lax.axis_size("row")
    n_loop = n_row * lax.axis_size("core")
    n_inner = lax.axis_size("inner")
    column = lax.axis_index("inner")
    group = lax.axis_index(("row", "core"))
    route = routes(n_loop, n_inner)

    def move(value, name):
        return lax.ppermute(value, ALL, route[name])

    half = row_count // 2
    near_a = move(snapshots[:half], "near")
    near_b = move(snapshots[half:], "near")
    across = move(snapshots, "row")
    far_a = move(near_a, "relay")
    far_b = move(near_b, "relay")
    mate = move(snapshots, "core")
    across_mate = move(across, "core")
    group_rows = (snapshots, across, mate, across_mate)

    odd = column % 2
    near_column = jnp.where(odd == 1, column - 1, column + 1)
    far_column = jnp.where(odd == 1, column + 1, column - 1)
    bin_grid = bins.reshape(n_loop, n_inner, row_count)

    def bins_of(l, c):
        return lax.dynamic_slice(bin_grid, (l, c, 0), (1, 1, row_count)).reshape(-1)

    row_bins = jnp.concatenate([bins_of(group ^ r, column) for r in (0, 2, 1, 3)])
    row_ids = column * BINS_COL + jnp.arange(BINS_COL, dtype=jnp.int32)
    row_hot = (row_ids[:, None] == row_bins[None, :]).astype(BF16)
    left_bins = pairs[:, 0]
    right_bins = pairs[:, 1]
    links = []
    hots = []
    for other in (column, near_column, far_column):
        ids = other * BINS_COL + jnp.arange(BINS_COL, dtype=jnp.int32)
        count = nn(matches(left_bins, ids).T, matches(right_bins, row_ids), HI)
        count = count + nn(matches(right_bins, ids).T, matches(left_bins, row_ids), HI)
        linked = jnp.where(count > 0.5, 1.0, 0.0).astype(BF16)
        links.append(nn(linked, row_hot, None).astype(BF16))
        inside = jnp.logical_and(other >= 0, other < n_inner)
        their_bins = jnp.where(inside, bins_of(group, jnp.clip(other, 0, n_inner - 1)), -1)
        hots.append((their_bins[:, None] == ids[None, :]).astype(BF16))

    n_all = n_loop * n_inner
    start, copies = call(
        start_kernel,
        [((width, row_count), F32), ((n_all, 8, width * width // 8), F32)],
        start_weights.T,
        snapshots,
    )
    parts = lax.all_to_all(copies, ALL, 0, 0)
    (basis_0,) = call(first_basis_kernel, [((width, row_count), F32)], parts, start)

    def norms_of(rows):
        wide = rows.astype(F32)
        return jnp.sum(wide * wide, axis=1)

    norms = jnp.concatenate([norms_of(rows) for rows in group_rows])[None, :]
    span = n_loop * row_count
    degree = jnp.zeros((1, span), F32)
    tiles = []
    for rows, hot, link in (
        (snapshots, hots[0], links[0]),
        (near_a, hots[1][:half], links[1]),
        (near_b, hots[1][half:], links[1]),
        (far_a, hots[2][:half], links[2]),
        (far_b, hots[2][half:], links[2]),
    ):
        size = rows.shape[0]
        high, low, degree = call(
            functools.partial(tile_kernel, -3.0 / features),
            [((size, span), BF16), ((size, span), BF16), ((1, span), F32)],
            rows, hot, link, norms, degree, *group_rows,
        )
        tiles += [high, low]

    def group_sum(keep, send):
        keep = keep + move(send, "core")
        return keep[:, :row_count], move(keep[:, row_count:], "row")

    mine, got = group_sum(degree[:, :span // 2], degree[:, span // 2:])
    inv_root = lax.rsqrt(mine + got)

    def apply(vectors):
        scaled = inv_root * vectors
        keep, send = call(
            apply_kernel,
            [((width, span // 2), F32)] * 2,
            scaled, move(scaled, "near"), move(scaled, "far"), *tiles,
        )
        return group_sum(keep, send)

    mine, got = apply(basis_0)
    image_1 = inv_root * (mine + got)
    mine, got = apply(image_1)
    image_2, packed = call(
        gram_kernel,
        [((width, row_count), F32), ((width, 4 * width), F32)],
        mine, got, inv_root, basis_0, image_1,
    )
    packed = packed + move(packed, "core")
    copies = jnp.broadcast_to(packed[None], (n_row * n_inner,) + packed.shape)
    parts = lax.all_to_all(copies, ("row", "inner"), 0, 0)
    basis, coefficients = call(
        last_kernel,
        [((3 * width, row_count), F32), ((4, width, width), F32)],
        parts, basis_0, image_1, image_2,
    )
    return basis.T, coefficients


def solution(mesh):
    n_loop, n_inner = mesh.shape["loop"], mesh.shape["inner"]
    fine = Mesh(mesh.devices.reshape(n_loop // 2, 2, n_inner), ALL)
    in_specs = (P(ALL, None), P(), P(), P())
    out_specs = (P(ALL, None), P())
    return jax.shard_map(local, mesh=fine, in_specs=in_specs, out_specs=out_specs, check_vma=False)
```

```python
import functools

import jax
import jax.numpy as jnp
from jax import lax
from jax.experimental import pallas as pl
from jax.experimental.pallas import tpu as pltpu
from jax.sharding import Mesh, PartitionSpec as P

BINS_COL = 8
LANES = 128
KERNEL_VMEM = 16 * 2**20
ALL = ("row", "core", "inner")
HI = lax.Precision.HIGHEST
F32 = jnp.float32
BF16 = jnp.bfloat16


def nt(left, right, precision=HI):
    return lax.dot_general(
        left, right, (((1,), (1,)), ((), ())), precision=precision, preferred_element_type=F32
    )


def nn(left, right, precision=HI):
    return lax.dot_general(
        left, right, (((1,), (0,)), ((), ())), precision=precision, preferred_element_type=F32
    )


def tn(left, right):
    return nn(left.T, right)


def matches(values, targets):
    return (values[:, None] == targets[None, :]).astype(F32)


def call(kernel, outs, *args, final=False):
    result = jax.ShapeDtypeStruct if final else pltpu.VMEM
    args = [pltpu.with_memory_space_constraint(a, pltpu.VMEM) for a in args]
    return pl.pallas_call(
        kernel,
        out_shape=[result(shape, kind) for shape, kind in outs],
        compiler_params=pltpu.CompilerParams(vmem_limit_bytes=KERNEL_VMEM),
    )(*args)


def spread(value):
    return jnp.broadcast_to(value, (8, LANES))


def eliminate(groups, count):
    sub = lax.broadcasted_iota(jnp.int32, (8, LANES), 0)
    lane = lax.broadcasted_iota(jnp.int32, (8, LANES), 1)
    g = list(groups)
    for j in range(0, count, 2):
        q, s = divmod(j, 8)
        first = [spread(v[:, j:j + 1]) for v in g[q:]]
        second = [spread(v[:, j + 1:j + 2]) for v in g[q:]]
        row_a = spread(g[q][s:s + 1, :])
        row_b = spread(g[q][s + 1:s + 2, :])
        a = spread(first[0][s:s + 1, :])
        b = spread(first[0][s + 1:s + 2, :])
        d = spread(second[0][s + 1:s + 2, :])
        inverse = 1.0 / (a * d - b * b)
        left = (d * inverse) * row_a - (b * inverse) * row_b
        right = (a * inverse) * row_b - (b * inverse) * row_a
        for i in range(len(g) - q):
            change = first[i] * left + second[i] * right
            if i == 0:
                change = jnp.where(sub > s + 1, change, 0.0)
            g[q + i] = g[q + i] - change
    odd = sub % 2 == 1
    done = []
    for q, v in enumerate(g):
        above = pltpu.roll(v, 1, 0)
        at = lane == sub + (8 * q - 1)
        b = jnp.sum(jnp.where(at, v, 0.0), axis=1, keepdims=True)
        a = jnp.sum(jnp.where(at, above, 0.0), axis=1, keepdims=True)
        v = jnp.where(odd, v - (b / jnp.where(odd, a, 1.0)) * above, v)
        pivot = jnp.sum(jnp.where(lane == sub + 8 * q, v, 0.0), axis=1, keepdims=True)
        done.append(v * lax.rsqrt(pivot))
    return done


def eye_lanes(rows, start):
    row = lax.broadcasted_iota(jnp.int32, (rows, LANES), 0)
    lane = lax.broadcasted_iota(jnp.int32, (rows, LANES), 1)
    return jnp.where(lane == row + start, 1.0, 0.0)


def start_kernel(weights, rows, start, copies):
    value = nt(weights[...], rows[...], None)
    start[...] = value
    gram = nt(value, value)
    width = gram.shape[0]
    packed = jnp.concatenate([gram[8 * q:8 * q + 8, :] for q in range(width // 8)], axis=1)
    copies[...] = jnp.broadcast_to(packed[None], copies.shape)


def first_basis_kernel(parts, start, basis):
    packed = jnp.sum(parts[...], axis=0)
    width = start.shape[0]
    eye = eye_lanes(width, LANES // 2)
    groups = []
    for q in range(width // 8):
        piece = packed[:, width * q:width * (q + 1)]
        piece = jnp.concatenate([piece, jnp.zeros((8, LANES - width), F32)], axis=1)
        groups.append(piece + eye[8 * q:8 * q + 8, :])
    whole = jnp.concatenate(eliminate(groups, width), axis=0)
    inverse = whole[:, LANES // 2:LANES // 2 + width]
    basis[...] = nn(inverse, start[...])


def turn_kernel(r0, r1, r2, r3, turned, norms):
    span = r0.shape[0]
    for i, rows in enumerate((r0, r1, r2, r3)):
        at = slice(i * span, (i + 1) * span)
        value = rows[...].T
        turned[:, at] = value
        wide = value.astype(F32)
        norms[:, at] = jnp.sum(wide * wide, axis=0, keepdims=True)


def tile_kernel(scale, other, hot, links, norms, degree, turned, *refs):
    high, low, out = refs[-3:]
    x = other[...]
    wide = x.astype(F32)
    own = jnp.sum(wide * wide, axis=1, keepdims=True)
    mask = nn(hot[...], links[...], None)
    products = nn(x, turned[...], None)
    distance = own + norms[...] - 2.0 * products
    value = mask * jnp.exp(distance * scale)
    top = value.astype(BF16)
    high[...] = top
    low[...] = (value - top.astype(F32)).astype(BF16)
    out[...] = degree[...] + jnp.sum(value, axis=0, keepdims=True)


def apply_kernel(*refs):
    vectors, tiles, (keep, send) = refs[:3], refs[3:-2], refs[-2:]
    width = vectors[0].shape[0]
    half = keep.shape[1]
    total = None
    parts = []
    count = len(tiles) // 2
    strip = jnp.concatenate([v[...] for v in vectors], axis=1)
    top = strip.astype(BF16)
    low = (strip - top.astype(F32)).astype(BF16)
    both = jnp.concatenate([top, low], axis=0)
    at = 0
    for i in range(count):
        high_tile, low_tile = tiles[2 * i][...], tiles[2 * i + 1][...]
        size = high_tile.shape[0]
        piece = nn(both[:, at:at + size], high_tile, None)
        piece = piece[:width] + piece[width:] + nn(top[:, at:at + size], low_tile, None)
        total = piece if total is None else total + piece
        at += size
    keep[...] = total[:, :half]
    send[...] = total[:, half:]


def gram_kernel(mine, got, inv_root, basis, image, image_next, packed):
    value = inv_root[...] * (mine[...] + got[...])
    image_next[...] = value
    first = image[...]
    packed[...] = jnp.concatenate(
        [nt(basis[...], first), nt(first, first), nt(first, value), nt(value, value)], axis=1
    )


def last_kernel(parts, q0, v1, v2, basis, coefficients):
    packed = jnp.sum(parts[...], axis=0)
    width = q0.shape[0]
    a_0, m_11, m_12, m_22 = [packed[:, width * i:width * (i + 1)] for i in range(4)]
    left_0 = jnp.concatenate([a_0, m_11], axis=1)
    cross = tn(left_0, left_0)
    top = jnp.concatenate([m_11, m_12], axis=1) - cross[:width]
    low = jnp.concatenate([m_12, m_22], axis=1) - cross[width:]
    gram = jnp.concatenate([top, low], axis=0)
    rows = 2 * width
    gram = jnp.concatenate([gram, jnp.zeros((rows, LANES - rows), F32)], axis=1)
    gram = gram + eye_lanes(rows, LANES // 2)
    groups = [gram[8 * q:8 * q + 8, :] for q in range(rows // 8)]
    whole = jnp.concatenate(eliminate(groups, rows), axis=0)
    inverse = whole[:, LANES // 2:LANES // 2 + rows]
    q = q0[...]
    rest = jnp.concatenate([v1[...], v2[...]], axis=0) - tn(left_0, q)
    basis[:width, :] = q
    basis[width:, :] = nn(inverse, rest)
    row = lax.broadcasted_iota(jnp.int32, (width, width), 0)
    col = lax.broadcasted_iota(jnp.int32, (width, width), 1)
    r_11 = jnp.where(col >= row, whole[:width, :width], 0.0)
    r_12 = whole[:width, width:rows]
    r_22 = jnp.where(col >= row, whole[width:, width:rows], 0.0)
    z_11 = inverse[:width, :width]
    coefficients[0] = a_0
    coefficients[1] = r_11
    coefficients[2] = nt(r_12 - nn(r_11, a_0), z_11)
    coefficients[3] = jnp.where(col >= row, nt(r_22, z_11), 0.0)


def routes(n_loop, n_inner):
    def build(loop_of, inner_of):
        pairs = []
        for l in range(n_loop):
            for c in range(n_inner):
                if 0 <= inner_of(c) < n_inner:
                    pairs.append((l * n_inner + c, loop_of(l) * n_inner + inner_of(c)))
        return pairs

    same = lambda v: v
    return {
        "core": build(lambda l: l ^ 1, same),
        "row": build(lambda l: l ^ 2, same),
        "near": build(same, lambda c: c ^ 1),
        "far": build(same, lambda c: c + 1 if c % 2 else c - 1),
        "relay": build(same, lambda c: c - 2 if c % 2 else c + 2),
    }


def local(snapshots, bins, pairs, start_weights):
    row_count, features = snapshots.shape
    width = start_weights.shape[1]
    n_row = lax.axis_size("row")
    n_loop = n_row * lax.axis_size("core")
    n_inner = lax.axis_size("inner")
    column = lax.axis_index("inner")
    group = lax.axis_index(("row", "core"))
    route = routes(n_loop, n_inner)

    def move(value, name):
        return lax.ppermute(value, ALL, route[name])

    half = row_count // 2
    near_a = move(snapshots[:half], "near")
    near_b = move(snapshots[half:], "near")
    across = move(snapshots, "row")
    far_a = move(near_a, "relay")
    far_b = move(near_b, "relay")
    mate = move(snapshots, "core")
    across_mate = move(across, "core")
    group_rows = (snapshots, across, mate, across_mate)

    bins, pairs, near_b = lax.optimization_barrier((bins, pairs, near_b))
    odd = column % 2
    near_column = jnp.where(odd == 1, column - 1, column + 1)
    far_column = jnp.where(odd == 1, column + 1, column - 1)
    bin_grid = bins.reshape(n_loop, n_inner, row_count)

    def bins_of(l, c):
        return lax.dynamic_slice(bin_grid, (l, c, 0), (1, 1, row_count)).reshape(-1)

    row_bins = jnp.concatenate([bins_of(group ^ r, column) for r in (0, 2, 1, 3)])
    row_ids = column * BINS_COL + jnp.arange(BINS_COL, dtype=jnp.int32)
    row_hot = (row_ids[:, None] == row_bins[None, :]).astype(BF16)
    left_bins = pairs[:, 0]
    right_bins = pairs[:, 1]
    links = []
    hots = []
    for other in (column, near_column, far_column):
        ids = other * BINS_COL + jnp.arange(BINS_COL, dtype=jnp.int32)
        count = nn(matches(left_bins, ids).T, matches(right_bins, row_ids), HI)
        count = count + nn(matches(right_bins, ids).T, matches(left_bins, row_ids), HI)
        linked = jnp.where(count > 0.5, 1.0, 0.0).astype(BF16)
        links.append(nn(linked, row_hot, None).astype(BF16))
        inside = jnp.logical_and(other >= 0, other < n_inner)
        their_bins = jnp.where(inside, bins_of(group, jnp.clip(other, 0, n_inner - 1)), -1)
        hots.append((their_bins[:, None] == ids[None, :]).astype(BF16))

    n_all = n_loop * n_inner
    start, copies = call(
        start_kernel,
        [((width, row_count), F32), ((n_all, 8, width * width // 8), F32)],
        start_weights.T,
        snapshots,
    )
    parts = lax.all_to_all(copies, ALL, 0, 0)
    (basis_0,) = call(first_basis_kernel, [((width, row_count), F32)], parts, start)

    span = n_loop * row_count
    turned, norms = call(turn_kernel, [((features, span), BF16), ((1, span), F32)], *group_rows)
    degree = jnp.zeros((1, span), F32)
    tiles = []
    for rows, hot, link, after in (
        (snapshots, hots[0], links[0], ()),
        (near_a, hots[1][:half], links[1], ()),
        (near_b, hots[1][half:], links[1], (basis_0,)),
        (far_a, hots[2][:half], links[2], ()),
        (far_b, hots[2][half:], links[2], ()),
    ):
        size = rows.shape[0]
        high, low, degree = call(
            functools.partial(tile_kernel, -3.0 / features),
            [((size, span), BF16), ((size, span), BF16), ((1, span), F32)],
            rows, hot, link, norms, degree, turned, *after,
        )
        tiles += [high, low]

    def group_sum(keep, send):
        keep = keep + move(send, "core")
        return keep[:, :row_count], move(keep[:, row_count:], "row")

    mine, got = group_sum(degree[:, :span // 2], degree[:, span // 2:])
    inv_root = lax.rsqrt(mine + got)

    def apply(vectors):
        scaled = inv_root * vectors
        keep, send = call(
            apply_kernel,
            [((width, span // 2), F32)] * 2,
            scaled, move(scaled, "near"), move(scaled, "far"), *tiles,
        )
        return group_sum(keep, send)

    mine, got = apply(basis_0)
    image_1 = inv_root * (mine + got)
    mine, got = apply(image_1)
    image_2, packed = call(
        gram_kernel,
        [((width, row_count), F32), ((width, 4 * width), F32)],
        mine, got, inv_root, basis_0, image_1,
    )
    packed = packed + move(packed, "core")
    copies = jnp.broadcast_to(packed[None], (n_row * n_inner,) + packed.shape)
    parts = lax.all_to_all(copies, ("row", "inner"), 0, 0)
    basis, coefficients = call(
        last_kernel,
        [((3 * width, row_count), F32), ((4, width, width), F32)],
        parts, basis_0, image_1, image_2,
        final=True,
    )
    return basis.T, coefficients


def solution(mesh):
    n_loop, n_inner = mesh.shape["loop"], mesh.shape["inner"]
    fine = Mesh(mesh.devices.reshape(n_loop // 2, 2, n_inner), ALL)
    in_specs = (P(ALL, None), P(), P(), P())
    out_specs = (P(ALL, None), P())
    return jax.shard_map(local, mesh=fine, in_specs=in_specs, out_specs=out_specs, check_vma=False)
```

```python
import functools

import jax
import jax.numpy as jnp
from jax import lax
from jax.experimental import pallas as pl
from jax.experimental.pallas import tpu as pltpu
from jax.sharding import Mesh, PartitionSpec as P

BINS_COL = 8
LANES = 128
KERNEL_VMEM = 16 * 2**20
ALL = ("row", "core", "inner")
HI = lax.Precision.HIGHEST
F32 = jnp.float32
BF16 = jnp.bfloat16


def nt(left, right, precision=HI):
    return lax.dot_general(
        left, right, (((1,), (1,)), ((), ())), precision=precision, preferred_element_type=F32
    )


def nn(left, right, precision=HI):
    return lax.dot_general(
        left, right, (((1,), (0,)), ((), ())), precision=precision, preferred_element_type=F32
    )


def tn(left, right):
    return nn(left.T, right)


def call(kernel, outs, *args, final=False, scalars=0):
    result = jax.ShapeDtypeStruct if final else pltpu.VMEM
    vectors = [pltpu.with_memory_space_constraint(a, pltpu.VMEM) for a in args[scalars:]]
    return pl.pallas_call(
        kernel,
        out_shape=[result(shape, kind) for shape, kind in outs],
        in_specs=[pl.BlockSpec(memory_space=pltpu.SMEM)] * scalars
        + [pl.BlockSpec(memory_space=pltpu.VMEM)] * len(vectors),
        compiler_params=pltpu.CompilerParams(vmem_limit_bytes=KERNEL_VMEM),
    )(*args[:scalars], *vectors)


def spread(value):
    return jnp.broadcast_to(value, (8, LANES))


def eliminate(groups, count):
    sub = lax.broadcasted_iota(jnp.int32, (8, LANES), 0)
    lane = lax.broadcasted_iota(jnp.int32, (8, LANES), 1)
    g = list(groups)
    for j in range(0, count, 2):
        q, s = divmod(j, 8)
        first = [spread(v[:, j:j + 1]) for v in g[q:]]
        second = [spread(v[:, j + 1:j + 2]) for v in g[q:]]
        row_a = spread(g[q][s:s + 1, :])
        row_b = spread(g[q][s + 1:s + 2, :])
        a = spread(first[0][s:s + 1, :])
        b = spread(first[0][s + 1:s + 2, :])
        d = spread(second[0][s + 1:s + 2, :])
        inverse = 1.0 / (a * d - b * b)
        left = (d * inverse) * row_a - (b * inverse) * row_b
        right = (a * inverse) * row_b - (b * inverse) * row_a
        for i in range(len(g) - q):
            change = first[i] * left + second[i] * right
            if i == 0:
                change = jnp.where(sub > s + 1, change, 0.0)
            g[q + i] = g[q + i] - change
    odd = sub % 2 == 1
    done = []
    for q, v in enumerate(g):
        above = pltpu.roll(v, 1, 0)
        at = lane == sub + (8 * q - 1)
        b = jnp.sum(jnp.where(at, v, 0.0), axis=1, keepdims=True)
        a = jnp.sum(jnp.where(at, above, 0.0), axis=1, keepdims=True)
        v = jnp.where(odd, v - (b / jnp.where(odd, a, 1.0)) * above, v)
        pivot = jnp.sum(jnp.where(lane == sub + 8 * q, v, 0.0), axis=1, keepdims=True)
        done.append(v * lax.rsqrt(pivot))
    return done


def eye_lanes(rows, start):
    row = lax.broadcasted_iota(jnp.int32, (rows, LANES), 0)
    lane = lax.broadcasted_iota(jnp.int32, (rows, LANES), 1)
    return jnp.where(lane == row + start, 1.0, 0.0)


def start_kernel(weights, rows, start, copies):
    value = nt(weights[...], rows[...], None)
    start[...] = value
    gram = nt(value, value)
    width = gram.shape[0]
    packed = jnp.concatenate([gram[8 * q:8 * q + 8, :] for q in range(width // 8)], axis=1)
    copies[...] = jnp.broadcast_to(packed[None], copies.shape)


def first_basis_kernel(parts, start, basis):
    packed = jnp.sum(parts[...], axis=0)
    width = start.shape[0]
    eye = eye_lanes(width, LANES // 2)
    groups = []
    for q in range(width // 8):
        piece = packed[:, width * q:width * (q + 1)]
        piece = jnp.concatenate([piece, jnp.zeros((8, LANES - width), F32)], axis=1)
        groups.append(piece + eye[8 * q:8 * q + 8, :])
    whole = jnp.concatenate(eliminate(groups, width), axis=0)
    inverse = whole[:, LANES // 2:LANES // 2 + width]
    basis[...] = nn(inverse, start[...])


def links_kernel(n_inner, place, bins, pairs, hots, links):
    column, group = place[0], place[1]
    odd = column % 2
    step = 2 * odd - 1
    others = (column, column - step, column + step)
    bin_of = lax.broadcasted_iota(jnp.int32, (BINS_COL, 1), 0)

    def hot(values, base):
        return jnp.where(values == bin_of + base, 1.0, 0.0)

    def bins_at(l, c):
        return bins[pl.ds(l * n_inner + c, 1), :]

    rows = jnp.concatenate(
        [hot(bins_at(group ^ r, column), column * BINS_COL) for r in (0, 2, 1, 3)], axis=1
    )
    left, right = pairs[0:1, :], pairs[1:2, :]
    base = column * BINS_COL
    left_mine, right_mine = hot(left, base), hot(right, base)
    for i, other in enumerate(others):
        base = other * BINS_COL
        count = nt(hot(left, base), right_mine, None) + nt(hot(right, base), left_mine, None)
        linked = jnp.where(count > 0.5, 1.0, 0.0)
        links[i] = nn(linked, rows, None)
        theirs = bins_at(group, jnp.clip(other, 0, n_inner - 1))
        hots[i] = hot(theirs, base)


def turn_kernel(r0, r1, r2, r3, turned, norms):
    span = r0.shape[0]
    for i, rows in enumerate((r0, r1, r2, r3)):
        at = slice(i * span, (i + 1) * span)
        value = rows[...].T
        turned[:, at] = value
        wide = value.astype(F32)
        norms[:, at] = jnp.sum(wide * wide, axis=0, keepdims=True)


def tile_kernel(scale, kind, part, other, hots, all_links, norms, degree, turned, *refs):
    high, low, out = refs[-3:]
    x = other[...]
    wide = x.astype(F32)
    own = jnp.sum(wide * wide, axis=1, keepdims=True)
    size = x.shape[0]
    hot = hots[kind, :, part * size:(part + 1) * size]
    mask = nn(hot.T, all_links[kind], None)
    products = nn(x, turned[...], None)
    distance = own + norms[...] - 2.0 * products
    value = mask * jnp.exp(distance * scale)
    top = value.astype(BF16)
    high[...] = top
    low[...] = (value - top.astype(F32)).astype(BF16)
    out[...] = degree[...] + jnp.sum(value, axis=0, keepdims=True)


def apply_kernel(*refs):
    vectors, tiles, (keep, send) = refs[:3], refs[3:-2], refs[-2:]
    width = vectors[0].shape[0]
    half = keep.shape[1]
    total = None
    count = len(tiles) // 2
    strip = jnp.concatenate([v[...] for v in vectors], axis=1)
    top = strip.astype(BF16)
    low = (strip - top.astype(F32)).astype(BF16)
    both = jnp.concatenate([top, low], axis=0)
    at = 0
    for i in range(count):
        high_tile, low_tile = tiles[2 * i][...], tiles[2 * i + 1][...]
        size = high_tile.shape[0]
        piece = nn(both[:, at:at + size], high_tile, None)
        piece = piece[:width] + piece[width:] + nn(top[:, at:at + size], low_tile, None)
        total = piece if total is None else total + piece
        at += size
    keep[...] = total[:, :half]
    send[...] = total[:, half:]


def gram_kernel(mine, got, inv_root, basis, image, image_next, packed):
    value = inv_root[...] * (mine[...] + got[...])
    image_next[...] = value
    first = image[...]
    packed[...] = jnp.concatenate(
        [nt(basis[...], first), nt(first, first), nt(first, value), nt(value, value)], axis=1
    )


def last_kernel(parts, q0, v1, v2, basis, coefficients):
    packed = jnp.sum(parts[...], axis=0)
    width = q0.shape[0]
    a_0, m_11, m_12, m_22 = [packed[:, width * i:width * (i + 1)] for i in range(4)]
    left_0 = jnp.concatenate([a_0, m_11], axis=1)
    cross = tn(left_0, left_0)
    top = jnp.concatenate([m_11, m_12], axis=1) - cross[:width]
    low = jnp.concatenate([m_12, m_22], axis=1) - cross[width:]
    gram = jnp.concatenate([top, low], axis=0)
    rows = 2 * width
    gram = jnp.concatenate([gram, jnp.zeros((rows, LANES - rows), F32)], axis=1)
    gram = gram + eye_lanes(rows, LANES // 2)
    groups = [gram[8 * q:8 * q + 8, :] for q in range(rows // 8)]
    whole = jnp.concatenate(eliminate(groups, rows), axis=0)
    inverse = whole[:, LANES // 2:LANES // 2 + rows]
    q = q0[...]
    rest = jnp.concatenate([v1[...], v2[...]], axis=0) - tn(left_0, q)
    basis[:width, :] = q
    basis[width:, :] = nn(inverse, rest)
    row = lax.broadcasted_iota(jnp.int32, (width, width), 0)
    col = lax.broadcasted_iota(jnp.int32, (width, width), 1)
    r_11 = jnp.where(col >= row, whole[:width, :width], 0.0)
    r_12 = whole[:width, width:rows]
    r_22 = jnp.where(col >= row, whole[width:, width:rows], 0.0)
    z_11 = inverse[:width, :width]
    coefficients[0] = a_0
    coefficients[1] = r_11
    coefficients[2] = nt(r_12 - nn(r_11, a_0), z_11)
    coefficients[3] = jnp.where(col >= row, nt(r_22, z_11), 0.0)


def routes(n_loop, n_inner):
    def build(loop_of, inner_of):
        pairs = []
        for l in range(n_loop):
            for c in range(n_inner):
                if 0 <= inner_of(c) < n_inner:
                    pairs.append((l * n_inner + c, loop_of(l) * n_inner + inner_of(c)))
        return pairs

    same = lambda v: v
    return {
        "core": build(lambda l: l ^ 1, same),
        "row": build(lambda l: l ^ 2, same),
        "near": build(same, lambda c: c ^ 1),
        "far": build(same, lambda c: c + 1 if c % 2 else c - 1),
        "relay": build(same, lambda c: c - 2 if c % 2 else c + 2),
    }


def steps(snapshots, bins, pairs, start_weights):
    row_count, features = snapshots.shape
    width = start_weights.shape[1]
    n_row = lax.axis_size("row")
    n_loop = n_row * lax.axis_size("core")
    n_inner = lax.axis_size("inner")
    column = lax.axis_index("inner")
    group = lax.axis_index(("row", "core"))
    route = routes(n_loop, n_inner)

    def move(value, name):
        return lax.ppermute(value, ALL, route[name])

    half = row_count // 2
    across = move(snapshots, "row")
    mate = move(snapshots, "core")
    near_a = move(snapshots[:half], "near")
    near_b = move(snapshots[half:], "near")
    far_a = move(near_a, "relay")
    far_b = move(near_b, "relay")
    across_mate = move(across, "core")
    group_rows = (snapshots, across, mate, across_mate)

    place = jnp.where(jnp.arange(2) == 0, column, group).astype(jnp.int32)
    hots, links = call(
        functools.partial(links_kernel, n_inner),
        [((3, BINS_COL, row_count), F32), ((3, BINS_COL, n_loop * row_count), F32)],
        place, bins.reshape(n_loop * n_inner, row_count), pairs.T,
        scalars=1,
    )

    n_all = n_loop * n_inner
    start, copies = call(
        start_kernel,
        [((width, row_count), F32), ((n_all, 8, width * width // 8), F32)],
        start_weights.T,
        snapshots,
    )
    parts = lax.all_to_all(copies, ALL, 0, 0)
    (basis_0,) = call(first_basis_kernel, [((width, row_count), F32)], parts, start)

    span = n_loop * row_count
    turned, norms = call(turn_kernel, [((features, span), BF16), ((1, span), F32)], *group_rows)
    degree = jnp.zeros((1, span), F32)
    tiles = []
    for kind, part, rows, after in (
        (0, 0, snapshots, ()),
        (1, 0, near_a, ()),
        (1, 1, near_b, (basis_0,)),
        (2, 0, far_a, ()),
        (2, 1, far_b, ()),
    ):
        size = rows.shape[0]
        high, low, degree = call(
            functools.partial(tile_kernel, -3.0 / features, kind, part),
            [((size, span), BF16), ((size, span), BF16), ((1, span), F32)],
            rows, hots, links, norms, degree, turned, *after,
        )
        tiles += [high, low]

    def group_sum(keep, send):
        keep = keep + move(send, "core")
        return keep[:, :row_count], move(keep[:, row_count:], "row")

    mine, got = group_sum(degree[:, :span // 2], degree[:, span // 2:])
    inv_root = lax.rsqrt(mine + got)

    def apply(vectors):
        scaled = inv_root * vectors
        keep, send = call(
            apply_kernel,
            [((width, span // 2), F32)] * 2,
            scaled, move(scaled, "near"), move(scaled, "far"), *tiles,
        )
        return group_sum(keep, send)

    mine, got = apply(basis_0)
    image_1 = inv_root * (mine + got)
    mine, got = apply(image_1)
    image_2, packed = call(
        gram_kernel,
        [((width, row_count), F32), ((width, 4 * width), F32)],
        mine, got, inv_root, basis_0, image_1,
    )
    packed = packed + move(packed, "core")
    copies = jnp.broadcast_to(packed[None], (n_row * n_inner,) + packed.shape)
    parts = lax.all_to_all(copies, ("row", "inner"), 0, 0)
    basis, coefficients = call(
        last_kernel,
        [((3 * width, row_count), F32), ((4, width, width), F32)],
        parts, basis_0, image_1, image_2,
        final=True,
    )
    return basis.T, coefficients


def solution(mesh):
    n_loop, n_inner = mesh.shape["loop"], mesh.shape["inner"]
    fine = Mesh(mesh.devices.reshape(n_loop // 2, 2, n_inner), ALL)
    in_specs = (P(ALL, None), P(), P(), P())
    out_specs = (P(ALL, None), P())
    return jax.shard_map(steps, mesh=fine, in_specs=in_specs, out_specs=out_specs, check_vma=False)
```

```python
import functools

import jax
import jax.numpy as jnp
from jax import lax
from jax.experimental import pallas as pl
from jax.experimental.pallas import tpu as pltpu
from jax.sharding import Mesh, PartitionSpec as P

BINS_COL = 8
LANES = 128
KERNEL_VMEM = 16 * 2**20
ALL = ("row", "core", "inner")
HI = lax.Precision.HIGHEST
F32 = jnp.float32
BF16 = jnp.bfloat16


def nt(left, right, precision=HI):
    return lax.dot_general(
        left, right, (((1,), (1,)), ((), ())), precision=precision, preferred_element_type=F32
    )


def nn(left, right, precision=HI):
    return lax.dot_general(
        left, right, (((1,), (0,)), ((), ())), precision=precision, preferred_element_type=F32
    )


def tn(left, right):
    return nn(left.T, right)


def call(kernel, outs, *args, final=False, scalars=0):
    result = jax.ShapeDtypeStruct if final else pltpu.VMEM
    vectors = [pltpu.with_memory_space_constraint(a, pltpu.VMEM) for a in args[scalars:]]
    return pl.pallas_call(
        kernel,
        out_shape=[result(shape, kind) for shape, kind in outs],
        in_specs=[pl.BlockSpec(memory_space=pltpu.SMEM)] * scalars
        + [pl.BlockSpec(memory_space=pltpu.VMEM)] * len(vectors),
        compiler_params=pltpu.CompilerParams(vmem_limit_bytes=KERNEL_VMEM),
    )(*args[:scalars], *vectors)


def spread(value):
    return jnp.broadcast_to(value, (8, LANES))


def pivot_rows(row_a, row_b, a, b, d, lane, at):
    row_a = jnp.where(lane == at, 1.0, jnp.where(lane == at + 1, 0.0, row_a))
    row_b = jnp.where(lane == at, 0.0, jnp.where(lane == at + 1, 1.0, row_b))
    inverse = 1.0 / (a * d - b * b)
    a, b, d = a * inverse, b * inverse, d * inverse
    return d * row_a - b * row_b, a * row_b - b * row_a


def eliminate(groups):
    sub = lax.broadcasted_iota(jnp.int32, (8, LANES), 0)
    lane = lax.broadcasted_iota(jnp.int32, (8, LANES), 1)
    g = list(groups)
    for j in range(0, 8 * len(g), 4):
        q, s = divmod(j, 8)
        cols = [[spread(v[:, j + k:j + k + 1]) for v in g[q:]] for k in range(4)]
        rows = [spread(g[q][s + k:s + k + 1, :]) for k in range(4)]
        m = [[spread(cols[k][0][s + i:s + i + 1, :]) for k in range(4)] for i in range(4)]
        first_pair = jnp.logical_or(lane == j, lane == j + 1)
        last_pair = jnp.logical_or(lane == j + 2, lane == j + 3)
        w0, w1 = pivot_rows(rows[0], rows[1], m[0][0], m[0][1], m[1][1], lane, j)
        inverse = 1.0 / (m[0][0] * m[1][1] - m[0][1] * m[0][1])
        u = [
            ((m[1][1] * m[0][k] - m[0][1] * m[1][k]) * inverse,
             (m[0][0] * m[1][k] - m[0][1] * m[0][k]) * inverse)
            for k in (2, 3)
        ]
        third = jnp.where(first_pair, 0.0, rows[2]) - (m[2][0] * w0 + m[2][1] * w1)
        fourth = jnp.where(first_pair, 0.0, rows[3]) - (m[3][0] * w0 + m[3][1] * w1)
        a = m[2][2] - (m[2][0] * u[0][0] + m[2][1] * u[0][1])
        b = m[2][3] - (m[2][0] * u[1][0] + m[2][1] * u[1][1])
        d = m[3][3] - (m[3][0] * u[1][0] + m[3][1] * u[1][1])
        w2, w3 = pivot_rows(third, fourth, a, b, d, lane, j + 2)
        clear_0, clear_1 = jnp.where(last_pair, 0.0, w0), jnp.where(last_pair, 0.0, w1)
        pair = jnp.logical_or(first_pair, last_pair)
        for i in range(len(g) - q):
            c0, c1 = cols[0][i], cols[1][i]
            c2 = cols[2][i] - (c0 * u[0][0] + c1 * u[0][1])
            c3 = cols[3][i] - (c0 * u[1][0] + c1 * u[1][1])
            old = g[q + i]
            new = jnp.where(pair, 0.0, old) - (c0 * clear_0 + c1 * clear_1) - (c2 * w2 + c3 * w3)
            if i == 0:
                new = jnp.where(sub > s + 3, new, old)
                new = jnp.where(sub == s + 2, third, jnp.where(sub == s + 3, fourth, new))
            g[q + i] = new
    odd = sub % 2 == 1
    done = []
    for q, v in enumerate(g):
        row = sub + 8 * q
        above = pltpu.roll(v, 1, 0)
        at = lane == row - 1
        b = jnp.sum(jnp.where(at, v, 0.0), axis=1, keepdims=True)
        a = jnp.sum(jnp.where(at, above, 0.0), axis=1, keepdims=True)
        above = jnp.where(at, 1.0, above)
        split = jnp.where(at, 0.0, v) - (b / jnp.where(odd, a, 1.0)) * above
        v = jnp.where(odd, split, v)
        pivot = jnp.sum(jnp.where(lane == row, v, 0.0), axis=1, keepdims=True)
        done.append(v * lax.rsqrt(pivot))
    return done


def start_kernel(weights, rows, start):
    start[...] = nt(weights[...], rows[...], None)


def links_kernel(n_inner, place, bins, pairs, hots, links):
    column, group = place[0], place[1]
    odd = column % 2
    step = 2 * odd - 1
    others = (column, column - step, column + step)
    bin_of = lax.broadcasted_iota(jnp.int32, (BINS_COL, 1), 0)

    def hot(values, base):
        return jnp.where(values == bin_of + base, 1.0, 0.0)

    def bins_at(l, c):
        return bins[pl.ds(l * n_inner + c, 1), :]

    rows = jnp.concatenate(
        [hot(bins_at(group ^ r, column), column * BINS_COL) for r in (0, 2, 1, 3)], axis=1
    )
    left, right = pairs[0:1, :], pairs[1:2, :]
    base = column * BINS_COL
    left_mine, right_mine = hot(left, base), hot(right, base)
    for i, other in enumerate(others):
        base = other * BINS_COL
        count = nt(hot(left, base), right_mine, None) + nt(hot(right, base), left_mine, None)
        linked = jnp.where(count > 0.5, 1.0, 0.0)
        links[i] = nn(linked, rows, None)
        theirs = bins_at(group, jnp.clip(other, 0, n_inner - 1))
        hots[i] = hot(theirs, base)


def turn_kernel(r0, r1, r2, r3, turned, norms):
    span = r0.shape[0]
    for i, rows in enumerate((r0, r1, r2, r3)):
        at = slice(i * span, (i + 1) * span)
        value = rows[...].T
        turned[:, at] = value
        wide = value.astype(F32)
        norms[:, at] = jnp.sum(wide * wide, axis=0, keepdims=True)


def tile_kernel(scale, kind, part, other, hots, all_links, norms, degree, turned, high, low, out):
    x = other[...]
    wide = x.astype(F32)
    own = jnp.sum(wide * wide, axis=1, keepdims=True)
    size = x.shape[0]
    hot = hots[kind, :, part * size:(part + 1) * size]
    mask = nn(hot.T, all_links[kind], None)
    products = nn(x, turned[...], None)
    distance = own + norms[...] - 2.0 * products
    value = mask * jnp.exp(distance * scale)
    top = value.astype(BF16)
    high[...] = top
    low[...] = (value - top.astype(F32)).astype(BF16)
    out[...] = degree[...] + jnp.sum(value, axis=0, keepdims=True)


def apply_kernel(*refs):
    vectors, tiles, (keep, send) = refs[:3], refs[3:-2], refs[-2:]
    width = vectors[0].shape[0]
    half = keep.shape[1]
    total = None
    count = len(tiles) // 2
    strip = jnp.concatenate([v[...] for v in vectors], axis=1)
    top = strip.astype(BF16)
    low = (strip - top.astype(F32)).astype(BF16)
    both = jnp.concatenate([top, low], axis=0)
    at = 0
    for i in range(count):
        high_tile, low_tile = tiles[2 * i][...], tiles[2 * i + 1][...]
        size = high_tile.shape[0]
        piece = nn(both[:, at:at + size], high_tile, None)
        piece = piece[:width] + piece[width:] + nn(top[:, at:at + size], low_tile, None)
        total = piece if total is None else total + piece
        at += size
    keep[...] = total[:, :half]
    send[...] = total[:, half:]


def gram_kernel(mine, got, inv_root, start, image, image_next, packed):
    value = inv_root[...] * (mine[...] + got[...])
    image_next[...] = value
    first, begin = image[...], start[...]
    width = first.shape[0]
    packed[:width, :] = jnp.concatenate(
        [nt(begin, first), nt(first, first), nt(first, value), nt(value, value)], axis=1
    )
    gram = nt(begin, begin)
    packed[width:, :] = jnp.concatenate(
        [gram[8 * i:8 * i + 8, :] for i in range(width // 8)], axis=1
    )


def spread_kernel(mine, got, copies):
    copies[...] = jnp.broadcast_to((mine[...] + got[...])[None], copies.shape)


def last_kernel(parts, v0, v1, v2, basis, coefficients):
    packed = jnp.sum(parts[...], axis=0)
    width = v0.shape[0]
    m_01, m_11, m_12, m_22 = [packed[:width, width * i:width * (i + 1)] for i in range(4)]
    m_00 = jnp.concatenate(
        [packed[width:, width * i:width * (i + 1)] for i in range(width // 8)], axis=0
    )
    blank = jnp.zeros((width, LANES - 3 * width), F32)
    gram = jnp.concatenate(
        [
            jnp.concatenate([m_00, m_01, m_11, blank], axis=1),
            jnp.concatenate([m_01.T, m_11, m_12, blank], axis=1),
            jnp.concatenate([m_11, m_12.T, m_22, blank], axis=1),
        ],
        axis=0,
    )
    rows = 3 * width
    groups = [gram[8 * i:8 * i + 8, :] for i in range(rows // 8)]
    whole = jnp.concatenate(eliminate(groups), axis=0)[:, :rows]
    row = lax.broadcasted_iota(jnp.int32, (rows, rows), 0)
    col = lax.broadcasted_iota(jnp.int32, (rows, rows), 1)
    upper = jnp.where(col >= row, whole, 0.0)
    pivot = jnp.sum(jnp.where(col == row, whole, 0.0), axis=1, keepdims=True)
    inverse = jnp.where(col < row, whole, jnp.where(col == row, 1.0 / pivot, 0.0))
    basis[...] = nn(inverse, jnp.concatenate([v0[...], v1[...], v2[...]], axis=0))

    def block(value, i, j):
        return value[width * i:width * (i + 1), width * j:width * (j + 1)]

    z_00, z_11 = block(inverse, 0, 0), block(inverse, 1, 1)
    r_01, r_11 = block(upper, 0, 1), block(upper, 1, 1)
    first = nt(jnp.concatenate([r_01, r_11], axis=0), z_00)
    mixed = block(upper, 1, 2) - nn(r_11, tn(z_00, r_01))
    second = nt(jnp.concatenate([mixed, block(upper, 2, 2)], axis=0), z_11)
    coefficients[0] = first[:width]
    coefficients[1] = first[width:]
    coefficients[2] = second[:width]
    coefficients[3] = second[width:]


def routes(n_loop, n_inner):
    def build(loop_of, inner_of):
        pairs = []
        for l in range(n_loop):
            for c in range(n_inner):
                if 0 <= inner_of(c) < n_inner:
                    pairs.append((l * n_inner + c, loop_of(l) * n_inner + inner_of(c)))
        return pairs

    same = lambda v: v
    return {
        "core": build(lambda l: l ^ 1, same),
        "row": build(lambda l: l ^ 2, same),
        "near": build(same, lambda c: c ^ 1),
        "far": build(same, lambda c: c + 1 if c % 2 else c - 1),
        "relay": build(same, lambda c: c - 2 if c % 2 else c + 2),
    }


def steps(snapshots, bins, pairs, start_weights):
    row_count, features = snapshots.shape
    width = start_weights.shape[1]
    n_row = lax.axis_size("row")
    n_loop = n_row * lax.axis_size("core")
    n_inner = lax.axis_size("inner")
    column = lax.axis_index("inner")
    group = lax.axis_index(("row", "core"))
    route = routes(n_loop, n_inner)

    def move(value, name):
        return lax.ppermute(value, ALL, route[name])

    half = row_count // 2
    across = move(snapshots, "row")
    mate = move(snapshots, "core")
    near_a = move(snapshots[:half], "near")
    near_b = move(snapshots[half:], "near")
    far_a = move(near_a, "relay")
    far_b = move(near_b, "relay")
    across_mate = move(across, "core")
    group_rows = (snapshots, across, mate, across_mate)

    place = jnp.where(jnp.arange(2) == 0, column, group).astype(jnp.int32)
    hots, links = call(
        functools.partial(links_kernel, n_inner),
        [((3, BINS_COL, row_count), F32), ((3, BINS_COL, n_loop * row_count), F32)],
        place, bins.reshape(n_loop * n_inner, row_count), pairs.T,
        scalars=1,
    )

    (start,) = call(start_kernel, [((width, row_count), F32)], start_weights.T, snapshots)

    span = n_loop * row_count
    turned, norms = call(turn_kernel, [((features, span), BF16), ((1, span), F32)], *group_rows)
    degree = jnp.zeros((1, span), F32)
    tiles = []
    for kind, part, rows in (
        (0, 0, snapshots), (1, 0, near_a), (1, 1, near_b), (2, 0, far_a), (2, 1, far_b)
    ):
        size = rows.shape[0]
        high, low, degree = call(
            functools.partial(tile_kernel, -3.0 / features, kind, part),
            [((size, span), BF16), ((size, span), BF16), ((1, span), F32)],
            rows, hots, links, norms, degree, turned,
        )
        tiles += [high, low]

    def group_sum(keep, send):
        keep = keep + move(send, "core")
        return keep[:, :row_count], move(keep[:, row_count:], "row")

    mine, got = group_sum(degree[:, :span // 2], degree[:, span // 2:])
    inv_root = lax.rsqrt(mine + got)

    def apply(vectors):
        scaled = inv_root * vectors
        keep, send = call(
            apply_kernel,
            [((width, span // 2), F32)] * 2,
            scaled, move(scaled, "near"), move(scaled, "far"), *tiles,
        )
        return group_sum(keep, send)

    mine, got = apply(start)
    image_1 = inv_root * (mine + got)
    mine, got = apply(image_1)
    image_2, packed = call(
        gram_kernel,
        [((width, row_count), F32), ((width + 8, 4 * width), F32)],
        mine, got, inv_root, start, image_1,
    )
    (copies,) = call(
        spread_kernel,
        [((n_row * n_inner,) + packed.shape, F32)],
        packed, move(packed, "core"),
    )
    parts = lax.all_to_all(copies, ("row", "inner"), 0, 0)
    basis, coefficients = call(
        last_kernel,
        [((3 * width, row_count), F32), ((4, width, width), F32)],
        parts, start, image_1, image_2,
        final=True,
    )
    return basis.T, coefficients


def solution(mesh):
    n_loop, n_inner = mesh.shape["loop"], mesh.shape["inner"]
    fine = Mesh(mesh.devices.reshape(n_loop // 2, 2, n_inner), ALL)
    in_specs = (P(ALL, None), P(), P(), P())
    out_specs = (P(ALL, None), P())
    return jax.shard_map(steps, mesh=fine, in_specs=in_specs, out_specs=out_specs, check_vma=False)
```

```python
import functools

import jax
import jax.numpy as jnp
from jax import lax
from jax.experimental import pallas as pl
from jax.experimental.pallas import tpu as pltpu
from jax.sharding import Mesh, PartitionSpec as P

BINS_COL = 8
LANES = 128
KERNEL_VMEM = 16 * 2**20
ALL = ("row", "core", "inner")
HI = lax.Precision.HIGHEST
F32 = jnp.float32
BF16 = jnp.bfloat16


def nt(left, right, precision=HI):
    return lax.dot_general(
        left, right, (((1,), (1,)), ((), ())), precision=precision, preferred_element_type=F32
    )


def nn(left, right, precision=HI):
    return lax.dot_general(
        left, right, (((1,), (0,)), ((), ())), precision=precision, preferred_element_type=F32
    )


def tn(left, right):
    return nn(left.T, right)


def call(kernel, outs, *args, final=False, scalars=0):
    result = jax.ShapeDtypeStruct if final else pltpu.VMEM
    vectors = [pltpu.with_memory_space_constraint(a, pltpu.VMEM) for a in args[scalars:]]
    return pl.pallas_call(
        kernel,
        out_shape=[result(shape, kind) for shape, kind in outs],
        in_specs=[pl.BlockSpec(memory_space=pltpu.SMEM)] * scalars
        + [pl.BlockSpec(memory_space=pltpu.VMEM)] * len(vectors),
        compiler_params=pltpu.CompilerParams(vmem_limit_bytes=KERNEL_VMEM),
    )(*args[:scalars], *vectors)


def spread(value):
    return jnp.broadcast_to(value, (8, LANES))


def pivot_rows(row_a, row_b, a, b, d, lane, at):
    row_a = jnp.where(lane == at, 1.0, jnp.where(lane == at + 1, 0.0, row_a))
    row_b = jnp.where(lane == at, 0.0, jnp.where(lane == at + 1, 1.0, row_b))
    inverse = 1.0 / (a * d - b * b)
    a, b, d = a * inverse, b * inverse, d * inverse
    return d * row_a - b * row_b, a * row_b - b * row_a


def eliminate(groups):
    sub = lax.broadcasted_iota(jnp.int32, (8, LANES), 0)
    lane = lax.broadcasted_iota(jnp.int32, (8, LANES), 1)
    g = list(groups)
    for j in range(0, 8 * len(g), 4):
        q, s = divmod(j, 8)
        cols = [[spread(v[:, j + k:j + k + 1]) for v in g[q:]] for k in range(4)]
        rows = [spread(g[q][s + k:s + k + 1, :]) for k in range(4)]
        m = [[spread(cols[k][0][s + i:s + i + 1, :]) for k in range(4)] for i in range(4)]
        first_pair = jnp.logical_or(lane == j, lane == j + 1)
        last_pair = jnp.logical_or(lane == j + 2, lane == j + 3)
        w0, w1 = pivot_rows(rows[0], rows[1], m[0][0], m[0][1], m[1][1], lane, j)
        inverse = 1.0 / (m[0][0] * m[1][1] - m[0][1] * m[0][1])
        u = [
            ((m[1][1] * m[0][k] - m[0][1] * m[1][k]) * inverse,
             (m[0][0] * m[1][k] - m[0][1] * m[0][k]) * inverse)
            for k in (2, 3)
        ]
        third = jnp.where(first_pair, 0.0, rows[2]) - (m[2][0] * w0 + m[2][1] * w1)
        fourth = jnp.where(first_pair, 0.0, rows[3]) - (m[3][0] * w0 + m[3][1] * w1)
        a = m[2][2] - (m[2][0] * u[0][0] + m[2][1] * u[0][1])
        b = m[2][3] - (m[2][0] * u[1][0] + m[2][1] * u[1][1])
        d = m[3][3] - (m[3][0] * u[1][0] + m[3][1] * u[1][1])
        w2, w3 = pivot_rows(third, fourth, a, b, d, lane, j + 2)
        clear_0, clear_1 = jnp.where(last_pair, 0.0, w0), jnp.where(last_pair, 0.0, w1)
        pair = jnp.logical_or(first_pair, last_pair)
        for i in range(len(g) - q):
            c0, c1 = cols[0][i], cols[1][i]
            c2 = cols[2][i] - (c0 * u[0][0] + c1 * u[0][1])
            c3 = cols[3][i] - (c0 * u[1][0] + c1 * u[1][1])
            old = g[q + i]
            new = jnp.where(pair, 0.0, old) - (c0 * clear_0 + c1 * clear_1) - (c2 * w2 + c3 * w3)
            if i == 0:
                new = jnp.where(sub > s + 3, new, old)
                new = jnp.where(sub == s + 2, third, jnp.where(sub == s + 3, fourth, new))
            g[q + i] = new
    odd = sub % 2 == 1
    done = []
    for q, v in enumerate(g):
        row = sub + 8 * q
        above = pltpu.roll(v, 1, 0)
        at = lane == row - 1
        b = jnp.sum(jnp.where(at, v, 0.0), axis=1, keepdims=True)
        a = jnp.sum(jnp.where(at, above, 0.0), axis=1, keepdims=True)
        above = jnp.where(at, 1.0, above)
        split = jnp.where(at, 0.0, v) - (b / jnp.where(odd, a, 1.0)) * above
        v = jnp.where(odd, split, v)
        pivot = jnp.sum(jnp.where(lane == row, v, 0.0), axis=1, keepdims=True)
        done.append(v * lax.rsqrt(pivot))
    return done


def links_kernel(n_inner, place, bins, pairs, hots, links):
    column, group = place[0], place[1]
    odd = column % 2
    step = 2 * odd - 1
    others = (column, column - step, column + step)
    bin_of = lax.broadcasted_iota(jnp.int32, (BINS_COL, 1), 0)

    def hot(values, base):
        return jnp.where(values == bin_of + base, 1.0, 0.0)

    def bins_at(l, c):
        return bins[pl.ds(l * n_inner + c, 1), :]

    rows = jnp.concatenate(
        [hot(bins_at(group ^ r, column), column * BINS_COL) for r in range(4)], axis=1
    )
    left, right = pairs[0:1, :], pairs[1:2, :]
    base = column * BINS_COL
    left_mine, right_mine = hot(left, base), hot(right, base)
    for i, other in enumerate(others):
        base = other * BINS_COL
        count = nt(hot(left, base), right_mine, None) + nt(hot(right, base), left_mine, None)
        linked = jnp.where(count > 0.5, 1.0, 0.0)
        links[i] = nn(linked, rows, None)
        theirs = bins_at(group, jnp.clip(other, 0, n_inner - 1))
        hots[i] = hot(theirs, base)


def turn_kernel(weights, r0, r1, turned, norms, start):
    span = r0.shape[0]
    for i, rows in enumerate((r0, r1)):
        at = slice(i * span, (i + 1) * span)
        value = rows[...].T
        turned[:, at] = value
        wide = value.astype(F32)
        norms[:, at] = jnp.sum(wide * wide, axis=0, keepdims=True)
        start[:, at] = nn(weights[...], value, None)


def tile_kernel(scale, kind, part, other, hots, all_links, *refs):
    groups, (high, low, out) = refs[:4], refs[-3:]
    first = len(refs) == 7
    x = other[...]
    wide = x.astype(F32)
    own = jnp.sum(wide * wide, axis=1, keepdims=True)
    size = x.shape[0]
    hot = hots[kind, :, part * size:(part + 1) * size].T
    span = groups[0].shape[1]
    for i in range(2):
        turned, norms = groups[2 * i:2 * i + 2]
        at = slice(i * span, (i + 1) * span)
        mask = nn(hot, all_links[kind, :, at], None)
        distance = own + norms[...] - 2.0 * nn(x, turned[...], None)
        value = mask * jnp.exp(distance * scale)
        top = value.astype(BF16)
        high[:, at] = top
        low[:, at] = (value - top.astype(F32)).astype(BF16)
        total = jnp.sum(value, axis=0, keepdims=True)
        out[:, at] = total if first else refs[4][:, at] + total


def send_back_kernel(degree, got, start_a, start_b, *refs):
    tiles, (inv_root, own, near, far) = refs[:-4], refs[-4:]
    width, size = own.shape
    other = jnp.concatenate([got[:, size * i:size * (i + 1)] for i in (2, 3, 0, 1)], axis=1)
    scale = lax.rsqrt(degree[...] + other)
    inv_root[...] = scale[:, :size]
    vectors = (jnp.concatenate([start_a[...], start_b[...]], axis=1) * scale).T
    top = vectors.astype(BF16)
    low = (vectors - top.astype(F32)).astype(BF16)
    both = jnp.concatenate([top, low], axis=1)
    pieces = []
    for i in range(len(tiles) // 2):
        piece = nn(tiles[2 * i][...], both, None)
        pieces.append(piece[:, :width] + piece[:, width:] + nn(tiles[2 * i + 1][...], top, None))
    own[...] = pieces[0].T
    near[...] = jnp.concatenate(pieces[1:3], axis=0).T
    far[...] = jnp.concatenate(pieces[3:5], axis=0).T


def apply_kernel(*refs):
    vectors, tiles, (keep, send) = refs[:3], refs[3:-2], refs[-2:]
    width = vectors[0].shape[0]
    half = keep.shape[1]
    total = None
    count = len(tiles) // 2
    strip = jnp.concatenate([v[...] for v in vectors], axis=1)
    top = strip.astype(BF16)
    low = (strip - top.astype(F32)).astype(BF16)
    both = jnp.concatenate([top, low], axis=0)
    at = 0
    for i in range(count):
        high_tile, low_tile = tiles[2 * i][...], tiles[2 * i + 1][...]
        size = high_tile.shape[0]
        piece = nn(both[:, at:at + size], high_tile, None)
        piece = piece[:width] + piece[width:] + nn(top[:, at:at + size], low_tile, None)
        total = piece if total is None else total + piece
        at += size
    size = half // 2
    keep[:, :size], keep[:, size:] = total[:, :size], total[:, half:half + size]
    send[:, :size], send[:, size:] = total[:, size:half], total[:, half + size:]


def gram_kernel(mine, got, inv_root, start, image, image_next, packed):
    value = inv_root[...] * (mine[...] + got[...])
    image_next[...] = value
    first, begin = image[...], start[...]
    width = first.shape[0]
    packed[:width, :] = jnp.concatenate(
        [nt(begin, first), nt(first, first), nt(first, value), nt(value, value)], axis=1
    )
    gram = nt(begin, begin)
    packed[width:, :] = jnp.concatenate(
        [gram[8 * i:8 * i + 8, :] for i in range(width // 8)], axis=1
    )


def spread_kernel(mine, got, copies):
    copies[...] = jnp.broadcast_to((mine[...] + got[...])[None], copies.shape)


def last_kernel(parts, v0, v1, v2, basis, coefficients):
    packed = jnp.sum(parts[...], axis=0)
    width = v0.shape[0]
    m_01, m_11, m_12, m_22 = [packed[:width, width * i:width * (i + 1)] for i in range(4)]
    m_00 = jnp.concatenate(
        [packed[width:, width * i:width * (i + 1)] for i in range(width // 8)], axis=0
    )
    blank = jnp.zeros((width, LANES - 3 * width), F32)
    gram = jnp.concatenate(
        [
            jnp.concatenate([m_00, m_01, m_11, blank], axis=1),
            jnp.concatenate([m_01.T, m_11, m_12, blank], axis=1),
            jnp.concatenate([m_11, m_12.T, m_22, blank], axis=1),
        ],
        axis=0,
    )
    rows = 3 * width
    groups = [gram[8 * i:8 * i + 8, :] for i in range(rows // 8)]
    whole = jnp.concatenate(eliminate(groups), axis=0)[:, :rows]
    row = lax.broadcasted_iota(jnp.int32, (rows, rows), 0)
    col = lax.broadcasted_iota(jnp.int32, (rows, rows), 1)
    upper = jnp.where(col >= row, whole, 0.0)
    pivot = jnp.sum(jnp.where(col == row, whole, 0.0), axis=1, keepdims=True)
    inverse = jnp.where(col < row, whole, jnp.where(col == row, 1.0 / pivot, 0.0))
    basis[...] = nn(inverse, jnp.concatenate([v0[...], v1[...], v2[...]], axis=0))

    def block(value, i, j):
        return value[width * i:width * (i + 1), width * j:width * (j + 1)]

    z_00, z_11 = block(inverse, 0, 0), block(inverse, 1, 1)
    r_01, r_11 = block(upper, 0, 1), block(upper, 1, 1)
    first = nt(jnp.concatenate([r_01, r_11], axis=0), z_00)
    mixed = block(upper, 1, 2) - nn(r_11, tn(z_00, r_01))
    second = nt(jnp.concatenate([mixed, block(upper, 2, 2)], axis=0), z_11)
    coefficients[0] = first[:width]
    coefficients[1] = first[width:]
    coefficients[2] = second[:width]
    coefficients[3] = second[width:]


def routes(n_loop, n_inner):
    def build(loop_of, inner_of):
        pairs = []
        for l in range(n_loop):
            for c in range(n_inner):
                if 0 <= inner_of(c) < n_inner:
                    pairs.append((l * n_inner + c, loop_of(l) * n_inner + inner_of(c)))
        return pairs

    same = lambda v: v
    return {
        "core": build(lambda l: l ^ 1, same),
        "row": build(lambda l: l ^ 2, same),
        "near": build(same, lambda c: c ^ 1),
        "far": build(same, lambda c: c + 1 if c % 2 else c - 1),
        "relay": build(same, lambda c: c - 2 if c % 2 else c + 2),
    }


def steps(snapshots, bins, pairs, start_weights):
    row_count, features = snapshots.shape
    width = start_weights.shape[1]
    n_row = lax.axis_size("row")
    n_loop = n_row * lax.axis_size("core")
    n_inner = lax.axis_size("inner")
    column = lax.axis_index("inner")
    group = lax.axis_index(("row", "core"))
    route = routes(n_loop, n_inner)

    def move(value, name):
        return lax.ppermute(value, ALL, route[name])

    half = row_count // 2
    across = move(snapshots, "row")
    mate = move(snapshots, "core")
    near_a = move(snapshots[:half], "near")
    near_b = move(snapshots[half:], "near")
    far_a = move(near_a, "relay")
    far_b = move(near_b, "relay")
    across_mate = move(across, "core")

    place = jnp.where(jnp.arange(2) == 0, column, group).astype(jnp.int32)
    hots, links = call(
        functools.partial(links_kernel, n_inner),
        [((3, BINS_COL, row_count), F32), ((3, BINS_COL, n_loop * row_count), F32)],
        place, bins.reshape(n_loop * n_inner, row_count), pairs.T,
        scalars=1,
    )

    span = n_loop * row_count
    turn_outs = [((features, span // 2), BF16), ((1, span // 2), F32), ((width, span // 2), F32)]
    turned_a, norms_a, start_a = call(
        turn_kernel, turn_outs, start_weights.T, snapshots, mate
    )
    turned_b, norms_b, start_b = call(turn_kernel, turn_outs, start_weights.T, across, across_mate)
    tiles = []
    degree = ()
    for kind, part, rows in (
        (0, 0, snapshots), (1, 0, near_a), (1, 1, near_b), (2, 0, far_a), (2, 1, far_b)
    ):
        size = rows.shape[0]
        high, low, *degree = call(
            functools.partial(tile_kernel, -3.0 / features, kind, part),
            [((size, span), BF16), ((size, span), BF16), ((1, span), F32)],
            rows, hots, links, turned_a, norms_a, turned_b, norms_b, *degree,
        )
        tiles += [high, low]
    (degree,) = degree

    got = move(degree, "core")
    degree = degree + jnp.concatenate(
        [got[:, row_count * i:row_count * (i + 1)] for i in (1, 0, 3, 2)], axis=1
    )
    block = ((width, row_count), F32)
    inv_root, own, near, far = call(
        send_back_kernel,
        [((1, row_count), F32), block, block, block],
        degree, move(degree, "row"), start_a, start_b, *tiles,
    )
    start = start_a[:, :row_count]
    image_1 = inv_root * (own + move(near, "near") + move(far, "far"))

    scaled = inv_root * image_1
    keep, send = call(
        apply_kernel,
        [((width, span // 2), F32)] * 2,
        scaled, move(scaled, "near"), move(scaled, "far"), *tiles,
    )
    keep = keep + move(send, "core")
    mine, got = keep[:, :row_count], move(keep[:, row_count:], "row")
    image_2, packed = call(
        gram_kernel,
        [((width, row_count), F32), ((width + 8, 4 * width), F32)],
        mine, got, inv_root, start, image_1,
    )
    (copies,) = call(
        spread_kernel,
        [((n_row * n_inner,) + packed.shape, F32)],
        packed, move(packed, "core"),
    )
    parts = lax.all_to_all(copies, ("row", "inner"), 0, 0)
    basis, coefficients = call(
        last_kernel,
        [((3 * width, row_count), F32), ((4, width, width), F32)],
        parts, start, image_1, image_2,
        final=True,
    )
    return basis.T, coefficients


def solution(mesh):
    n_loop, n_inner = mesh.shape["loop"], mesh.shape["inner"]
    fine = Mesh(mesh.devices.reshape(n_loop // 2, 2, n_inner), ALL)
    in_specs = (P(ALL, None), P(), P(), P())
    out_specs = (P(ALL, None), P())
    return jax.shard_map(steps, mesh=fine, in_specs=in_specs, out_specs=out_specs, check_vma=False)
```

```python
import functools

import jax
import jax.numpy as jnp
from jax import lax
from jax.experimental import pallas as pl
from jax.experimental.pallas import tpu as pltpu
from jax.sharding import Mesh, PartitionSpec as P

BINS_COL = 8
LANES = 128
KERNEL_VMEM = 16 * 2**20
ALL = ("row", "core", "inner")
HI = lax.Precision.HIGHEST
F32 = jnp.float32
BF16 = jnp.bfloat16


def nt(left, right, precision=HI):
    return lax.dot_general(
        left, right, (((1,), (1,)), ((), ())), precision=precision, preferred_element_type=F32
    )


def nn(left, right, precision=HI):
    return lax.dot_general(
        left, right, (((1,), (0,)), ((), ())), precision=precision, preferred_element_type=F32
    )


def tn(left, right):
    return nn(left.T, right)


def call(kernel, outs, *args, final=False, scalars=0):
    result = jax.ShapeDtypeStruct if final else pltpu.VMEM
    vectors = [pltpu.with_memory_space_constraint(a, pltpu.VMEM) for a in args[scalars:]]
    return pl.pallas_call(
        kernel,
        out_shape=[result(shape, kind) for shape, kind in outs],
        in_specs=[pl.BlockSpec(memory_space=pltpu.SMEM)] * scalars
        + [pl.BlockSpec(memory_space=pltpu.VMEM)] * len(vectors),
        compiler_params=pltpu.CompilerParams(vmem_limit_bytes=KERNEL_VMEM),
    )(*args[:scalars], *vectors)


def spread(value):
    return jnp.broadcast_to(value, (8, LANES))


def pivot_rows(row_a, row_b, a, b, d, lane, at):
    row_a = jnp.where(lane == at, 1.0, jnp.where(lane == at + 1, 0.0, row_a))
    row_b = jnp.where(lane == at, 0.0, jnp.where(lane == at + 1, 1.0, row_b))
    inverse = 1.0 / (a * d - b * b)
    a, b, d = a * inverse, b * inverse, d * inverse
    return d * row_a - b * row_b, a * row_b - b * row_a


def eliminate(groups):
    sub = lax.broadcasted_iota(jnp.int32, (8, LANES), 0)
    lane = lax.broadcasted_iota(jnp.int32, (8, LANES), 1)
    g = list(groups)
    for j in range(0, 8 * len(g), 4):
        q, s = divmod(j, 8)
        cols = [[spread(v[:, j + k:j + k + 1]) for v in g[q:]] for k in range(4)]
        rows = [spread(g[q][s + k:s + k + 1, :]) for k in range(4)]
        m = [[spread(cols[k][0][s + i:s + i + 1, :]) for k in range(4)] for i in range(4)]
        first_pair = jnp.logical_or(lane == j, lane == j + 1)
        last_pair = jnp.logical_or(lane == j + 2, lane == j + 3)
        w0, w1 = pivot_rows(rows[0], rows[1], m[0][0], m[0][1], m[1][1], lane, j)
        inverse = 1.0 / (m[0][0] * m[1][1] - m[0][1] * m[0][1])
        u = [
            ((m[1][1] * m[0][k] - m[0][1] * m[1][k]) * inverse,
             (m[0][0] * m[1][k] - m[0][1] * m[0][k]) * inverse)
            for k in (2, 3)
        ]
        third = jnp.where(first_pair, 0.0, rows[2]) - (m[2][0] * w0 + m[2][1] * w1)
        fourth = jnp.where(first_pair, 0.0, rows[3]) - (m[3][0] * w0 + m[3][1] * w1)
        a = m[2][2] - (m[2][0] * u[0][0] + m[2][1] * u[0][1])
        b = m[2][3] - (m[2][0] * u[1][0] + m[2][1] * u[1][1])
        d = m[3][3] - (m[3][0] * u[1][0] + m[3][1] * u[1][1])
        w2, w3 = pivot_rows(third, fourth, a, b, d, lane, j + 2)
        clear_0, clear_1 = jnp.where(last_pair, 0.0, w0), jnp.where(last_pair, 0.0, w1)
        pair = jnp.logical_or(first_pair, last_pair)
        for i in range(len(g) - q):
            c0, c1 = cols[0][i], cols[1][i]
            c2 = cols[2][i] - (c0 * u[0][0] + c1 * u[0][1])
            c3 = cols[3][i] - (c0 * u[1][0] + c1 * u[1][1])
            old = g[q + i]
            new = jnp.where(pair, 0.0, old) - (c0 * clear_0 + c1 * clear_1) - (c2 * w2 + c3 * w3)
            if i == 0:
                new = jnp.where(sub > s + 3, new, old)
                new = jnp.where(sub == s + 2, third, jnp.where(sub == s + 3, fourth, new))
            g[q + i] = new
    odd = sub % 2 == 1
    done = []
    for q, v in enumerate(g):
        row = sub + 8 * q
        above = pltpu.roll(v, 1, 0)
        at = lane == row - 1
        b = jnp.sum(jnp.where(at, v, 0.0), axis=1, keepdims=True)
        a = jnp.sum(jnp.where(at, above, 0.0), axis=1, keepdims=True)
        above = jnp.where(at, 1.0, above)
        split = jnp.where(at, 0.0, v) - (b / jnp.where(odd, a, 1.0)) * above
        v = jnp.where(odd, split, v)
        pivot = jnp.sum(jnp.where(lane == row, v, 0.0), axis=1, keepdims=True)
        done.append(v * lax.rsqrt(pivot))
    return done


def links_kernel(n_inner, place, bins, pairs, hots, links):
    column, group = place[0], place[1]
    odd = column % 2
    step = 2 * odd - 1
    others = (column, column - step, column + step)
    bin_of = lax.broadcasted_iota(jnp.int32, (BINS_COL, 1), 0)

    def hot(values, base):
        return jnp.where(values == bin_of + base, 1.0, 0.0)

    def bins_at(l, c):
        return bins[pl.ds(l * n_inner + c, 1), :]

    rows = jnp.concatenate(
        [hot(bins_at(group ^ r, column), column * BINS_COL) for r in range(4)], axis=1
    )
    left, right = pairs[0:1, :], pairs[1:2, :]
    base = column * BINS_COL
    left_mine, right_mine = hot(left, base), hot(right, base)
    for i, other in enumerate(others):
        base = other * BINS_COL
        count = nt(hot(left, base), right_mine, None) + nt(hot(right, base), left_mine, None)
        linked = jnp.where(count > 0.5, 1.0, 0.0)
        links[i] = nn(linked, rows, None)
        theirs = bins_at(group, jnp.clip(other, 0, n_inner - 1))
        hots[i] = hot(theirs, base)


def turn_kernel(weights, r0, r1, turned, norms, start):
    span = r0.shape[0]
    for i, rows in enumerate((r0, r1)):
        at = slice(i * span, (i + 1) * span)
        value = rows[...].T
        turned[:, at] = value
        wide = value.astype(F32)
        norms[:, at] = jnp.sum(wide * wide, axis=0, keepdims=True)
        start[:, at] = nn(weights[...], value, None)


def tile_kernel(scale, kind, part, other, hots, all_links, *refs):
    groups, (high, low, out) = refs[:4], refs[-3:]
    first = len(refs) == 7
    x = other[...]
    wide = x.astype(F32)
    own = jnp.sum(wide * wide, axis=1, keepdims=True)
    size = x.shape[0]
    hot = hots[kind, :, part * size:(part + 1) * size].T
    span = groups[0].shape[1]
    for i in range(2):
        turned, norms = groups[2 * i:2 * i + 2]
        at = slice(i * span, (i + 1) * span)
        mask = nn(hot, all_links[kind, :, at], None)
        distance = own + norms[...] - 2.0 * nn(x, turned[...], None)
        value = mask * jnp.exp(distance * scale)
        top = value.astype(BF16)
        high[:, at] = top
        low[:, at] = (value - top.astype(F32)).astype(BF16)
        total = jnp.sum(value, axis=0, keepdims=True)
        out[:, at] = total if first else refs[4][:, at] + total


def send_back_kernel(degree, got, start_a, start_b, *refs):
    tiles, (inv_root, own, near, far) = refs[:-4], refs[-4:]
    width, size = own.shape
    other = jnp.concatenate([got[:, size * i:size * (i + 1)] for i in (2, 3, 0, 1)], axis=1)
    scale = lax.rsqrt(degree[...] + other)
    inv_root[...] = scale[:, :size]
    vectors = (jnp.concatenate([start_a[...], start_b[...]], axis=1) * scale).T
    top = vectors.astype(BF16)
    low = (vectors - top.astype(F32)).astype(BF16)
    both = jnp.concatenate([top, low], axis=1)
    pieces = []
    for i in range(len(tiles) // 2):
        piece = nn(tiles[2 * i][...], both, None)
        pieces.append(piece[:, :width] + piece[:, width:] + nn(tiles[2 * i + 1][...], top, None))
    own[...] = pieces[0].T
    near[...] = jnp.concatenate(pieces[1:3], axis=0).T
    far[...] = jnp.concatenate(pieces[3:5], axis=0).T


def apply_kernel(*refs):
    vectors, tiles, (keep, send) = refs[:3], refs[3:-2], refs[-2:]
    width = vectors[0].shape[0]
    half = keep.shape[1]
    total = None
    count = len(tiles) // 2
    strip = jnp.concatenate([v[...] for v in vectors], axis=1)
    top = strip.astype(BF16)
    low = (strip - top.astype(F32)).astype(BF16)
    both = jnp.concatenate([top, low], axis=0)
    at = 0
    for i in range(count):
        high_tile, low_tile = tiles[2 * i][...], tiles[2 * i + 1][...]
        size = high_tile.shape[0]
        piece = nn(both[:, at:at + size], high_tile, None)
        piece = piece[:width] + piece[width:] + nn(top[:, at:at + size], low_tile, None)
        total = piece if total is None else total + piece
        at += size
    size = half // 2
    keep[:, :size], keep[:, size:] = total[:, :size], total[:, half:half + size]
    send[:, :size], send[:, size:] = total[:, size:half], total[:, half + size:]


def fold(upper, lower):
    width = upper.shape[0]
    row = lax.broadcasted_iota(jnp.int32, upper.shape, 0)
    col = lax.broadcasted_iota(jnp.int32, upper.shape, 1)
    both = jnp.where(col >= row, upper, lower)
    flat = jnp.concatenate([both[8 * i:8 * i + 8, :] for i in range(width // 8)], axis=1)
    return flat, jnp.sum(jnp.where(col == row, lower, 0.0), axis=0, keepdims=True)


def unfold(flat, diagonal):
    width = diagonal.shape[1]
    both = jnp.concatenate([flat[:, width * i:width * (i + 1)] for i in range(width // 8)], axis=0)
    turned = both.T
    row = lax.broadcasted_iota(jnp.int32, both.shape, 0)
    col = lax.broadcasted_iota(jnp.int32, both.shape, 1)
    upper = jnp.where(col >= row, both, turned)
    return upper, jnp.where(col < row, both, jnp.where(col == row, diagonal, turned))


def gram_kernel(mine, got, inv_root, start, image, image_next, packed):
    value = inv_root[...] * (mine[...] + got[...])
    image_next[...] = value
    first, begin = image[...], start[...]
    width = first.shape[0]
    half = width // 2
    packed[:8, :], row_a = fold(nt(begin, begin), nt(begin, first))
    packed[8:16, :], row_b = fold(nt(first, first), nt(first, value))
    last = nt(value, value)
    block = jnp.concatenate([last[:half, :], last[half:, half:]], axis=1)
    rows = jnp.concatenate([row_a, row_b, jnp.zeros((6, width), F32)], axis=0)
    packed[16:, :] = jnp.concatenate([block[:8, :], block[8:, :], rows], axis=1)


def spread_kernel(mine, got, copies):
    copies[...] = jnp.broadcast_to((mine[...] + got[...])[None], copies.shape)


def last_kernel(parts, v0, v1, v2, basis, coefficients):
    packed = jnp.sum(parts[...], axis=0)
    width = v0.shape[0]
    half = width // 2
    span = width + half
    rows = packed[16:, 2 * span:2 * span + width]
    m_00, m_01 = unfold(packed[:8, :], rows[0:1, :])
    m_11, m_12 = unfold(packed[8:16, :], rows[1:2, :])
    block = jnp.concatenate([packed[16:, :span], packed[16:, span:2 * span]], axis=0)
    corner = block[:, half:width].T
    m_22 = jnp.concatenate(
        [block[:, :width], jnp.concatenate([corner, block[:, width:]], axis=1)], axis=0
    )
    blank = jnp.zeros((width, LANES - 3 * width), F32)
    gram = jnp.concatenate(
        [
            jnp.concatenate([m_00, m_01, m_11, blank], axis=1),
            jnp.concatenate([m_01, m_11, m_12, blank], axis=1),
            jnp.concatenate([m_11, m_12, m_22, blank], axis=1),
        ],
        axis=0,
    )
    rows = 3 * width
    groups = [gram[8 * i:8 * i + 8, :] for i in range(rows // 8)]
    whole = jnp.concatenate(eliminate(groups), axis=0)[:, :rows]
    row = lax.broadcasted_iota(jnp.int32, (rows, rows), 0)
    col = lax.broadcasted_iota(jnp.int32, (rows, rows), 1)
    upper = jnp.where(col >= row, whole, 0.0)
    pivot = jnp.sum(jnp.where(col == row, whole, 0.0), axis=1, keepdims=True)
    inverse = jnp.where(col < row, whole, jnp.where(col == row, 1.0 / pivot, 0.0))
    basis[...] = nn(inverse, jnp.concatenate([v0[...], v1[...], v2[...]], axis=0))

    def block(value, i, j):
        return value[width * i:width * (i + 1), width * j:width * (j + 1)]

    z_00, z_11 = block(inverse, 0, 0), block(inverse, 1, 1)
    r_01, r_11 = block(upper, 0, 1), block(upper, 1, 1)
    first = nt(jnp.concatenate([r_01, r_11], axis=0), z_00)
    mixed = block(upper, 1, 2) - nn(r_11, tn(z_00, r_01))
    second = nt(jnp.concatenate([mixed, block(upper, 2, 2)], axis=0), z_11)
    coefficients[0] = first[:width]
    coefficients[1] = first[width:]
    coefficients[2] = second[:width]
    coefficients[3] = second[width:]


def routes(n_loop, n_inner):
    def build(loop_of, inner_of):
        pairs = []
        for l in range(n_loop):
            for c in range(n_inner):
                if 0 <= inner_of(c) < n_inner:
                    pairs.append((l * n_inner + c, loop_of(l) * n_inner + inner_of(c)))
        return pairs

    same = lambda v: v
    return {
        "core": build(lambda l: l ^ 1, same),
        "row": build(lambda l: l ^ 2, same),
        "near": build(same, lambda c: c ^ 1),
        "far": build(same, lambda c: c + 1 if c % 2 else c - 1),
        "relay": build(same, lambda c: c - 2 if c % 2 else c + 2),
    }


def steps(snapshots, bins, pairs, start_weights):
    row_count, features = snapshots.shape
    width = start_weights.shape[1]
    n_row = lax.axis_size("row")
    n_loop = n_row * lax.axis_size("core")
    n_inner = lax.axis_size("inner")
    column = lax.axis_index("inner")
    group = lax.axis_index(("row", "core"))
    route = routes(n_loop, n_inner)

    def move(value, name):
        return lax.ppermute(value, ALL, route[name])

    half = row_count // 2
    across = move(snapshots, "row")
    mate = move(snapshots, "core")
    near_a = move(snapshots[:half], "near")
    near_b = move(snapshots[half:], "near")
    far_a = move(near_a, "relay")
    far_b = move(near_b, "relay")
    across_mate = move(across, "core")

    place = jnp.where(jnp.arange(2) == 0, column, group).astype(jnp.int32)
    hots, links = call(
        functools.partial(links_kernel, n_inner),
        [((3, BINS_COL, row_count), F32), ((3, BINS_COL, n_loop * row_count), F32)],
        place, bins.reshape(n_loop * n_inner, row_count), pairs.T,
        scalars=1,
    )

    span = n_loop * row_count
    turn_outs = [((features, span // 2), BF16), ((1, span // 2), F32), ((width, span // 2), F32)]
    turned_a, norms_a, start_a = call(
        turn_kernel, turn_outs, start_weights.T, snapshots, mate
    )
    turned_b, norms_b, start_b = call(turn_kernel, turn_outs, start_weights.T, across, across_mate)
    tiles = []
    degree = ()
    for kind, part, rows in (
        (0, 0, snapshots), (1, 0, near_a), (1, 1, near_b), (2, 0, far_a), (2, 1, far_b)
    ):
        size = rows.shape[0]
        high, low, *degree = call(
            functools.partial(tile_kernel, -3.0 / features, kind, part),
            [((size, span), BF16), ((size, span), BF16), ((1, span), F32)],
            rows, hots, links, turned_a, norms_a, turned_b, norms_b, *degree,
        )
        tiles += [high, low]
    (degree,) = degree

    got = move(degree, "core")
    degree = degree + jnp.concatenate(
        [got[:, row_count * i:row_count * (i + 1)] for i in (1, 0, 3, 2)], axis=1
    )
    block = ((width, row_count), F32)
    inv_root, own, near, far = call(
        send_back_kernel,
        [((1, row_count), F32), block, block, block],
        degree, move(degree, "row"), start_a, start_b, *tiles,
    )
    start = start_a[:, :row_count]
    image_1 = inv_root * (own + move(near, "near") + move(far, "far"))

    scaled = inv_root * image_1
    keep, send = call(
        apply_kernel,
        [((width, span // 2), F32)] * 2,
        scaled, move(scaled, "near"), move(scaled, "far"), *tiles,
    )
    keep = keep + move(send, "core")
    mine, got = keep[:, :row_count], move(keep[:, row_count:], "row")
    image_2, packed = call(
        gram_kernel,
        [((width, row_count), F32), ((24, LANES), F32)],
        mine, got, inv_root, start, image_1,
    )
    (copies,) = call(
        spread_kernel,
        [((n_row * n_inner,) + packed.shape, F32)],
        packed, move(packed, "core"),
    )
    parts = lax.all_to_all(copies, ("row", "inner"), 0, 0)
    basis, coefficients = call(
        last_kernel,
        [((3 * width, row_count), F32), ((4, width, width), F32)],
        parts, start, image_1, image_2,
        final=True,
    )
    return basis.T, coefficients


def solution(mesh):
    n_loop, n_inner = mesh.shape["loop"], mesh.shape["inner"]
    fine = Mesh(mesh.devices.reshape(n_loop // 2, 2, n_inner), ALL)
    in_specs = (P(ALL, None), P(), P(), P())
    out_specs = (P(ALL, None), P())
    return jax.shard_map(steps, mesh=fine, in_specs=in_specs, out_specs=out_specs, check_vma=False)
```

```python
import functools

import jax
import jax.numpy as jnp
from jax import lax
from jax.experimental import pallas as pl
from jax.experimental.pallas import tpu as pltpu
from jax.sharding import Mesh, PartitionSpec as P

BINS_COL = 8
LANES = 128
KERNEL_VMEM = 16 * 2**20
ALL = ("row", "core", "inner")
HI = lax.Precision.HIGHEST
F32 = jnp.float32
BF16 = jnp.bfloat16


def nt(left, right, precision=HI):
    return lax.dot_general(
        left, right, (((1,), (1,)), ((), ())), precision=precision, preferred_element_type=F32
    )


def nn(left, right, precision=HI):
    return lax.dot_general(
        left, right, (((1,), (0,)), ((), ())), precision=precision, preferred_element_type=F32
    )


def tn(left, right):
    return nn(left.T, right)


def call(kernel, outs, *args, final=False, scalars=0):
    result = jax.ShapeDtypeStruct if final else pltpu.VMEM
    vectors = [pltpu.with_memory_space_constraint(a, pltpu.VMEM) for a in args[scalars:]]
    return pl.pallas_call(
        kernel,
        out_shape=[result(shape, kind) for shape, kind in outs],
        in_specs=[pl.BlockSpec(memory_space=pltpu.SMEM)] * scalars
        + [pl.BlockSpec(memory_space=pltpu.VMEM)] * len(vectors),
        compiler_params=pltpu.CompilerParams(vmem_limit_bytes=KERNEL_VMEM),
    )(*args[:scalars], *vectors)


def spread(value):
    return jnp.broadcast_to(value, (8, LANES))


def pivot_rows(row_a, row_b, a, b, d, lane, at):
    row_a = jnp.where(lane == at, 1.0, jnp.where(lane == at + 1, 0.0, row_a))
    row_b = jnp.where(lane == at, 0.0, jnp.where(lane == at + 1, 1.0, row_b))
    inverse = 1.0 / (a * d - b * b)
    a, b, d = a * inverse, b * inverse, d * inverse
    return d * row_a - b * row_b, a * row_b - b * row_a


def eliminate(groups):
    sub = lax.broadcasted_iota(jnp.int32, (8, LANES), 0)
    lane = lax.broadcasted_iota(jnp.int32, (8, LANES), 1)
    g = list(groups)
    for j in range(0, 8 * len(g), 4):
        q, s = divmod(j, 8)
        cols = [[spread(v[:, j + k:j + k + 1]) for v in g[q:]] for k in range(4)]
        rows = [spread(g[q][s + k:s + k + 1, :]) for k in range(4)]
        m = [[spread(cols[k][0][s + i:s + i + 1, :]) for k in range(4)] for i in range(4)]
        first_pair = jnp.logical_or(lane == j, lane == j + 1)
        last_pair = jnp.logical_or(lane == j + 2, lane == j + 3)
        w0, w1 = pivot_rows(rows[0], rows[1], m[0][0], m[0][1], m[1][1], lane, j)
        inverse = 1.0 / (m[0][0] * m[1][1] - m[0][1] * m[0][1])
        u = [
            ((m[1][1] * m[0][k] - m[0][1] * m[1][k]) * inverse,
             (m[0][0] * m[1][k] - m[0][1] * m[0][k]) * inverse)
            for k in (2, 3)
        ]
        third = jnp.where(first_pair, 0.0, rows[2]) - (m[2][0] * w0 + m[2][1] * w1)
        fourth = jnp.where(first_pair, 0.0, rows[3]) - (m[3][0] * w0 + m[3][1] * w1)
        a = m[2][2] - (m[2][0] * u[0][0] + m[2][1] * u[0][1])
        b = m[2][3] - (m[2][0] * u[1][0] + m[2][1] * u[1][1])
        d = m[3][3] - (m[3][0] * u[1][0] + m[3][1] * u[1][1])
        w2, w3 = pivot_rows(third, fourth, a, b, d, lane, j + 2)
        clear_0, clear_1 = jnp.where(last_pair, 0.0, w0), jnp.where(last_pair, 0.0, w1)
        pair = jnp.logical_or(first_pair, last_pair)
        for i in range(len(g) - q):
            c0, c1 = cols[0][i], cols[1][i]
            c2 = cols[2][i] - (c0 * u[0][0] + c1 * u[0][1])
            c3 = cols[3][i] - (c0 * u[1][0] + c1 * u[1][1])
            old = g[q + i]
            new = jnp.where(pair, 0.0, old) - (c0 * clear_0 + c1 * clear_1) - (c2 * w2 + c3 * w3)
            if i == 0:
                new = jnp.where(sub > s + 3, new, old)
                new = jnp.where(sub == s + 2, third, jnp.where(sub == s + 3, fourth, new))
            g[q + i] = new
    odd = sub % 2 == 1
    done = []
    for q, v in enumerate(g):
        row = sub + 8 * q
        above = pltpu.roll(v, 1, 0)
        at = lane == row - 1
        b = jnp.sum(jnp.where(at, v, 0.0), axis=1, keepdims=True)
        a = jnp.sum(jnp.where(at, above, 0.0), axis=1, keepdims=True)
        above = jnp.where(at, 1.0, above)
        split = jnp.where(at, 0.0, v) - (b / jnp.where(odd, a, 1.0)) * above
        v = jnp.where(odd, split, v)
        pivot = jnp.sum(jnp.where(lane == row, v, 0.0), axis=1, keepdims=True)
        done.append(v * lax.rsqrt(pivot))
    return done


def links_kernel(n_inner, place, bins, pairs, hots, links):
    column, group = place[0], place[1]
    odd = column % 2
    step = 2 * odd - 1
    others = (column, column - step, column + step)
    bin_of = lax.broadcasted_iota(jnp.int32, (BINS_COL, 1), 0)

    def hot(values, base):
        return jnp.where(values == bin_of + base, 1.0, 0.0)

    def bins_at(l, c):
        return bins[pl.ds(l * n_inner + c, 1), :]

    rows = jnp.concatenate(
        [hot(bins_at(group ^ r, column), column * BINS_COL) for r in range(4)], axis=1
    )
    left, right = pairs[0:1, :], pairs[1:2, :]
    base = column * BINS_COL
    left_mine, right_mine = hot(left, base), hot(right, base)
    for i, other in enumerate(others):
        base = other * BINS_COL
        count = nt(hot(left, base), right_mine, None) + nt(hot(right, base), left_mine, None)
        linked = jnp.where(count > 0.5, 1.0, 0.0)
        links[i] = nn(linked, rows, None)
        theirs = bins_at(group, jnp.clip(other, 0, n_inner - 1))
        hots[i] = hot(theirs, base)


def turn_kernel(weights, r0, r1, turned, norms, start):
    span = r0.shape[0]
    for i, rows in enumerate((r0, r1)):
        at = slice(i * span, (i + 1) * span)
        value = rows[...].T
        turned[:, at] = value
        wide = value.astype(F32)
        norms[:, at] = jnp.sum(wide * wide, axis=0, keepdims=True)
        start[:, at] = nn(weights[...], value, None)


def tile_kernel(scale, places, hots, all_links, *refs):
    count = len(places)
    groups, others, outs = refs[:4], refs[4:4 + count], refs[-2 * count - 1:]
    degree = refs[4 + count:-2 * count - 1]
    span = groups[0].shape[1]
    totals = [degree[0][:, span * i:span * (i + 1)] if degree else 0.0 for i in range(2)]
    for k, (kind, part) in enumerate(places):
        x = others[k][...]
        wide = x.astype(F32)
        own = jnp.sum(wide * wide, axis=1, keepdims=True)
        size = x.shape[0]
        hot = hots[kind, :, part * size:(part + 1) * size].T
        high, low = outs[2 * k:2 * k + 2]
        for i in range(2):
            turned, norms = groups[2 * i:2 * i + 2]
            at = slice(i * span, (i + 1) * span)
            mask = nn(hot, all_links[kind, :, at], None)
            distance = own + norms[...] - 2.0 * nn(x, turned[...], None)
            value = mask * jnp.exp(distance * scale)
            top = value.astype(BF16)
            high[:, at] = top
            low[:, at] = (value - top.astype(F32)).astype(BF16)
            totals[i] = totals[i] + jnp.sum(value, axis=0, keepdims=True)
    outs[-1][...] = jnp.concatenate(totals, axis=1)


def send_back_kernel(degree, got, start_a, start_b, *refs):
    tiles, (inv_root, own, near, far) = refs[:-4], refs[-4:]
    width, size = own.shape
    other = jnp.concatenate([got[:, size * i:size * (i + 1)] for i in (2, 3, 0, 1)], axis=1)
    scale = lax.rsqrt(degree[...] + other)
    inv_root[...] = scale[:, :size]
    vectors = (jnp.concatenate([start_a[...], start_b[...]], axis=1) * scale).T
    top = vectors.astype(BF16)
    low = (vectors - top.astype(F32)).astype(BF16)
    both = jnp.concatenate([top, low], axis=1)
    pieces = []
    for i in range(len(tiles) // 2):
        piece = nn(tiles[2 * i][...], both, None)
        pieces.append(piece[:, :width] + piece[:, width:] + nn(tiles[2 * i + 1][...], top, None))
    own[...] = pieces[0].T
    near[...] = jnp.concatenate(pieces[1:3], axis=0).T
    far[...] = jnp.concatenate(pieces[3:5], axis=0).T


def apply_kernel(*refs):
    vectors, tiles, (keep, send) = refs[:3], refs[3:-2], refs[-2:]
    width = vectors[0].shape[0]
    half = keep.shape[1]
    total = None
    count = len(tiles) // 2
    strip = jnp.concatenate([v[...] for v in vectors], axis=1)
    top = strip.astype(BF16)
    low = (strip - top.astype(F32)).astype(BF16)
    both = jnp.concatenate([top, low], axis=0)
    at = 0
    for i in range(count):
        high_tile, low_tile = tiles[2 * i][...], tiles[2 * i + 1][...]
        size = high_tile.shape[0]
        piece = nn(both[:, at:at + size], high_tile, None)
        piece = piece[:width] + piece[width:] + nn(top[:, at:at + size], low_tile, None)
        total = piece if total is None else total + piece
        at += size
    size = half // 2
    keep[:, :size], keep[:, size:] = total[:, :size], total[:, half:half + size]
    send[:, :size], send[:, size:] = total[:, size:half], total[:, half + size:]


def fold(upper, lower):
    width = upper.shape[0]
    row = lax.broadcasted_iota(jnp.int32, upper.shape, 0)
    col = lax.broadcasted_iota(jnp.int32, upper.shape, 1)
    both = jnp.where(col >= row, upper, lower)
    flat = jnp.concatenate([both[8 * i:8 * i + 8, :] for i in range(width // 8)], axis=1)
    return flat, jnp.sum(jnp.where(col == row, lower, 0.0), axis=0, keepdims=True)


def unfold(flat, diagonal):
    width = diagonal.shape[1]
    both = jnp.concatenate([flat[:, width * i:width * (i + 1)] for i in range(width // 8)], axis=0)
    turned = both.T
    row = lax.broadcasted_iota(jnp.int32, both.shape, 0)
    col = lax.broadcasted_iota(jnp.int32, both.shape, 1)
    upper = jnp.where(col >= row, both, turned)
    return upper, jnp.where(col < row, both, jnp.where(col == row, diagonal, turned))


def gram_kernel(mine, got, inv_root, start, image, image_next, packed):
    value = inv_root[...] * (mine[...] + got[...])
    image_next[...] = value
    first, begin = image[...], start[...]
    width = first.shape[0]
    half = width // 2
    packed[:8, :], row_a = fold(nt(begin, begin), nt(begin, first))
    packed[8:16, :], row_b = fold(nt(first, first), nt(first, value))
    last = nt(value, value)
    block = jnp.concatenate([last[:half, :], last[half:, half:]], axis=1)
    rows = jnp.concatenate([row_a, row_b, jnp.zeros((6, width), F32)], axis=0)
    packed[16:, :] = jnp.concatenate([block[:8, :], block[8:, :], rows], axis=1)


def spread_kernel(mine, got, copies):
    copies[...] = jnp.broadcast_to((mine[...] + got[...])[None], copies.shape)


def last_kernel(parts, v0, v1, v2, basis, coefficients):
    packed = jnp.sum(parts[...], axis=0)
    width = v0.shape[0]
    half = width // 2
    span = width + half
    rows = packed[16:, 2 * span:2 * span + width]
    m_00, m_01 = unfold(packed[:8, :], rows[0:1, :])
    m_11, m_12 = unfold(packed[8:16, :], rows[1:2, :])
    block = jnp.concatenate([packed[16:, :span], packed[16:, span:2 * span]], axis=0)
    corner = block[:, half:width].T
    m_22 = jnp.concatenate(
        [block[:, :width], jnp.concatenate([corner, block[:, width:]], axis=1)], axis=0
    )
    blank = jnp.zeros((width, LANES - 3 * width), F32)
    gram = jnp.concatenate(
        [
            jnp.concatenate([m_00, m_01, m_11, blank], axis=1),
            jnp.concatenate([m_01, m_11, m_12, blank], axis=1),
            jnp.concatenate([m_11, m_12, m_22, blank], axis=1),
        ],
        axis=0,
    )
    rows = 3 * width
    groups = [gram[8 * i:8 * i + 8, :] for i in range(rows // 8)]
    whole = jnp.concatenate(eliminate(groups), axis=0)[:, :rows]
    row = lax.broadcasted_iota(jnp.int32, (rows, rows), 0)
    col = lax.broadcasted_iota(jnp.int32, (rows, rows), 1)
    upper = jnp.where(col >= row, whole, 0.0)
    pivot = jnp.sum(jnp.where(col == row, whole, 0.0), axis=1, keepdims=True)
    inverse = jnp.where(col < row, whole, jnp.where(col == row, 1.0 / pivot, 0.0))
    basis[...] = nn(inverse, jnp.concatenate([v0[...], v1[...], v2[...]], axis=0))

    def block(value, i, j):
        return value[width * i:width * (i + 1), width * j:width * (j + 1)]

    z_00, z_11 = block(inverse, 0, 0), block(inverse, 1, 1)
    r_01, r_11 = block(upper, 0, 1), block(upper, 1, 1)
    first = nt(jnp.concatenate([r_01, r_11], axis=0), z_00)
    mixed = block(upper, 1, 2) - nn(r_11, tn(z_00, r_01))
    second = nt(jnp.concatenate([mixed, block(upper, 2, 2)], axis=0), z_11)
    coefficients[0] = first[:width]
    coefficients[1] = first[width:]
    coefficients[2] = second[:width]
    coefficients[3] = second[width:]


def routes(n_loop, n_inner):
    def build(loop_of, inner_of):
        pairs = []
        for l in range(n_loop):
            for c in range(n_inner):
                if 0 <= inner_of(c) < n_inner:
                    pairs.append((l * n_inner + c, loop_of(l) * n_inner + inner_of(c)))
        return pairs

    same = lambda v: v
    return {
        "core": build(lambda l: l ^ 1, same),
        "row": build(lambda l: l ^ 2, same),
        "near": build(same, lambda c: c ^ 1),
        "far": build(same, lambda c: c + 1 if c % 2 else c - 1),
        "relay": build(same, lambda c: c - 2 if c % 2 else c + 2),
    }


def steps(snapshots, bins, pairs, start_weights):
    row_count, features = snapshots.shape
    width = start_weights.shape[1]
    n_row = lax.axis_size("row")
    n_loop = n_row * lax.axis_size("core")
    n_inner = lax.axis_size("inner")
    column = lax.axis_index("inner")
    group = lax.axis_index(("row", "core"))
    route = routes(n_loop, n_inner)

    def move(value, name):
        return lax.ppermute(value, ALL, route[name])

    half = row_count // 2
    across = move(snapshots, "row")
    mate = move(snapshots, "core")
    near_a = move(snapshots[:half], "near")
    far_b = move(snapshots[half:], "far")
    near_b = move(snapshots[half:], "near")
    far_a = move(near_a, "relay")
    across_mate = move(across, "core")

    place = jnp.where(jnp.arange(2) == 0, column, group).astype(jnp.int32)
    hots, links = call(
        functools.partial(links_kernel, n_inner),
        [((3, BINS_COL, row_count), F32), ((3, BINS_COL, n_loop * row_count), F32)],
        place, bins.reshape(n_loop * n_inner, row_count), pairs.T,
        scalars=1,
    )

    span = n_loop * row_count
    turn_outs = [((features, span // 2), BF16), ((1, span // 2), F32), ((width, span // 2), F32)]
    turned_a, norms_a, start_a = call(
        turn_kernel, turn_outs, start_weights.T, snapshots, mate
    )
    turned_b, norms_b, start_b = call(turn_kernel, turn_outs, start_weights.T, across, across_mate)
    made = {}
    degree = ()
    for blocks in (
        (((0, 0), snapshots), ((1, 0), near_a)),
        (((2, 0), far_a),),
        (((1, 1), near_b), ((2, 1), far_b)),
    ):
        places = tuple(place for place, rows in blocks)
        outs = [((rows.shape[0], span), BF16) for place, rows in blocks for _ in range(2)]
        *out, total = call(
            functools.partial(tile_kernel, -3.0 / features, places),
            outs + [((1, span), F32)],
            hots, links, turned_a, norms_a, turned_b, norms_b,
            *(rows for place, rows in blocks), *degree,
        )
        degree = (total,)
        made.update((place, out[2 * i:2 * i + 2]) for i, place in enumerate(places))
    (degree,) = degree
    tiles = sum((made[place] for place in sorted(made)), [])

    got = move(degree, "core")
    degree = degree + jnp.concatenate(
        [got[:, row_count * i:row_count * (i + 1)] for i in (1, 0, 3, 2)], axis=1
    )
    block = ((width, row_count), F32)
    inv_root, own, near, far = call(
        send_back_kernel,
        [((1, row_count), F32), block, block, block],
        degree, move(degree, "row"), start_a, start_b, *tiles,
    )
    start = start_a[:, :row_count]
    image_1 = inv_root * (own + move(near, "near") + move(far, "far"))

    scaled = inv_root * image_1
    keep, send = call(
        apply_kernel,
        [((width, span // 2), F32)] * 2,
        scaled, move(scaled, "near"), move(scaled, "far"), *tiles,
    )
    keep = keep + move(send, "core")
    mine, got = keep[:, :row_count], move(keep[:, row_count:], "row")
    image_2, packed = call(
        gram_kernel,
        [((width, row_count), F32), ((24, LANES), F32)],
        mine, got, inv_root, start, image_1,
    )
    (copies,) = call(
        spread_kernel,
        [((n_row * n_inner,) + packed.shape, F32)],
        packed, move(packed, "core"),
    )
    parts = lax.all_to_all(copies, ("row", "inner"), 0, 0)
    basis, coefficients = call(
        last_kernel,
        [((3 * width, row_count), F32), ((4, width, width), F32)],
        parts, start, image_1, image_2,
        final=True,
    )
    return basis.T, coefficients


def solution(mesh):
    n_loop, n_inner = mesh.shape["loop"], mesh.shape["inner"]
    fine = Mesh(mesh.devices.reshape(n_loop // 2, 2, n_inner), ALL)
    in_specs = (P(ALL, None), P(), P(), P())
    out_specs = (P(ALL, None), P())
    return jax.shard_map(steps, mesh=fine, in_specs=in_specs, out_specs=out_specs, check_vma=False)
```

```python
import functools

import jax
import jax.numpy as jnp
from jax import lax
from jax.experimental import pallas as pl
from jax.experimental.pallas import tpu as pltpu
from jax.sharding import Mesh, PartitionSpec as P

BINS_COL = 8
LANES = 128
KERNEL_VMEM = 16 * 2**20
ALL = ("row", "core", "inner")
HI = lax.Precision.HIGHEST
F32 = jnp.float32
BF16 = jnp.bfloat16


def nt(left, right, precision=HI):
    return lax.dot_general(
        left, right, (((1,), (1,)), ((), ())), precision=precision, preferred_element_type=F32
    )


def nn(left, right, precision=HI):
    return lax.dot_general(
        left, right, (((1,), (0,)), ((), ())), precision=precision, preferred_element_type=F32
    )


def tn(left, right):
    return nn(left.T, right)


def call(kernel, outs, *args, final=False, scalars=0):
    result = jax.ShapeDtypeStruct if final else pltpu.VMEM
    vectors = [pltpu.with_memory_space_constraint(a, pltpu.VMEM) for a in args[scalars:]]
    return pl.pallas_call(
        kernel,
        out_shape=[result(shape, kind) for shape, kind in outs],
        in_specs=[pl.BlockSpec(memory_space=pltpu.SMEM)] * scalars
        + [pl.BlockSpec(memory_space=pltpu.VMEM)] * len(vectors),
        compiler_params=pltpu.CompilerParams(vmem_limit_bytes=KERNEL_VMEM),
    )(*args[:scalars], *vectors)


def spread(value):
    return jnp.broadcast_to(value, (8, LANES))


def pivot_rows(row_a, row_b, a, b, d, lane, at):
    row_a = jnp.where(lane == at, 1.0, jnp.where(lane == at + 1, 0.0, row_a))
    row_b = jnp.where(lane == at, 0.0, jnp.where(lane == at + 1, 1.0, row_b))
    inverse = 1.0 / (a * d - b * b)
    a, b, d = a * inverse, b * inverse, d * inverse
    return d * row_a - b * row_b, a * row_b - b * row_a


def eliminate(groups):
    sub = lax.broadcasted_iota(jnp.int32, (8, LANES), 0)
    lane = lax.broadcasted_iota(jnp.int32, (8, LANES), 1)
    g = list(groups)
    for j in range(0, 8 * len(g), 4):
        q, s = divmod(j, 8)
        cols = [[spread(v[:, j + k:j + k + 1]) for v in g[q:]] for k in range(4)]
        rows = [spread(g[q][s + k:s + k + 1, :]) for k in range(4)]
        m = [[spread(cols[k][0][s + i:s + i + 1, :]) for k in range(4)] for i in range(4)]
        first_pair = jnp.logical_or(lane == j, lane == j + 1)
        last_pair = jnp.logical_or(lane == j + 2, lane == j + 3)
        w0, w1 = pivot_rows(rows[0], rows[1], m[0][0], m[0][1], m[1][1], lane, j)
        inverse = 1.0 / (m[0][0] * m[1][1] - m[0][1] * m[0][1])
        u = [
            ((m[1][1] * m[0][k] - m[0][1] * m[1][k]) * inverse,
             (m[0][0] * m[1][k] - m[0][1] * m[0][k]) * inverse)
            for k in (2, 3)
        ]
        third = jnp.where(first_pair, 0.0, rows[2]) - (m[2][0] * w0 + m[2][1] * w1)
        fourth = jnp.where(first_pair, 0.0, rows[3]) - (m[3][0] * w0 + m[3][1] * w1)
        a = m[2][2] - (m[2][0] * u[0][0] + m[2][1] * u[0][1])
        b = m[2][3] - (m[2][0] * u[1][0] + m[2][1] * u[1][1])
        d = m[3][3] - (m[3][0] * u[1][0] + m[3][1] * u[1][1])
        w2, w3 = pivot_rows(third, fourth, a, b, d, lane, j + 2)
        clear_0, clear_1 = jnp.where(last_pair, 0.0, w0), jnp.where(last_pair, 0.0, w1)
        pair = jnp.logical_or(first_pair, last_pair)
        for i in range(len(g) - q):
            c0, c1 = cols[0][i], cols[1][i]
            c2 = cols[2][i] - (c0 * u[0][0] + c1 * u[0][1])
            c3 = cols[3][i] - (c0 * u[1][0] + c1 * u[1][1])
            old = g[q + i]
            new = jnp.where(pair, 0.0, old) - (c0 * clear_0 + c1 * clear_1) - (c2 * w2 + c3 * w3)
            if i == 0:
                new = jnp.where(sub > s + 3, new, old)
                new = jnp.where(sub == s + 2, third, jnp.where(sub == s + 3, fourth, new))
            g[q + i] = new
    odd = sub % 2 == 1
    done = []
    for q, v in enumerate(g):
        row = sub + 8 * q
        above = pltpu.roll(v, 1, 0)
        at = lane == row - 1
        b = jnp.sum(jnp.where(at, v, 0.0), axis=1, keepdims=True)
        a = jnp.sum(jnp.where(at, above, 0.0), axis=1, keepdims=True)
        above = jnp.where(at, 1.0, above)
        split = jnp.where(at, 0.0, v) - (b / jnp.where(odd, a, 1.0)) * above
        v = jnp.where(odd, split, v)
        pivot = jnp.sum(jnp.where(lane == row, v, 0.0), axis=1, keepdims=True)
        done.append(v * lax.rsqrt(pivot))
    return done


def links_kernel(n_inner, place, bins, pairs, hots, links):
    column, group = place[0], place[1]
    odd = column % 2
    step = 2 * odd - 1
    others = (column, column - step, column + step)
    bin_of = lax.broadcasted_iota(jnp.int32, (BINS_COL, 1), 0)

    def hot(values, base):
        return jnp.where(values == bin_of + base, 1.0, 0.0)

    def bins_at(l, c):
        return bins[pl.ds(l * n_inner + c, 1), :]

    rows = jnp.concatenate(
        [hot(bins_at(group ^ r, column), column * BINS_COL) for r in range(4)], axis=1
    )
    left, right = pairs[0:1, :], pairs[1:2, :]
    base = column * BINS_COL
    left_mine, right_mine = hot(left, base), hot(right, base)
    for i, other in enumerate(others):
        base = other * BINS_COL
        count = nt(hot(left, base), right_mine, None) + nt(hot(right, base), left_mine, None)
        linked = jnp.where(count > 0.5, 1.0, 0.0)
        links[i] = nn(linked, rows, None)
        theirs = bins_at(group, jnp.clip(other, 0, n_inner - 1))
        hots[i] = hot(theirs, base)


def turn_kernel(weights, r0, r1, turned, norms, start):
    span = r0.shape[0]
    for i, rows in enumerate((r0, r1)):
        at = slice(i * span, (i + 1) * span)
        value = rows[...].T
        turned[:, at] = value
        wide = value.astype(F32)
        norms[:, at] = jnp.sum(wide * wide, axis=0, keepdims=True)
        start[:, at] = nn(weights[...], value, None)


def tile_kernel(scale, places, hots, all_links, *refs):
    count = len(places)
    groups, others, outs = refs[:4], refs[4:4 + count], refs[-2 * count - 1:]
    degree = refs[4 + count:-2 * count - 1]
    span = groups[0].shape[1]
    totals = [degree[0][:, span * i:span * (i + 1)] if degree else 0.0 for i in range(2)]
    for k, (kind, part) in enumerate(places):
        x = others[k][...]
        wide = x.astype(F32)
        own = jnp.sum(wide * wide, axis=1, keepdims=True)
        size = x.shape[0]
        hot = hots[kind, :, part:part + size].T
        high, low = outs[2 * k:2 * k + 2]
        for i in range(2):
            turned, norms = groups[2 * i:2 * i + 2]
            at = slice(i * span, (i + 1) * span)
            mask = nn(hot, all_links[kind, :, at], None)
            distance = own + norms[...] - 2.0 * nn(x, turned[...], None)
            value = mask * jnp.exp(distance * scale)
            top = value.astype(BF16)
            high[:, at] = top
            low[:, at] = (value - top.astype(F32)).astype(BF16)
            totals[i] = totals[i] + jnp.sum(value, axis=0, keepdims=True)
    outs[-1][...] = jnp.concatenate(totals, axis=1)


def send_back_kernel(degree, got, start_a, start_b, *refs):
    tiles, (inv_root, own, near, far) = refs[:-4], refs[-4:]
    width, size = own.shape
    other = jnp.concatenate([got[:, size * i:size * (i + 1)] for i in (2, 3, 0, 1)], axis=1)
    scale = lax.rsqrt(degree[...] + other)
    inv_root[...] = scale[:, :size]
    vectors = (jnp.concatenate([start_a[...], start_b[...]], axis=1) * scale).T
    top = vectors.astype(BF16)
    low = (vectors - top.astype(F32)).astype(BF16)
    both = jnp.concatenate([top, low], axis=1)
    pieces = []
    for i in range(len(tiles) // 2):
        piece = nn(tiles[2 * i][...], both, None)
        pieces.append(piece[:, :width] + piece[:, width:] + nn(tiles[2 * i + 1][...], top, None))
    own[...] = pieces[0].T
    cut = (len(pieces) + 1) // 2
    near[...] = jnp.concatenate(pieces[1:cut], axis=0).T
    far[...] = jnp.concatenate(pieces[cut:], axis=0).T


def apply_kernel(*refs):
    vectors, tiles, (keep, send) = refs[:3], refs[3:-2], refs[-2:]
    width = vectors[0].shape[0]
    half = keep.shape[1]
    total = None
    count = len(tiles) // 2
    strip = jnp.concatenate([v[...] for v in vectors], axis=1)
    top = strip.astype(BF16)
    low = (strip - top.astype(F32)).astype(BF16)
    both = jnp.concatenate([top, low], axis=0)
    at = 0
    for i in range(count):
        high_tile, low_tile = tiles[2 * i][...], tiles[2 * i + 1][...]
        size = high_tile.shape[0]
        piece = nn(both[:, at:at + size], high_tile, None)
        piece = piece[:width] + piece[width:] + nn(top[:, at:at + size], low_tile, None)
        total = piece if total is None else total + piece
        at += size
    size = half // 2
    keep[:, :size], keep[:, size:] = total[:, :size], total[:, half:half + size]
    send[:, :size], send[:, size:] = total[:, size:half], total[:, half + size:]


def fold(upper, lower):
    width = upper.shape[0]
    row = lax.broadcasted_iota(jnp.int32, upper.shape, 0)
    col = lax.broadcasted_iota(jnp.int32, upper.shape, 1)
    both = jnp.where(col >= row, upper, lower)
    flat = jnp.concatenate([both[8 * i:8 * i + 8, :] for i in range(width // 8)], axis=1)
    return flat, jnp.sum(jnp.where(col == row, lower, 0.0), axis=0, keepdims=True)


def unfold(flat, diagonal):
    width = diagonal.shape[1]
    both = jnp.concatenate([flat[:, width * i:width * (i + 1)] for i in range(width // 8)], axis=0)
    turned = both.T
    row = lax.broadcasted_iota(jnp.int32, both.shape, 0)
    col = lax.broadcasted_iota(jnp.int32, both.shape, 1)
    upper = jnp.where(col >= row, both, turned)
    return upper, jnp.where(col < row, both, jnp.where(col == row, diagonal, turned))


def gram_kernel(mine, got, inv_root, start, image, image_next, packed):
    value = inv_root[...] * (mine[...] + got[...])
    image_next[...] = value
    first, begin = image[...], start[...]
    width = first.shape[0]
    half = width // 2
    packed[:8, :], row_a = fold(nt(begin, begin), nt(begin, first))
    packed[8:16, :], row_b = fold(nt(first, first), nt(first, value))
    last = nt(value, value)
    block = jnp.concatenate([last[:half, :], last[half:, half:]], axis=1)
    rows = jnp.concatenate([row_a, row_b, jnp.zeros((6, width), F32)], axis=0)
    packed[16:, :] = jnp.concatenate([block[:8, :], block[8:, :], rows], axis=1)


def spread_kernel(mine, got, copies):
    copies[...] = jnp.broadcast_to((mine[...] + got[...])[None], copies.shape)


def last_kernel(parts, v0, v1, v2, basis, coefficients):
    packed = jnp.sum(parts[...], axis=0)
    width = v0.shape[0]
    half = width // 2
    span = width + half
    rows = packed[16:, 2 * span:2 * span + width]
    m_00, m_01 = unfold(packed[:8, :], rows[0:1, :])
    m_11, m_12 = unfold(packed[8:16, :], rows[1:2, :])
    block = jnp.concatenate([packed[16:, :span], packed[16:, span:2 * span]], axis=0)
    corner = block[:, half:width].T
    m_22 = jnp.concatenate(
        [block[:, :width], jnp.concatenate([corner, block[:, width:]], axis=1)], axis=0
    )
    blank = jnp.zeros((width, LANES - 3 * width), F32)
    gram = jnp.concatenate(
        [
            jnp.concatenate([m_00, m_01, m_11, blank], axis=1),
            jnp.concatenate([m_01, m_11, m_12, blank], axis=1),
            jnp.concatenate([m_11, m_12, m_22, blank], axis=1),
        ],
        axis=0,
    )
    rows = 3 * width
    groups = [gram[8 * i:8 * i + 8, :] for i in range(rows // 8)]
    whole = jnp.concatenate(eliminate(groups), axis=0)[:, :rows]
    row = lax.broadcasted_iota(jnp.int32, (rows, rows), 0)
    col = lax.broadcasted_iota(jnp.int32, (rows, rows), 1)
    upper = jnp.where(col >= row, whole, 0.0)
    pivot = jnp.sum(jnp.where(col == row, whole, 0.0), axis=1, keepdims=True)
    inverse = jnp.where(col < row, whole, jnp.where(col == row, 1.0 / pivot, 0.0))
    basis[...] = nn(inverse, jnp.concatenate([v0[...], v1[...], v2[...]], axis=0))

    def block(value, i, j):
        return value[width * i:width * (i + 1), width * j:width * (j + 1)]

    z_00, z_11 = block(inverse, 0, 0), block(inverse, 1, 1)
    r_01, r_11 = block(upper, 0, 1), block(upper, 1, 1)
    first = nt(jnp.concatenate([r_01, r_11], axis=0), z_00)
    mixed = block(upper, 1, 2) - nn(r_11, tn(z_00, r_01))
    second = nt(jnp.concatenate([mixed, block(upper, 2, 2)], axis=0), z_11)
    coefficients[0] = first[:width]
    coefficients[1] = first[width:]
    coefficients[2] = second[:width]
    coefficients[3] = second[width:]


def routes(n_loop, n_inner):
    def build(target):
        pairs = []
        for l in range(n_loop):
            for c in range(n_inner):
                m, d = target(l, c)
                if 0 <= d < n_inner:
                    pairs.append((l * n_inner + c, m * n_inner + d))
        return pairs

    def far(l, c):
        d = c + 1 if c % 2 else c - 1
        return (l, d) if 0 <= d < n_inner else (l ^ 1, c)

    return {
        "core": build(lambda l, c: (l ^ 1, c)),
        "row": build(lambda l, c: (l ^ 2, c)),
        "near": build(lambda l, c: (l, c ^ 1)),
        "far": build(far),
        "relay": build(lambda l, c: (l, c - 2 if c % 2 else c + 2)),
    }


def steps(snapshots, bins, pairs, start_weights):
    row_count, features = snapshots.shape
    width = start_weights.shape[1]
    n_row = lax.axis_size("row")
    n_loop = n_row * lax.axis_size("core")
    n_inner = lax.axis_size("inner")
    column = lax.axis_index("inner")
    group = lax.axis_index(("row", "core"))
    route = routes(n_loop, n_inner)

    def move(value, name):
        return lax.ppermute(value, ALL, route[name])

    half = row_count // 2
    across = move(snapshots, "row")
    near_a = move(snapshots[:half], "near")
    mate = move(snapshots, "core")
    far_b = move(snapshots[half:], "far")
    near_b = move(snapshots[half:], "near")
    far_a = move(near_a, "relay")
    across_mate = move(across, "core")

    place = jnp.where(jnp.arange(2) == 0, column, group).astype(jnp.int32)
    hots, links = call(
        functools.partial(links_kernel, n_inner),
        [((3, BINS_COL, row_count), F32), ((3, BINS_COL, n_loop * row_count), F32)],
        place, bins.reshape(n_loop * n_inner, row_count), pairs.T,
        scalars=1,
    )

    span = n_loop * row_count
    turn_outs = [((features, span // 2), BF16), ((1, span // 2), F32), ((width, span // 2), F32)]
    turned_a, norms_a, start_a = call(
        turn_kernel, turn_outs, start_weights.T, snapshots, mate
    )
    turned_b, norms_b, start_b = call(turn_kernel, turn_outs, start_weights.T, across, across_mate)
    made = {}
    degree = ()
    for blocks in (
        (((0, 0), snapshots), ((1, 0), near_a)),
        (((2, 0), far_a),),
        (((1, half), near_b), ((2, half), far_b)),
    ):
        places = tuple(place for place, rows in blocks)
        outs = [((rows.shape[0], span), BF16) for place, rows in blocks for _ in range(2)]
        *out, total = call(
            functools.partial(tile_kernel, -3.0 / features, places),
            outs + [((1, span), F32)],
            hots, links, turned_a, norms_a, turned_b, norms_b,
            *(rows for place, rows in blocks), *degree,
        )
        degree = (total,)
        made.update((place, out[2 * i:2 * i + 2]) for i, place in enumerate(places))
    (degree,) = degree
    tiles = sum((made[place] for place in sorted(made)), [])

    got = move(degree, "core")
    degree = degree + jnp.concatenate(
        [got[:, row_count * i:row_count * (i + 1)] for i in (1, 0, 3, 2)], axis=1
    )
    block = ((width, row_count), F32)
    inv_root, own, near, far = call(
        send_back_kernel,
        [((1, row_count), F32), block, block, block],
        degree, move(degree, "row"), start_a, start_b, *tiles,
    )
    start = start_a[:, :row_count]
    near = move(near, "near")
    far = move(far, "far")
    image_1 = inv_root * (own + near + far)

    scaled = inv_root * image_1
    near = move(scaled, "near")
    far = move(scaled, "far")
    keep, send = call(
        apply_kernel,
        [((width, span // 2), F32)] * 2,
        scaled, near, far, *tiles,
    )
    keep = keep + move(send, "core")
    mine, got = keep[:, :row_count], move(keep[:, row_count:], "row")
    image_2, packed = call(
        gram_kernel,
        [((width, row_count), F32), ((24, LANES), F32)],
        mine, got, inv_root, start, image_1,
    )
    (copies,) = call(
        spread_kernel,
        [((n_row * n_inner,) + packed.shape, F32)],
        packed, move(packed, "core"),
    )
    parts = lax.all_to_all(copies, ("row", "inner"), 0, 0)
    basis, coefficients = call(
        last_kernel,
        [((3 * width, row_count), F32), ((4, width, width), F32)],
        parts, start, image_1, image_2,
        final=True,
    )
    return basis.T, coefficients


def solution(mesh):
    n_loop, n_inner = mesh.shape["loop"], mesh.shape["inner"]
    fine = Mesh(mesh.devices.reshape(n_loop // 2, 2, n_inner), ALL)
    in_specs = (P(ALL, None), P(), P(), P())
    out_specs = (P(ALL, None), P())
    return jax.shard_map(steps, mesh=fine, in_specs=in_specs, out_specs=out_specs, check_vma=False)
```

```python
import functools

import jax
import jax.numpy as jnp
from jax import lax
from jax.experimental import pallas as pl
from jax.experimental.pallas import tpu as pltpu
from jax.sharding import Mesh, PartitionSpec as P

BINS_COL = 8
LANES = 128
KERNEL_VMEM = 16 * 2**20
ALL = ("row", "core", "inner")
HI = lax.Precision.HIGHEST
F32 = jnp.float32
BF16 = jnp.bfloat16


def nt(left, right, precision=HI):
    return lax.dot_general(
        left, right, (((1,), (1,)), ((), ())), precision=precision, preferred_element_type=F32
    )


def nn(left, right, precision=HI):
    return lax.dot_general(
        left, right, (((1,), (0,)), ((), ())), precision=precision, preferred_element_type=F32
    )


def tn(left, right):
    return nn(left.T, right)


def call(kernel, outs, *args, final=False, scalars=0):
    result = jax.ShapeDtypeStruct if final else pltpu.VMEM
    vectors = [pltpu.with_memory_space_constraint(a, pltpu.VMEM) for a in args[scalars:]]
    return pl.pallas_call(
        kernel,
        out_shape=[result(shape, kind) for shape, kind in outs],
        in_specs=[pl.BlockSpec(memory_space=pltpu.SMEM)] * scalars
        + [pl.BlockSpec(memory_space=pltpu.VMEM)] * len(vectors),
        compiler_params=pltpu.CompilerParams(vmem_limit_bytes=KERNEL_VMEM),
    )(*args[:scalars], *vectors)


def spread(value):
    return jnp.broadcast_to(value, (8, LANES))


def eliminate(groups):
    sub = lax.broadcasted_iota(jnp.int32, (8, LANES), 0)
    lane = lax.broadcasted_iota(jnp.int32, (8, LANES), 1)
    g = list(groups)
    count = 8 * len(g)

    def lane_of(value, j):
        return spread(value[:, j:j + 1])

    def row_of(value, s):
        return spread(value[s:s + 1, :])

    p = {}
    for k in range(4):
        col = lane_of(g[0], k)
        for i in range(k + 1):
            p[i, k] = row_of(col, i)
    for j in range(0, count, 4):
        q, s = divmod(j, 8)
        cols = [[lane_of(v, j + k) for v in g[q:]] for k in range(4)]
        rows = [row_of(g[q], s + k) for k in range(4)]
        first_pair = jnp.logical_or(lane == j, lane == j + 1)
        last_pair = jnp.logical_or(lane == j + 2, lane == j + 3)
        pair = jnp.logical_or(first_pair, last_pair)

        inverse = 1.0 / (p[0, 0] * p[1, 1] - p[0, 1] * p[0, 1])
        d0, b0, a0 = p[1, 1] * inverse, p[0, 1] * inverse, p[0, 0] * inverse

        def first_two(x, y):
            return d0 * x - b0 * y, a0 * y - b0 * x

        u2, u3 = first_two(p[0, 2], p[1, 2]), first_two(p[0, 3], p[1, 3])
        a = p[2, 2] - (p[0, 2] * u2[0] + p[1, 2] * u2[1])
        b = p[2, 3] - (p[0, 2] * u3[0] + p[1, 2] * u3[1])
        d = p[3, 3] - (p[0, 3] * u3[0] + p[1, 3] * u3[1])
        inverse = 1.0 / (a * d - b * b)
        d1, b1, a1 = d * inverse, b * inverse, a * inverse

        def last_two(x, y):
            return d1 * x - b1 * y, a1 * y - b1 * x

        n = j + 4
        if n < count:
            r, t = divmod(n, 8)
            c = [[row_of(cols[k][r - q], t + i) for i in range(4)] for k in range(4)]
            w01 = [first_two(c[0][i], c[1][i]) for i in range(4)]
            c2 = [c[2][i] - (c[0][i] * u2[0] + c[1][i] * u2[1]) for i in range(4)]
            c3 = [c[3][i] - (c[0][i] * u3[0] + c[1][i] * u3[1]) for i in range(4)]
            w23 = [last_two(c2[i], c3[i]) for i in range(4)]
            p = {}
            for k in range(4):
                col = lane_of(g[r], n + k)
                for i in range(k + 1):
                    p[i, k] = row_of(col, t + i) - (
                        (c[0][i] * w01[k][0] + c[1][i] * w01[k][1])
                        + (c2[i] * w23[k][0] + c3[i] * w23[k][1])
                    )

        one = jnp.where(lane == j, 1.0, jnp.where(lane == j + 1, 0.0, rows[0]))
        two = jnp.where(lane == j, 0.0, jnp.where(lane == j + 1, 1.0, rows[1]))
        w0, w1 = first_two(one, two)
        third = jnp.where(first_pair, 0.0, rows[2]) - (u2[0] * one + u2[1] * two)
        fourth = jnp.where(first_pair, 0.0, rows[3]) - (u3[0] * one + u3[1] * two)
        three = jnp.where(lane == j + 2, 1.0, jnp.where(lane == j + 3, 0.0, third))
        four = jnp.where(lane == j + 2, 0.0, jnp.where(lane == j + 3, 1.0, fourth))
        w2, w3 = last_two(three, four)
        clear_0, clear_1 = jnp.where(last_pair, 0.0, w0), jnp.where(last_pair, 0.0, w1)
        for i in range(len(g) - q):
            k0, k1 = cols[0][i], cols[1][i]
            k2 = cols[2][i] - (k0 * u2[0] + k1 * u2[1])
            k3 = cols[3][i] - (k0 * u3[0] + k1 * u3[1])
            old = g[q + i]
            new = jnp.where(pair, 0.0, old) - ((k0 * clear_0 + k1 * clear_1) + (k2 * w2 + k3 * w3))
            if i == 0:
                new = jnp.where(sub > s + 3, new, old)
                new = jnp.where(sub == s + 2, third, jnp.where(sub == s + 3, fourth, new))
            g[q + i] = new
    odd = sub % 2 == 1
    done = []
    for q, v in enumerate(g):
        row = sub + 8 * q
        above = pltpu.roll(v, 1, 0)
        at = lane == row - 1
        b = jnp.sum(jnp.where(at, v, 0.0), axis=1, keepdims=True)
        a = jnp.sum(jnp.where(at, above, 0.0), axis=1, keepdims=True)
        above = jnp.where(at, 1.0, above)
        split = jnp.where(at, 0.0, v) - (b / jnp.where(odd, a, 1.0)) * above
        v = jnp.where(odd, split, v)
        pivot = jnp.sum(jnp.where(lane == row, v, 0.0), axis=1, keepdims=True)
        done.append(v * lax.rsqrt(pivot))
    return done


def links_kernel(n_inner, place, bins, pairs, hots, links):
    column, group = place[0], place[1]
    odd = column % 2
    step = 2 * odd - 1
    others = (column, column - step, column + step)
    bin_of = lax.broadcasted_iota(jnp.int32, (BINS_COL, 1), 0)

    def hot(values, base):
        return jnp.where(values == bin_of + base, 1.0, 0.0)

    def bins_at(l, c):
        return bins[pl.ds(l * n_inner + c, 1), :]

    rows = jnp.concatenate(
        [hot(bins_at(group ^ r, column), column * BINS_COL) for r in range(4)], axis=1
    )
    left, right = pairs[0:1, :], pairs[1:2, :]
    base = column * BINS_COL
    left_mine, right_mine = hot(left, base), hot(right, base)
    for i, other in enumerate(others):
        base = other * BINS_COL
        count = nt(hot(left, base), right_mine, None) + nt(hot(right, base), left_mine, None)
        linked = jnp.where(count > 0.5, 1.0, 0.0)
        links[i] = nn(linked, rows, None)
        theirs = bins_at(group, jnp.clip(other, 0, n_inner - 1))
        hots[i] = hot(theirs, base)


def turn_kernel(weights, r0, r1, turned, norms, start):
    span = r0.shape[0]
    for i, rows in enumerate((r0, r1)):
        at = slice(i * span, (i + 1) * span)
        value = rows[...].T
        turned[:, at] = value
        wide = value.astype(F32)
        norms[:, at] = jnp.sum(wide * wide, axis=0, keepdims=True)
        start[:, at] = nn(weights[...], value, None)


def tile_kernel(scale, places, hots, all_links, *refs):
    count = len(places)
    groups, others, outs = refs[:4], refs[4:4 + count], refs[-2 * count - 1:]
    degree = refs[4 + count:-2 * count - 1]
    span = groups[0].shape[1]
    totals = [degree[0][:, span * i:span * (i + 1)] if degree else 0.0 for i in range(2)]
    for k, (kind, part) in enumerate(places):
        x = others[k][...]
        wide = x.astype(F32)
        own = jnp.sum(wide * wide, axis=1, keepdims=True)
        size = x.shape[0]
        hot = hots[kind, :, part:part + size].T
        high, low = outs[2 * k:2 * k + 2]
        for i in range(2):
            turned, norms = groups[2 * i:2 * i + 2]
            at = slice(i * span, (i + 1) * span)
            mask = nn(hot, all_links[kind, :, at], None)
            distance = own + norms[...] - 2.0 * nn(x, turned[...], None)
            value = mask * jnp.exp(distance * scale)
            top = value.astype(BF16)
            high[:, at] = top
            low[:, at] = (value - top.astype(F32)).astype(BF16)
            totals[i] = totals[i] + jnp.sum(value, axis=0, keepdims=True)
    outs[-1][...] = jnp.concatenate(totals, axis=1)


def send_back_kernel(degree, got, start_a, start_b, *refs):
    tiles, (inv_root, own, near, far) = refs[:-4], refs[-4:]
    width, size = own.shape
    other = jnp.concatenate([got[:, size * i:size * (i + 1)] for i in (2, 3, 0, 1)], axis=1)
    scale = lax.rsqrt(degree[...] + other)
    inv_root[...] = scale[:, :size]
    vectors = (jnp.concatenate([start_a[...], start_b[...]], axis=1) * scale).T
    top = vectors.astype(BF16)
    low = (vectors - top.astype(F32)).astype(BF16)
    both = jnp.concatenate([top, low], axis=1)
    pieces = []
    for i in range(len(tiles) // 2):
        piece = nn(tiles[2 * i][...], both, None)
        pieces.append(piece[:, :width] + piece[:, width:] + nn(tiles[2 * i + 1][...], top, None))
    own[...] = pieces[0].T
    cut = (len(pieces) + 1) // 2
    near[...] = jnp.concatenate(pieces[1:cut], axis=0).T
    far[...] = jnp.concatenate(pieces[cut:], axis=0).T


def apply_kernel(*refs):
    vectors, tiles, (keep, send) = refs[:3], refs[3:-2], refs[-2:]
    width = vectors[0].shape[0]
    half = keep.shape[1]
    total = None
    count = len(tiles) // 2
    strip = jnp.concatenate([v[...] for v in vectors], axis=1)
    top = strip.astype(BF16)
    low = (strip - top.astype(F32)).astype(BF16)
    both = jnp.concatenate([top, low], axis=0)
    at = 0
    for i in range(count):
        high_tile, low_tile = tiles[2 * i][...], tiles[2 * i + 1][...]
        size = high_tile.shape[0]
        piece = nn(both[:, at:at + size], high_tile, None)
        piece = piece[:width] + piece[width:] + nn(top[:, at:at + size], low_tile, None)
        total = piece if total is None else total + piece
        at += size
    size = half // 2
    keep[:, :size], keep[:, size:] = total[:, :size], total[:, half:half + size]
    send[:, :size], send[:, size:] = total[:, size:half], total[:, half + size:]


def fold(upper, lower):
    width = upper.shape[0]
    row = lax.broadcasted_iota(jnp.int32, upper.shape, 0)
    col = lax.broadcasted_iota(jnp.int32, upper.shape, 1)
    both = jnp.where(col >= row, upper, lower)
    flat = jnp.concatenate([both[8 * i:8 * i + 8, :] for i in range(width // 8)], axis=1)
    return flat, jnp.sum(jnp.where(col == row, lower, 0.0), axis=0, keepdims=True)


def unfold(flat, diagonal):
    width = diagonal.shape[1]
    both = jnp.concatenate([flat[:, width * i:width * (i + 1)] for i in range(width // 8)], axis=0)
    turned = both.T
    row = lax.broadcasted_iota(jnp.int32, both.shape, 0)
    col = lax.broadcasted_iota(jnp.int32, both.shape, 1)
    upper = jnp.where(col >= row, both, turned)
    return upper, jnp.where(col < row, both, jnp.where(col == row, diagonal, turned))


def gram_kernel(mine, got, inv_root, start, image, image_next, packed):
    value = inv_root[...] * (mine[...] + got[...])
    image_next[...] = value
    first, begin = image[...], start[...]
    width = first.shape[0]
    half = width // 2
    packed[:8, :], row_a = fold(nt(begin, begin), nt(begin, first))
    packed[8:16, :], row_b = fold(nt(first, first), nt(first, value))
    last = nt(value, value)
    block = jnp.concatenate([last[:half, :], last[half:, half:]], axis=1)
    rows = jnp.concatenate([row_a, row_b, jnp.zeros((6, width), F32)], axis=0)
    packed[16:, :] = jnp.concatenate([block[:8, :], block[8:, :], rows], axis=1)


def spread_kernel(mine, got, copies):
    copies[...] = jnp.broadcast_to((mine[...] + got[...])[None], copies.shape)


def last_kernel(parts, v0, v1, v2, basis, coefficients):
    packed = jnp.sum(parts[...], axis=0)
    width = v0.shape[0]
    half = width // 2
    span = width + half
    rows = packed[16:, 2 * span:2 * span + width]
    m_00, m_01 = unfold(packed[:8, :], rows[0:1, :])
    m_11, m_12 = unfold(packed[8:16, :], rows[1:2, :])
    block = jnp.concatenate([packed[16:, :span], packed[16:, span:2 * span]], axis=0)
    corner = block[:, half:width].T
    m_22 = jnp.concatenate(
        [block[:, :width], jnp.concatenate([corner, block[:, width:]], axis=1)], axis=0
    )
    blank = jnp.zeros((width, LANES - 3 * width), F32)
    gram = jnp.concatenate(
        [
            jnp.concatenate([m_00, m_01, m_11, blank], axis=1),
            jnp.concatenate([m_01, m_11, m_12, blank], axis=1),
            jnp.concatenate([m_11, m_12, m_22, blank], axis=1),
        ],
        axis=0,
    )
    rows = 3 * width
    groups = [gram[8 * i:8 * i + 8, :] for i in range(rows // 8)]
    whole = jnp.concatenate(eliminate(groups), axis=0)[:, :rows]
    row = lax.broadcasted_iota(jnp.int32, (rows, rows), 0)
    col = lax.broadcasted_iota(jnp.int32, (rows, rows), 1)
    upper = jnp.where(col >= row, whole, 0.0)
    pivot = jnp.sum(jnp.where(col == row, whole, 0.0), axis=1, keepdims=True)
    inverse = jnp.where(col < row, whole, jnp.where(col == row, 1.0 / pivot, 0.0))
    basis[...] = nn(inverse, jnp.concatenate([v0[...], v1[...], v2[...]], axis=0))

    def block(value, i, j):
        return value[width * i:width * (i + 1), width * j:width * (j + 1)]

    z_00, z_11 = block(inverse, 0, 0), block(inverse, 1, 1)
    r_01, r_11 = block(upper, 0, 1), block(upper, 1, 1)
    first = nt(jnp.concatenate([r_01, r_11], axis=0), z_00)
    mixed = block(upper, 1, 2) - nn(r_11, tn(z_00, r_01))
    second = nt(jnp.concatenate([mixed, block(upper, 2, 2)], axis=0), z_11)
    coefficients[0] = first[:width]
    coefficients[1] = first[width:]
    coefficients[2] = second[:width]
    coefficients[3] = second[width:]


def routes(n_loop, n_inner):
    def build(target):
        pairs = []
        for l in range(n_loop):
            for c in range(n_inner):
                m, d = target(l, c)
                if 0 <= d < n_inner:
                    pairs.append((l * n_inner + c, m * n_inner + d))
        return pairs

    def far(l, c):
        d = c + 1 if c % 2 else c - 1
        return (l, d) if 0 <= d < n_inner else (l ^ 1, c)

    return {
        "core": build(lambda l, c: (l ^ 1, c)),
        "row": build(lambda l, c: (l ^ 2, c)),
        "near": build(lambda l, c: (l, c ^ 1)),
        "far": build(far),
        "relay": build(lambda l, c: (l, c - 2 if c % 2 else c + 2)),
    }


def steps(snapshots, bins, pairs, start_weights):
    row_count, features = snapshots.shape
    width = start_weights.shape[1]
    n_row = lax.axis_size("row")
    n_loop = n_row * lax.axis_size("core")
    n_inner = lax.axis_size("inner")
    column = lax.axis_index("inner")
    group = lax.axis_index(("row", "core"))
    route = routes(n_loop, n_inner)

    def move(value, name):
        return lax.ppermute(value, ALL, route[name])

    half = row_count // 2
    across = move(snapshots, "row")
    near_a = move(snapshots[:half], "near")
    mate = move(snapshots, "core")
    far_b = move(snapshots[half:], "far")
    near_b = move(snapshots[half:], "near")
    far_a = move(near_a, "relay")
    across_mate = move(across, "core")

    place = jnp.where(jnp.arange(2) == 0, column, group).astype(jnp.int32)
    hots, links = call(
        functools.partial(links_kernel, n_inner),
        [((3, BINS_COL, row_count), F32), ((3, BINS_COL, n_loop * row_count), F32)],
        place, bins.reshape(n_loop * n_inner, row_count), pairs.T,
        scalars=1,
    )

    span = n_loop * row_count
    turn_outs = [((features, span // 2), BF16), ((1, span // 2), F32), ((width, span // 2), F32)]
    turned_a, norms_a, start_a = call(
        turn_kernel, turn_outs, start_weights.T, snapshots, mate
    )
    turned_b, norms_b, start_b = call(turn_kernel, turn_outs, start_weights.T, across, across_mate)
    made = {}
    degree = ()
    for blocks in (
        (((0, 0), snapshots), ((1, 0), near_a)),
        (((2, 0), far_a),),
        (((1, half), near_b), ((2, half), far_b)),
    ):
        places = tuple(place for place, rows in blocks)
        outs = [((rows.shape[0], span), BF16) for place, rows in blocks for _ in range(2)]
        *out, total = call(
            functools.partial(tile_kernel, -3.0 / features, places),
            outs + [((1, span), F32)],
            hots, links, turned_a, norms_a, turned_b, norms_b,
            *(rows for place, rows in blocks), *degree,
        )
        degree = (total,)
        made.update((place, out[2 * i:2 * i + 2]) for i, place in enumerate(places))
    (degree,) = degree
    tiles = sum((made[place] for place in sorted(made)), [])

    got = move(degree, "core")
    degree = degree + jnp.concatenate(
        [got[:, row_count * i:row_count * (i + 1)] for i in (1, 0, 3, 2)], axis=1
    )
    block = ((width, row_count), F32)
    inv_root, own, near, far = call(
        send_back_kernel,
        [((1, row_count), F32), block, block, block],
        degree, move(degree, "row"), start_a, start_b, *tiles,
    )
    start = start_a[:, :row_count]
    near = move(near, "near")
    far = move(far, "far")
    image_1 = inv_root * (own + near + far)

    scaled = inv_root * image_1
    near = move(scaled, "near")
    far = move(scaled, "far")
    keep, send = call(
        apply_kernel,
        [((width, span // 2), F32)] * 2,
        scaled, near, far, *tiles,
    )
    keep = keep + move(send, "core")
    mine, got = keep[:, :row_count], move(keep[:, row_count:], "row")
    image_2, packed = call(
        gram_kernel,
        [((width, row_count), F32), ((24, LANES), F32)],
        mine, got, inv_root, start, image_1,
    )
    (copies,) = call(
        spread_kernel,
        [((n_row * n_inner,) + packed.shape, F32)],
        packed, move(packed, "core"),
    )
    parts = lax.all_to_all(copies, ("row", "inner"), 0, 0)
    basis, coefficients = call(
        last_kernel,
        [((3 * width, row_count), F32), ((4, width, width), F32)],
        parts, start, image_1, image_2,
        final=True,
    )
    return basis.T, coefficients


def solution(mesh):
    n_loop, n_inner = mesh.shape["loop"], mesh.shape["inner"]
    fine = Mesh(mesh.devices.reshape(n_loop // 2, 2, n_inner), ALL)
    in_specs = (P(ALL, None), P(), P(), P())
    out_specs = (P(ALL, None), P())
    return jax.shard_map(steps, mesh=fine, in_specs=in_specs, out_specs=out_specs, check_vma=False)
```

```python
import functools

import jax
import jax.numpy as jnp
from jax import lax
from jax.experimental import pallas as pl
from jax.experimental.pallas import tpu as pltpu
from jax.sharding import Mesh, PartitionSpec as P

BINS_COL = 8
LANES = 128
KERNEL_VMEM = 16 * 2**20
ALL = ("row", "core", "inner")
HI = lax.Precision.HIGHEST
F32 = jnp.float32
BF16 = jnp.bfloat16


def nt(left, right, precision=HI):
    return lax.dot_general(
        left, right, (((1,), (1,)), ((), ())), precision=precision, preferred_element_type=F32
    )


def nn(left, right, precision=HI):
    return lax.dot_general(
        left, right, (((1,), (0,)), ((), ())), precision=precision, preferred_element_type=F32
    )


def tn(left, right):
    return nn(left.T, right)


def call(kernel, outs, *args, final=False, scalars=0):
    result = jax.ShapeDtypeStruct if final else pltpu.VMEM
    vectors = [pltpu.with_memory_space_constraint(a, pltpu.VMEM) for a in args[scalars:]]
    return pl.pallas_call(
        kernel,
        out_shape=[result(shape, kind) for shape, kind in outs],
        in_specs=[pl.BlockSpec(memory_space=pltpu.SMEM)] * scalars
        + [pl.BlockSpec(memory_space=pltpu.VMEM)] * len(vectors),
        compiler_params=pltpu.CompilerParams(vmem_limit_bytes=KERNEL_VMEM),
    )(*args[:scalars], *vectors)


def spread(value):
    return jnp.broadcast_to(value, (8, LANES))


def eliminate(groups):
    sub = lax.broadcasted_iota(jnp.int32, (8, LANES), 0)
    lane = lax.broadcasted_iota(jnp.int32, (8, LANES), 1)
    g = list(groups)
    count = 8 * len(g)

    def lane_of(value, j):
        return spread(value[:, j:j + 1])

    def row_of(value, s):
        return spread(value[s:s + 1, :])

    p = {}
    for k in range(4):
        col = lane_of(g[0], k)
        for i in range(k + 1):
            p[i, k] = row_of(col, i)
    for j in range(0, count, 4):
        q, s = divmod(j, 8)
        cols = [[lane_of(v, j + k) for v in g[q:]] for k in range(4)]
        rows = [row_of(g[q], s + k) for k in range(4)]
        first_pair = jnp.logical_or(lane == j, lane == j + 1)
        last_pair = jnp.logical_or(lane == j + 2, lane == j + 3)
        pair = jnp.logical_or(first_pair, last_pair)

        inverse = 1.0 / (p[0, 0] * p[1, 1] - p[0, 1] * p[0, 1])
        d0, b0, a0 = p[1, 1] * inverse, p[0, 1] * inverse, p[0, 0] * inverse

        def first_two(x, y):
            return d0 * x - b0 * y, a0 * y - b0 * x

        u2, u3 = first_two(p[0, 2], p[1, 2]), first_two(p[0, 3], p[1, 3])
        a = p[2, 2] - (p[0, 2] * u2[0] + p[1, 2] * u2[1])
        b = p[2, 3] - (p[0, 2] * u3[0] + p[1, 2] * u3[1])
        d = p[3, 3] - (p[0, 3] * u3[0] + p[1, 3] * u3[1])
        inverse = 1.0 / (a * d - b * b)
        d1, b1, a1 = d * inverse, b * inverse, a * inverse

        def last_two(x, y):
            return d1 * x - b1 * y, a1 * y - b1 * x

        n = j + 4
        if n < count:
            r, t = divmod(n, 8)
            c = [[row_of(cols[k][r - q], t + i) for i in range(4)] for k in range(4)]
            w01 = [first_two(c[0][i], c[1][i]) for i in range(4)]
            c2 = [c[2][i] - (c[0][i] * u2[0] + c[1][i] * u2[1]) for i in range(4)]
            c3 = [c[3][i] - (c[0][i] * u3[0] + c[1][i] * u3[1]) for i in range(4)]
            w23 = [last_two(c2[i], c3[i]) for i in range(4)]
            p = {}
            for k in range(4):
                col = lane_of(g[r], n + k)
                for i in range(k + 1):
                    p[i, k] = row_of(col, t + i) - (
                        (c[0][i] * w01[k][0] + c[1][i] * w01[k][1])
                        + (c2[i] * w23[k][0] + c3[i] * w23[k][1])
                    )

        one = jnp.where(lane == j, 1.0, jnp.where(lane == j + 1, 0.0, rows[0]))
        two = jnp.where(lane == j, 0.0, jnp.where(lane == j + 1, 1.0, rows[1]))
        w0, w1 = first_two(one, two)
        third = jnp.where(first_pair, 0.0, rows[2]) - (u2[0] * one + u2[1] * two)
        fourth = jnp.where(first_pair, 0.0, rows[3]) - (u3[0] * one + u3[1] * two)
        three = jnp.where(lane == j + 2, 1.0, jnp.where(lane == j + 3, 0.0, third))
        four = jnp.where(lane == j + 2, 0.0, jnp.where(lane == j + 3, 1.0, fourth))
        w2, w3 = last_two(three, four)
        clear_0, clear_1 = jnp.where(last_pair, 0.0, w0), jnp.where(last_pair, 0.0, w1)
        for i in range(len(g) - q):
            k0, k1 = cols[0][i], cols[1][i]
            k2 = cols[2][i] - (k0 * u2[0] + k1 * u2[1])
            k3 = cols[3][i] - (k0 * u3[0] + k1 * u3[1])
            old = g[q + i]
            new = jnp.where(pair, 0.0, old) - ((k0 * clear_0 + k1 * clear_1) + (k2 * w2 + k3 * w3))
            if i == 0:
                new = jnp.where(sub > s + 3, new, old)
                new = jnp.where(sub == s + 2, third, jnp.where(sub == s + 3, fourth, new))
            g[q + i] = new
    odd = sub % 2 == 1
    done = []
    for q, v in enumerate(g):
        row = sub + 8 * q
        above = pltpu.roll(v, 1, 0)
        at = lane == row - 1
        b = jnp.sum(jnp.where(at, v, 0.0), axis=1, keepdims=True)
        a = jnp.sum(jnp.where(at, above, 0.0), axis=1, keepdims=True)
        above = jnp.where(at, 1.0, above)
        split = jnp.where(at, 0.0, v) - (b / jnp.where(odd, a, 1.0)) * above
        v = jnp.where(odd, split, v)
        pivot = jnp.sum(jnp.where(lane == row, v, 0.0), axis=1, keepdims=True)
        done.append(v * lax.rsqrt(pivot))
    return done


def links_kernel(n_inner, place, bins, pairs, hots, links):
    column, group = place[0], place[1]
    odd = column % 2
    step = 2 * odd - 1
    others = (column, column - step, column + step)
    bin_of = lax.broadcasted_iota(jnp.int32, (BINS_COL, 1), 0)

    def hot(values, base):
        return jnp.where(values == bin_of + base, 1.0, 0.0)

    def bins_at(l, c):
        return bins[pl.ds(l * n_inner + c, 1), :]

    rows = jnp.concatenate(
        [hot(bins_at(group ^ r, column), column * BINS_COL) for r in range(4)], axis=1
    )
    left, right = pairs[0:1, :], pairs[1:2, :]
    base = column * BINS_COL
    left_mine, right_mine = hot(left, base), hot(right, base)
    for i, other in enumerate(others):
        base = other * BINS_COL
        count = nt(hot(left, base), right_mine, None) + nt(hot(right, base), left_mine, None)
        linked = jnp.where(count > 0.5, 1.0, 0.0)
        links[i] = nn(linked, rows, None)
        theirs = bins_at(group, jnp.clip(other, 0, n_inner - 1))
        hots[i] = hot(theirs, base)


def turn_kernel(weights, r0, r1, turned, norms, start):
    span = r0.shape[0]
    for i, rows in enumerate((r0, r1)):
        at = slice(i * span, (i + 1) * span)
        value = rows[...].T
        turned[:, at] = value
        wide = value.astype(F32)
        norms[:, at] = jnp.sum(wide * wide, axis=0, keepdims=True)
        start[:, at] = nn(weights[...], value, None)


def tile_kernel(scale, places, hots, all_links, *refs):
    count = len(places)
    groups, others, outs = refs[:4], refs[4:4 + count], refs[-2 * count - 1:]
    degree = refs[4 + count:-2 * count - 1]
    span = groups[0].shape[1]
    totals = [degree[0][:, span * i:span * (i + 1)] if degree else 0.0 for i in range(2)]
    for k, (kind, part) in enumerate(places):
        x = others[k][...]
        wide = x.astype(F32)
        own = jnp.sum(wide * wide, axis=1, keepdims=True)
        size = x.shape[0]
        hot = hots[kind, :, part:part + size].T
        high, low = outs[2 * k:2 * k + 2]
        for i in range(2):
            turned, norms = groups[2 * i:2 * i + 2]
            at = slice(i * span, (i + 1) * span)
            mask = nn(hot, all_links[kind, :, at], None)
            distance = own + norms[...] - 2.0 * nn(x, turned[...], None)
            value = mask * jnp.exp(distance * scale)
            top = value.astype(BF16)
            high[:, at] = top
            low[:, at] = (value - top.astype(F32)).astype(BF16)
            totals[i] = totals[i] + jnp.sum(value, axis=0, keepdims=True)
    outs[-1][...] = jnp.concatenate(totals, axis=1)


def send_back_kernel(degree, got, start_a, start_b, *refs):
    tiles, (inv_root, own, near, far) = refs[:-4], refs[-4:]
    width, size = own.shape
    other = jnp.concatenate([got[:, size * i:size * (i + 1)] for i in (2, 3, 0, 1)], axis=1)
    scale = lax.rsqrt(degree[...] + other)
    inv_root[...] = scale[:, :size]
    vectors = (jnp.concatenate([start_a[...], start_b[...]], axis=1) * scale)
    top = vectors.astype(BF16)
    low = (vectors - top.astype(F32)).astype(BF16)
    both = jnp.concatenate([top, low], axis=0)
    pieces = []
    for i in range(len(tiles) // 2):
        high = tiles[2 * i][...]
        piece = nt(both, high, None)
        pieces.append(piece[:width] + piece[width:] + nt(top, tiles[2 * i + 1][...], None))
    own[...] = pieces[0]
    cut = (len(pieces) + 1) // 2
    near[...] = jnp.concatenate(pieces[1:cut], axis=1)
    far[...] = jnp.concatenate(pieces[cut:], axis=1)


def apply_kernel(*refs):
    vectors, tiles, (keep, send) = refs[:3], refs[3:-2], refs[-2:]
    width = vectors[0].shape[0]
    half = keep.shape[1]
    total = None
    count = len(tiles) // 2
    strip = jnp.concatenate([v[...] for v in vectors], axis=1)
    top = strip.astype(BF16)
    low = (strip - top.astype(F32)).astype(BF16)
    both = jnp.concatenate([top, low], axis=0)
    at = 0
    for i in range(count):
        high_tile, low_tile = tiles[2 * i][...], tiles[2 * i + 1][...]
        size = high_tile.shape[0]
        piece = nn(both[:, at:at + size], high_tile, None)
        piece = piece[:width] + piece[width:] + nn(top[:, at:at + size], low_tile, None)
        total = piece if total is None else total + piece
        at += size
    size = half // 2
    keep[:, :size], keep[:, size:] = total[:, :size], total[:, half:half + size]
    send[:, :size], send[:, size:] = total[:, size:half], total[:, half + size:]


def fold(upper, lower):
    width = upper.shape[0]
    row = lax.broadcasted_iota(jnp.int32, upper.shape, 0)
    col = lax.broadcasted_iota(jnp.int32, upper.shape, 1)
    both = jnp.where(col >= row, upper, lower)
    flat = jnp.concatenate([both[8 * i:8 * i + 8, :] for i in range(width // 8)], axis=1)
    return flat, jnp.sum(jnp.where(col == row, lower, 0.0), axis=0, keepdims=True)


def unfold(flat, diagonal):
    width = diagonal.shape[1]
    both = jnp.concatenate([flat[:, width * i:width * (i + 1)] for i in range(width // 8)], axis=0)
    turned = both.T
    row = lax.broadcasted_iota(jnp.int32, both.shape, 0)
    col = lax.broadcasted_iota(jnp.int32, both.shape, 1)
    upper = jnp.where(col >= row, both, turned)
    return upper, jnp.where(col < row, both, jnp.where(col == row, diagonal, turned))


def gram_kernel(mine, got, inv_root, start, image, image_next, packed):
    value = inv_root[...] * (mine[...] + got[...])
    image_next[...] = value
    first, begin = image[...], start[...]
    width = first.shape[0]
    half = width // 2
    packed[:8, :], row_a = fold(nt(begin, begin), nt(begin, first))
    packed[8:16, :], row_b = fold(nt(first, first), nt(first, value))
    last = nt(value, value)
    block = jnp.concatenate([last[:half, :], last[half:, half:]], axis=1)
    rows = jnp.concatenate([row_a, row_b, jnp.zeros((6, width), F32)], axis=0)
    packed[16:, :] = jnp.concatenate([block[:8, :], block[8:, :], rows], axis=1)


def spread_kernel(mine, got, copies):
    copies[...] = jnp.broadcast_to((mine[...] + got[...])[None], copies.shape)


def last_kernel(parts, v0, v1, v2, basis, coefficients):
    packed = jnp.sum(parts[...], axis=0)
    width = v0.shape[0]
    half = width // 2
    span = width + half
    rows = packed[16:, 2 * span:2 * span + width]
    m_00, m_01 = unfold(packed[:8, :], rows[0:1, :])
    m_11, m_12 = unfold(packed[8:16, :], rows[1:2, :])
    block = jnp.concatenate([packed[16:, :span], packed[16:, span:2 * span]], axis=0)
    corner = block[:, half:width].T
    m_22 = jnp.concatenate(
        [block[:, :width], jnp.concatenate([corner, block[:, width:]], axis=1)], axis=0
    )
    blank = jnp.zeros((width, LANES - 3 * width), F32)
    gram = jnp.concatenate(
        [
            jnp.concatenate([m_00, m_01, m_11, blank], axis=1),
            jnp.concatenate([m_01, m_11, m_12, blank], axis=1),
            jnp.concatenate([m_11, m_12, m_22, blank], axis=1),
        ],
        axis=0,
    )
    rows = 3 * width
    groups = [gram[8 * i:8 * i + 8, :] for i in range(rows // 8)]
    whole = jnp.concatenate(eliminate(groups), axis=0)[:, :rows]
    row = lax.broadcasted_iota(jnp.int32, (rows, rows), 0)
    col = lax.broadcasted_iota(jnp.int32, (rows, rows), 1)
    upper = jnp.where(col >= row, whole, 0.0)
    pivot = jnp.sum(jnp.where(col == row, whole, 0.0), axis=1, keepdims=True)
    inverse = jnp.where(col < row, whole, jnp.where(col == row, 1.0 / pivot, 0.0))
    basis[...] = nn(inverse, jnp.concatenate([v0[...], v1[...], v2[...]], axis=0))

    def block(value, i, j):
        return value[width * i:width * (i + 1), width * j:width * (j + 1)]

    z_00, z_11 = block(inverse, 0, 0), block(inverse, 1, 1)
    r_01, r_11 = block(upper, 0, 1), block(upper, 1, 1)
    first = nt(jnp.concatenate([r_01, r_11], axis=0), z_00)
    mixed = block(upper, 1, 2) - nn(r_11, tn(z_00, r_01))
    second = nt(jnp.concatenate([mixed, block(upper, 2, 2)], axis=0), z_11)
    coefficients[0] = first[:width]
    coefficients[1] = first[width:]
    coefficients[2] = second[:width]
    coefficients[3] = second[width:]


def routes(n_loop, n_inner):
    def build(target):
        pairs = []
        for l in range(n_loop):
            for c in range(n_inner):
                m, d = target(l, c)
                if 0 <= d < n_inner:
                    pairs.append((l * n_inner + c, m * n_inner + d))
        return pairs

    def far(l, c):
        d = c + 1 if c % 2 else c - 1
        return (l, d) if 0 <= d < n_inner else (l ^ 1, c)

    return {
        "core": build(lambda l, c: (l ^ 1, c)),
        "row": build(lambda l, c: (l ^ 2, c)),
        "near": build(lambda l, c: (l, c ^ 1)),
        "far": build(far),
        "relay": build(lambda l, c: (l, c - 2 if c % 2 else c + 2)),
    }


def steps(snapshots, bins, pairs, start_weights):
    row_count, features = snapshots.shape
    width = start_weights.shape[1]
    n_row = lax.axis_size("row")
    n_loop = n_row * lax.axis_size("core")
    n_inner = lax.axis_size("inner")
    column = lax.axis_index("inner")
    group = lax.axis_index(("row", "core"))
    route = routes(n_loop, n_inner)

    def move(value, name):
        return lax.ppermute(value, ALL, route[name])

    half = row_count // 2
    across = move(snapshots, "row")
    first_half, later = lax.optimization_barrier((snapshots[:half], snapshots))
    near_a = move(first_half, "near")
    mate = move(snapshots, "core")
    far_b = move(later[half:], "far")
    near_b = move(later[half:], "near")
    far_a = move(near_a, "relay")
    across_mate = move(across, "core")

    place = jnp.where(jnp.arange(2) == 0, column, group).astype(jnp.int32)
    hots, links = call(
        functools.partial(links_kernel, n_inner),
        [((3, BINS_COL, row_count), F32), ((3, BINS_COL, n_loop * row_count), F32)],
        place, bins.reshape(n_loop * n_inner, row_count), pairs.T,
        scalars=1,
    )

    span = n_loop * row_count
    turn_outs = [((features, span // 2), BF16), ((1, span // 2), F32), ((width, span // 2), F32)]
    turned_a, norms_a, start_a = call(
        turn_kernel, turn_outs, start_weights.T, snapshots, mate
    )
    turned_b, norms_b, start_b = call(turn_kernel, turn_outs, start_weights.T, across, across_mate)
    made = {}
    degree = ()
    for blocks in (
        (((0, 0), snapshots), ((1, 0), near_a)),
        (((2, 0), far_a),),
        (((1, half), near_b), ((2, half), far_b)),
    ):
        places = tuple(place for place, rows in blocks)
        outs = [((rows.shape[0], span), BF16) for place, rows in blocks for _ in range(2)]
        *out, total = call(
            functools.partial(tile_kernel, -3.0 / features, places),
            outs + [((1, span), F32)],
            hots, links, turned_a, norms_a, turned_b, norms_b,
            *(rows for place, rows in blocks), *degree,
        )
        degree = (total,)
        made.update((place, out[2 * i:2 * i + 2]) for i, place in enumerate(places))
    (degree,) = degree
    tiles = sum((made[place] for place in sorted(made)), [])

    got = move(degree, "core")
    degree = degree + jnp.concatenate(
        [got[:, row_count * i:row_count * (i + 1)] for i in (1, 0, 3, 2)], axis=1
    )
    block = ((width, row_count), F32)
    inv_root, own, near, far = call(
        send_back_kernel,
        [((1, row_count), F32), block, block, block],
        degree, move(degree, "row"), start_a, start_b, *tiles,
    )
    start = start_a[:, :row_count]
    near = move(near, "near")
    far = move(far, "far")
    image_1 = inv_root * (own + near + far)

    scaled = inv_root * image_1
    near = move(scaled, "near")
    far = move(scaled, "far")
    keep, send = call(
        apply_kernel,
        [((width, span // 2), F32)] * 2,
        scaled, near, far, *tiles,
    )
    keep = keep + move(send, "core")
    mine, got = keep[:, :row_count], move(keep[:, row_count:], "row")
    image_2, packed = call(
        gram_kernel,
        [((width, row_count), F32), ((24, LANES), F32)],
        mine, got, inv_root, start, image_1,
    )
    (copies,) = call(
        spread_kernel,
        [((n_row * n_inner,) + packed.shape, F32)],
        packed, move(packed, "core"),
    )
    parts = lax.all_to_all(copies, ("row", "inner"), 0, 0)
    basis, coefficients = call(
        last_kernel,
        [((3 * width, row_count), F32), ((4, width, width), F32)],
        parts, start, image_1, image_2,
        final=True,
    )
    return basis.T, coefficients


def solution(mesh):
    n_loop, n_inner = mesh.shape["loop"], mesh.shape["inner"]
    fine = Mesh(mesh.devices.reshape(n_loop // 2, 2, n_inner), ALL)
    in_specs = (P(ALL, None), P(), P(), P())
    out_specs = (P(ALL, None), P())
    return jax.shard_map(steps, mesh=fine, in_specs=in_specs, out_specs=out_specs, check_vma=False)
```

```python
import functools

import jax
import jax.numpy as jnp
from jax import lax
from jax.experimental import pallas as pl
from jax.experimental.pallas import tpu as pltpu
from jax.sharding import Mesh, PartitionSpec as P

BINS_COL = 8
LANES = 128
KERNEL_VMEM = 16 * 2**20
ALL = ("row", "core", "inner")
HI = lax.Precision.HIGHEST
F32 = jnp.float32
BF16 = jnp.bfloat16


def nt(left, right, precision=HI):
    return lax.dot_general(
        left, right, (((1,), (1,)), ((), ())), precision=precision, preferred_element_type=F32
    )


def nn(left, right, precision=HI):
    return lax.dot_general(
        left, right, (((1,), (0,)), ((), ())), precision=precision, preferred_element_type=F32
    )


def tn(left, right):
    return nn(left.T, right)


def call(kernel, outs, *args, final=False, scalars=0):
    result = jax.ShapeDtypeStruct if final else pltpu.VMEM
    vectors = [pltpu.with_memory_space_constraint(a, pltpu.VMEM) for a in args[scalars:]]
    return pl.pallas_call(
        kernel,
        out_shape=[result(shape, kind) for shape, kind in outs],
        in_specs=[pl.BlockSpec(memory_space=pltpu.SMEM)] * scalars
        + [pl.BlockSpec(memory_space=pltpu.VMEM)] * len(vectors),
        compiler_params=pltpu.CompilerParams(vmem_limit_bytes=KERNEL_VMEM),
    )(*args[:scalars], *vectors)


def spread(value):
    return jnp.broadcast_to(value, (8, LANES))


def eliminate(groups):
    sub = lax.broadcasted_iota(jnp.int32, (8, LANES), 0)
    lane = lax.broadcasted_iota(jnp.int32, (8, LANES), 1)
    g = list(groups)
    count = 8 * len(g)

    def lane_of(value, j):
        return spread(value[:, j:j + 1])

    def row_of(value, s):
        return spread(value[s:s + 1, :])

    p = {}
    for k in range(4):
        col = lane_of(g[0], k)
        for i in range(k + 1):
            p[i, k] = row_of(col, i)
    for j in range(0, count, 4):
        q, s = divmod(j, 8)
        cols = [[lane_of(v, j + k) for v in g[q:]] for k in range(4)]
        rows = [row_of(g[q], s + k) for k in range(4)]
        first_pair = jnp.logical_or(lane == j, lane == j + 1)
        last_pair = jnp.logical_or(lane == j + 2, lane == j + 3)
        pair = jnp.logical_or(first_pair, last_pair)

        inverse = 1.0 / (p[0, 0] * p[1, 1] - p[0, 1] * p[0, 1])
        d0, b0, a0 = p[1, 1] * inverse, p[0, 1] * inverse, p[0, 0] * inverse

        def first_two(x, y):
            return d0 * x - b0 * y, a0 * y - b0 * x

        u2, u3 = first_two(p[0, 2], p[1, 2]), first_two(p[0, 3], p[1, 3])
        a = p[2, 2] - (p[0, 2] * u2[0] + p[1, 2] * u2[1])
        b = p[2, 3] - (p[0, 2] * u3[0] + p[1, 2] * u3[1])
        d = p[3, 3] - (p[0, 3] * u3[0] + p[1, 3] * u3[1])
        inverse = 1.0 / (a * d - b * b)
        d1, b1, a1 = d * inverse, b * inverse, a * inverse

        def last_two(x, y):
            return d1 * x - b1 * y, a1 * y - b1 * x

        n = j + 4
        if n < count:
            r, t = divmod(n, 8)
            c = [[row_of(cols[k][r - q], t + i) for i in range(4)] for k in range(4)]
            w01 = [first_two(c[0][i], c[1][i]) for i in range(4)]
            c2 = [c[2][i] - (c[0][i] * u2[0] + c[1][i] * u2[1]) for i in range(4)]
            c3 = [c[3][i] - (c[0][i] * u3[0] + c[1][i] * u3[1]) for i in range(4)]
            w23 = [last_two(c2[i], c3[i]) for i in range(4)]
            p = {}
            for k in range(4):
                col = lane_of(g[r], n + k)
                for i in range(k + 1):
                    p[i, k] = row_of(col, t + i) - (
                        (c[0][i] * w01[k][0] + c[1][i] * w01[k][1])
                        + (c2[i] * w23[k][0] + c3[i] * w23[k][1])
                    )

        one = jnp.where(lane == j, 1.0, jnp.where(lane == j + 1, 0.0, rows[0]))
        two = jnp.where(lane == j, 0.0, jnp.where(lane == j + 1, 1.0, rows[1]))
        w0, w1 = first_two(one, two)
        third = jnp.where(first_pair, 0.0, rows[2]) - (u2[0] * one + u2[1] * two)
        fourth = jnp.where(first_pair, 0.0, rows[3]) - (u3[0] * one + u3[1] * two)
        three = jnp.where(lane == j + 2, 1.0, jnp.where(lane == j + 3, 0.0, third))
        four = jnp.where(lane == j + 2, 0.0, jnp.where(lane == j + 3, 1.0, fourth))
        w2, w3 = last_two(three, four)
        clear_0, clear_1 = jnp.where(last_pair, 0.0, w0), jnp.where(last_pair, 0.0, w1)
        for i in range(len(g) - q):
            k0, k1 = cols[0][i], cols[1][i]
            k2 = cols[2][i] - (k0 * u2[0] + k1 * u2[1])
            k3 = cols[3][i] - (k0 * u3[0] + k1 * u3[1])
            old = g[q + i]
            new = jnp.where(pair, 0.0, old) - ((k0 * clear_0 + k1 * clear_1) + (k2 * w2 + k3 * w3))
            if i == 0:
                new = jnp.where(sub > s + 3, new, old)
                new = jnp.where(sub == s + 2, third, jnp.where(sub == s + 3, fourth, new))
            g[q + i] = new
    odd = sub % 2 == 1
    done = []
    for q, v in enumerate(g):
        row = sub + 8 * q
        above = pltpu.roll(v, 1, 0)
        at = lane == row - 1
        b = jnp.sum(jnp.where(at, v, 0.0), axis=1, keepdims=True)
        a = jnp.sum(jnp.where(at, above, 0.0), axis=1, keepdims=True)
        above = jnp.where(at, 1.0, above)
        split = jnp.where(at, 0.0, v) - (b / jnp.where(odd, a, 1.0)) * above
        v = jnp.where(odd, split, v)
        pivot = jnp.sum(jnp.where(lane == row, v, 0.0), axis=1, keepdims=True)
        done.append(v * lax.rsqrt(pivot))
    return done


def links_kernel(n_inner, place, bins, pairs, hots, links):
    column, group = place[0], place[1]
    odd = column % 2
    step = 2 * odd - 1
    others = (column, column - step, column + step)
    bin_of = lax.broadcasted_iota(jnp.int32, (BINS_COL, 1), 0)

    def hot(values, base):
        return jnp.where(values == bin_of + base, 1.0, 0.0)

    def bins_at(l, c):
        return bins[pl.ds(l * n_inner + c, 1), :]

    rows = jnp.concatenate(
        [hot(bins_at(group ^ r, column), column * BINS_COL) for r in range(4)], axis=1
    )
    left, right = pairs[0:1, :], pairs[1:2, :]
    base = column * BINS_COL
    left_mine, right_mine = hot(left, base), hot(right, base)
    for i, other in enumerate(others):
        base = other * BINS_COL
        count = nt(hot(left, base), right_mine, None) + nt(hot(right, base), left_mine, None)
        linked = jnp.where(count > 0.5, 1.0, 0.0)
        links[i] = nn(linked, rows, None)
        theirs = bins_at(group, jnp.clip(other, 0, n_inner - 1))
        hots[i] = hot(theirs, base)


def turn_kernel(weights, r0, r1, turned, norms, start):
    span = r0.shape[0]
    for i, rows in enumerate((r0, r1)):
        at = slice(i * span, (i + 1) * span)
        value = rows[...].T
        turned[:, at] = value
        wide = value.astype(F32)
        norms[:, at] = jnp.sum(wide * wide, axis=0, keepdims=True)
        start[:, at] = nn(weights[...], value, None)


def tile_kernel(scale, places, hots, all_links, *refs):
    count = len(places)
    groups, others, outs = refs[:4], refs[4:4 + count], refs[-2 * count - 1:]
    degree = refs[4 + count:-2 * count - 1]
    span = groups[0].shape[1]
    totals = [degree[0][:, span * i:span * (i + 1)] if degree else 0.0 for i in range(2)]
    for k, (kind, part) in enumerate(places):
        x = others[k][...]
        wide = x.astype(F32)
        own = jnp.sum(wide * wide, axis=1, keepdims=True)
        size = x.shape[0]
        hot = hots[kind, :, part:part + size].T
        high, low = outs[2 * k:2 * k + 2]
        for i in range(2):
            turned, norms = groups[2 * i:2 * i + 2]
            at = slice(i * span, (i + 1) * span)
            mask = nn(hot, all_links[kind, :, at], None)
            distance = own + norms[...] - 2.0 * nn(x, turned[...], None)
            value = mask * jnp.exp(distance * scale)
            top = value.astype(BF16)
            high[:, at] = top
            low[:, at] = (value - top.astype(F32)).astype(BF16)
            totals[i] = totals[i] + jnp.sum(value, axis=0, keepdims=True)
    outs[-1][...] = jnp.concatenate(totals, axis=1)


def send_back_kernel(degree, got, start_a, start_b, *refs):
    tiles, (inv_root, own, near, far) = refs[:-4], refs[-4:]
    width, size = own.shape
    other = jnp.concatenate([got[:, size * i:size * (i + 1)] for i in (2, 3, 0, 1)], axis=1)
    scale = lax.rsqrt(degree[...] + other)
    inv_root[...] = scale[:, :size]
    vectors = (jnp.concatenate([start_a[...], start_b[...]], axis=1) * scale)
    top = vectors.astype(BF16)
    low = (vectors - top.astype(F32)).astype(BF16)
    both = jnp.concatenate([top, low], axis=0)
    pieces = []
    for i in range(len(tiles) // 2):
        high = tiles[2 * i][...]
        piece = nt(both, high, None)
        pieces.append(piece[:width] + piece[width:] + nt(top, tiles[2 * i + 1][...], None))
    own[...] = pieces[0]
    cut = (len(pieces) + 1) // 2
    near[...] = jnp.concatenate(pieces[1:cut], axis=1)
    far[...] = jnp.concatenate(pieces[cut:], axis=1)


def apply_kernel(*refs):
    vectors, tiles, (keep, send) = refs[:3], refs[3:-2], refs[-2:]
    width = vectors[0].shape[0]
    half = keep.shape[1]
    total = None
    count = len(tiles) // 2
    strip = jnp.concatenate([v[...] for v in vectors], axis=1)
    top = strip.astype(BF16)
    low = (strip - top.astype(F32)).astype(BF16)
    both = jnp.concatenate([top, low], axis=0)
    at = 0
    for i in range(count):
        high_tile, low_tile = tiles[2 * i][...], tiles[2 * i + 1][...]
        size = high_tile.shape[0]
        piece = nn(both[:, at:at + size], high_tile, None)
        piece = piece[:width] + piece[width:] + nn(top[:, at:at + size], low_tile, None)
        total = piece if total is None else total + piece
        at += size
    size = half // 2
    keep[:, :size], keep[:, size:] = total[:, :size], total[:, half:half + size]
    send[:, :size], send[:, size:] = total[:, size:half], total[:, half + size:]


def fold(upper, lower):
    width = upper.shape[0]
    row = lax.broadcasted_iota(jnp.int32, upper.shape, 0)
    col = lax.broadcasted_iota(jnp.int32, upper.shape, 1)
    both = jnp.where(col >= row, upper, lower)
    flat = jnp.concatenate([both[8 * i:8 * i + 8, :] for i in range(width // 8)], axis=1)
    return flat, jnp.sum(jnp.where(col == row, lower, 0.0), axis=0, keepdims=True)


def unfold(flat, diagonal):
    width = diagonal.shape[1]
    both = jnp.concatenate([flat[:, width * i:width * (i + 1)] for i in range(width // 8)], axis=0)
    turned = both.T
    row = lax.broadcasted_iota(jnp.int32, both.shape, 0)
    col = lax.broadcasted_iota(jnp.int32, both.shape, 1)
    upper = jnp.where(col >= row, both, turned)
    return upper, jnp.where(col < row, both, jnp.where(col == row, diagonal, turned))


def gram_kernel(mine, got, inv_root, start, image, image_next, packed):
    value = inv_root[...] * (mine[...] + got[...])
    image_next[...] = value
    first, begin = image[...], start[...]
    width = first.shape[0]
    half = width // 2
    packed[:8, :], row_a = fold(nt(begin, begin), nt(begin, first))
    packed[8:16, :], row_b = fold(nt(first, first), nt(first, value))
    last = nt(value, value)
    block = jnp.concatenate([last[:half, :], last[half:, half:]], axis=1)
    rows = jnp.concatenate([row_a, row_b, jnp.zeros((6, width), F32)], axis=0)
    packed[16:, :] = jnp.concatenate([block[:8, :], block[8:, :], rows], axis=1)


def spread_kernel(mine, got, copies):
    copies[...] = jnp.broadcast_to((mine[...] + got[...])[None], copies.shape)


def last_kernel(parts, v0, v1, v2, basis, coefficients):
    packed = jnp.sum(parts[...], axis=0)
    width = v0.shape[0]
    half = width // 2
    span = width + half
    rows = packed[16:, 2 * span:2 * span + width]
    m_00, m_01 = unfold(packed[:8, :], rows[0:1, :])
    m_11, m_12 = unfold(packed[8:16, :], rows[1:2, :])
    block = jnp.concatenate([packed[16:, :span], packed[16:, span:2 * span]], axis=0)
    corner = block[:, half:width].T
    m_22 = jnp.concatenate(
        [block[:, :width], jnp.concatenate([corner, block[:, width:]], axis=1)], axis=0
    )
    blank = jnp.zeros((width, LANES - 3 * width), F32)
    gram = jnp.concatenate(
        [
            jnp.concatenate([m_00, m_01, m_11, blank], axis=1),
            jnp.concatenate([m_01, m_11, m_12, blank], axis=1),
            jnp.concatenate([m_11, m_12, m_22, blank], axis=1),
        ],
        axis=0,
    )
    rows = 3 * width
    row = lax.broadcasted_iota(jnp.int32, gram.shape, 0)
    col = lax.broadcasted_iota(jnp.int32, gram.shape, 1)
    diagonal = jnp.where(row == col, gram, 0.0)
    across = jnp.sum(diagonal, axis=0, keepdims=True)
    root = lax.rsqrt(jnp.where(col[:1, :] < rows, across, 1.0))
    gram = gram * lax.rsqrt(jnp.sum(diagonal, axis=1, keepdims=True)) * root
    groups = [gram[8 * i:8 * i + 8, :] for i in range(rows // 8)]
    whole = jnp.concatenate(eliminate(groups), axis=0)[:, :rows]
    row = lax.broadcasted_iota(jnp.int32, (rows, rows), 0)
    col = lax.broadcasted_iota(jnp.int32, (rows, rows), 1)
    root = root[:, :rows]
    upper = jnp.where(col >= row, whole, 0.0) / root
    pivot = jnp.sum(jnp.where(col == row, whole, 0.0), axis=1, keepdims=True)
    inverse = jnp.where(col < row, whole, jnp.where(col == row, 1.0 / pivot, 0.0)) * root
    basis[...] = nn(inverse, jnp.concatenate([v0[...], v1[...], v2[...]], axis=0))

    def block(value, i, j):
        return value[width * i:width * (i + 1), width * j:width * (j + 1)]

    z_00, z_11 = block(inverse, 0, 0), block(inverse, 1, 1)
    r_01, r_11 = block(upper, 0, 1), block(upper, 1, 1)
    first = nt(jnp.concatenate([r_01, r_11], axis=0), z_00)
    mixed = block(upper, 1, 2) - nn(r_11, tn(z_00, r_01))
    second = nt(jnp.concatenate([mixed, block(upper, 2, 2)], axis=0), z_11)
    coefficients[0] = first[:width]
    coefficients[1] = first[width:]
    coefficients[2] = second[:width]
    coefficients[3] = second[width:]


def routes(n_loop, n_inner):
    def build(target):
        pairs = []
        for l in range(n_loop):
            for c in range(n_inner):
                m, d = target(l, c)
                if 0 <= d < n_inner:
                    pairs.append((l * n_inner + c, m * n_inner + d))
        return pairs

    def far(l, c):
        d = c + 1 if c % 2 else c - 1
        return (l, d) if 0 <= d < n_inner else (l ^ 1, c)

    return {
        "core": build(lambda l, c: (l ^ 1, c)),
        "row": build(lambda l, c: (l ^ 2, c)),
        "near": build(lambda l, c: (l, c ^ 1)),
        "far": build(far),
        "relay": build(lambda l, c: (l, c - 2 if c % 2 else c + 2)),
    }


def steps(snapshots, bins, pairs, start_weights):
    row_count, features = snapshots.shape
    width = start_weights.shape[1]
    n_row = lax.axis_size("row")
    n_loop = n_row * lax.axis_size("core")
    n_inner = lax.axis_size("inner")
    column = lax.axis_index("inner")
    group = lax.axis_index(("row", "core"))
    route = routes(n_loop, n_inner)

    def move(value, name):
        return lax.ppermute(value, ALL, route[name])

    half = row_count // 2
    across = move(snapshots, "row")
    first_half, later = lax.optimization_barrier((snapshots[:half], snapshots))
    near_a = move(first_half, "near")
    mate = move(snapshots, "core")
    far_b = move(later[half:], "far")
    near_b = move(later[half:], "near")
    far_a = move(near_a, "relay")
    across_mate = move(across, "core")

    place = jnp.where(jnp.arange(2) == 0, column, group).astype(jnp.int32)
    hots, links = call(
        functools.partial(links_kernel, n_inner),
        [((3, BINS_COL, row_count), F32), ((3, BINS_COL, n_loop * row_count), F32)],
        place, bins.reshape(n_loop * n_inner, row_count), pairs.T,
        scalars=1,
    )

    span = n_loop * row_count
    turn_outs = [((features, span // 2), BF16), ((1, span // 2), F32), ((width, span // 2), F32)]
    turned_a, norms_a, start_a = call(
        turn_kernel, turn_outs, start_weights.T, snapshots, mate
    )
    turned_b, norms_b, start_b = call(turn_kernel, turn_outs, start_weights.T, across, across_mate)
    made = {}
    degree = ()
    for blocks in (
        (((0, 0), snapshots), ((1, 0), near_a)),
        (((2, 0), far_a),),
        (((1, half), near_b), ((2, half), far_b)),
    ):
        places = tuple(place for place, rows in blocks)
        outs = [((rows.shape[0], span), BF16) for place, rows in blocks for _ in range(2)]
        *out, total = call(
            functools.partial(tile_kernel, -3.0 / features, places),
            outs + [((1, span), F32)],
            hots, links, turned_a, norms_a, turned_b, norms_b,
            *(rows for place, rows in blocks), *degree,
        )
        degree = (total,)
        made.update((place, out[2 * i:2 * i + 2]) for i, place in enumerate(places))
    (degree,) = degree
    tiles = sum((made[place] for place in sorted(made)), [])

    got = move(degree, "core")
    degree = degree + jnp.concatenate(
        [got[:, row_count * i:row_count * (i + 1)] for i in (1, 0, 3, 2)], axis=1
    )
    block = ((width, row_count), F32)
    inv_root, own, near, far = call(
        send_back_kernel,
        [((1, row_count), F32), block, block, block],
        degree, move(degree, "row"), start_a, start_b, *tiles,
    )
    start = start_a[:, :row_count]
    near = move(near, "near")
    far = move(far, "far")
    image_1 = inv_root * (own + near + far)

    scaled = inv_root * image_1
    near = move(scaled, "near")
    far = move(scaled, "far")
    keep, send = call(
        apply_kernel,
        [((width, span // 2), F32)] * 2,
        scaled, near, far, *tiles,
    )
    keep = keep + move(send, "core")
    mine, got = keep[:, :row_count], move(keep[:, row_count:], "row")
    image_2, packed = call(
        gram_kernel,
        [((width, row_count), F32), ((24, LANES), F32)],
        mine, got, inv_root, start, image_1,
    )
    (copies,) = call(
        spread_kernel,
        [((n_row * n_inner,) + packed.shape, F32)],
        packed, move(packed, "core"),
    )
    parts = lax.all_to_all(copies, ("row", "inner"), 0, 0)
    basis, coefficients = call(
        last_kernel,
        [((3 * width, row_count), F32), ((4, width, width), F32)],
        parts, start, image_1, image_2,
        final=True,
    )
    return basis.T, coefficients


def solution(mesh):
    n_loop, n_inner = mesh.shape["loop"], mesh.shape["inner"]
    fine = Mesh(mesh.devices.reshape(n_loop // 2, 2, n_inner), ALL)
    in_specs = (P(ALL, None), P(), P(), P())
    out_specs = (P(ALL, None), P())
    return jax.shard_map(steps, mesh=fine, in_specs=in_specs, out_specs=out_specs, check_vma=False)
```

```python
import functools

import jax
import jax.numpy as jnp
from jax import lax
from jax.experimental import pallas as pl
from jax.experimental.pallas import tpu as pltpu
from jax.sharding import Mesh, PartitionSpec as P

BINS_COL = 8
LANES = 128
KERNEL_VMEM = 16 * 2**20
ALL = ("row", "core", "inner")
HI = lax.Precision.HIGHEST
F32 = jnp.float32
BF16 = jnp.bfloat16


def nt(left, right, precision=HI):
    return lax.dot_general(
        left, right, (((1,), (1,)), ((), ())), precision=precision, preferred_element_type=F32
    )


def nn(left, right, precision=HI):
    return lax.dot_general(
        left, right, (((1,), (0,)), ((), ())), precision=precision, preferred_element_type=F32
    )


def tn(left, right):
    return nn(left.T, right)


def call(kernel, outs, *args, final=False, scalars=0):
    result = jax.ShapeDtypeStruct if final else pltpu.VMEM
    vectors = [pltpu.with_memory_space_constraint(a, pltpu.VMEM) for a in args[scalars:]]
    return pl.pallas_call(
        kernel,
        out_shape=[result(shape, kind) for shape, kind in outs],
        in_specs=[pl.BlockSpec(memory_space=pltpu.SMEM)] * scalars
        + [pl.BlockSpec(memory_space=pltpu.VMEM)] * len(vectors),
        compiler_params=pltpu.CompilerParams(vmem_limit_bytes=KERNEL_VMEM),
    )(*args[:scalars], *vectors)


def spread(value):
    return jnp.broadcast_to(value, (8, LANES))


def eliminate(groups):
    sub = lax.broadcasted_iota(jnp.int32, (8, LANES), 0)
    lane = lax.broadcasted_iota(jnp.int32, (8, LANES), 1)
    g = list(groups)
    count = 8 * len(g)

    def lane_of(value, j):
        return spread(value[:, j:j + 1])

    def row_of(value, s):
        return spread(value[s:s + 1, :])

    p = {}
    for k in range(4):
        col = lane_of(g[0], k)
        for i in range(k + 1):
            p[i, k] = row_of(col, i)
    for j in range(0, count, 4):
        q, s = divmod(j, 8)
        cols = [[lane_of(v, j + k) for v in g[q:]] for k in range(4)]
        rows = [row_of(g[q], s + k) for k in range(4)]
        first_pair = jnp.logical_or(lane == j, lane == j + 1)
        last_pair = jnp.logical_or(lane == j + 2, lane == j + 3)
        pair = jnp.logical_or(first_pair, last_pair)

        inverse = 1.0 / (p[0, 0] * p[1, 1] - p[0, 1] * p[0, 1])
        d0, b0, a0 = p[1, 1] * inverse, p[0, 1] * inverse, p[0, 0] * inverse

        def first_two(x, y):
            return d0 * x - b0 * y, a0 * y - b0 * x

        u2, u3 = first_two(p[0, 2], p[1, 2]), first_two(p[0, 3], p[1, 3])
        a = p[2, 2] - (p[0, 2] * u2[0] + p[1, 2] * u2[1])
        b = p[2, 3] - (p[0, 2] * u3[0] + p[1, 2] * u3[1])
        d = p[3, 3] - (p[0, 3] * u3[0] + p[1, 3] * u3[1])
        inverse = 1.0 / (a * d - b * b)
        d1, b1, a1 = d * inverse, b * inverse, a * inverse

        def last_two(x, y):
            return d1 * x - b1 * y, a1 * y - b1 * x

        n = j + 4
        if n < count:
            r, t = divmod(n, 8)
            c = [[row_of(cols[k][r - q], t + i) for i in range(4)] for k in range(4)]
            w01 = [first_two(c[0][i], c[1][i]) for i in range(4)]
            c2 = [c[2][i] - (c[0][i] * u2[0] + c[1][i] * u2[1]) for i in range(4)]
            c3 = [c[3][i] - (c[0][i] * u3[0] + c[1][i] * u3[1]) for i in range(4)]
            w23 = [last_two(c2[i], c3[i]) for i in range(4)]
            p = {}
            for k in range(4):
                col = lane_of(g[r], n + k)
                for i in range(k + 1):
                    p[i, k] = row_of(col, t + i) - (
                        (c[0][i] * w01[k][0] + c[1][i] * w01[k][1])
                        + (c2[i] * w23[k][0] + c3[i] * w23[k][1])
                    )

        one = jnp.where(lane == j, 1.0, jnp.where(lane == j + 1, 0.0, rows[0]))
        two = jnp.where(lane == j, 0.0, jnp.where(lane == j + 1, 1.0, rows[1]))
        w0, w1 = first_two(one, two)
        third = jnp.where(first_pair, 0.0, rows[2]) - (u2[0] * one + u2[1] * two)
        fourth = jnp.where(first_pair, 0.0, rows[3]) - (u3[0] * one + u3[1] * two)
        three = jnp.where(lane == j + 2, 1.0, jnp.where(lane == j + 3, 0.0, third))
        four = jnp.where(lane == j + 2, 0.0, jnp.where(lane == j + 3, 1.0, fourth))
        w2, w3 = last_two(three, four)
        clear_0, clear_1 = jnp.where(last_pair, 0.0, w0), jnp.where(last_pair, 0.0, w1)
        for i in range(len(g) - q):
            k0, k1 = cols[0][i], cols[1][i]
            k2 = cols[2][i] - (k0 * u2[0] + k1 * u2[1])
            k3 = cols[3][i] - (k0 * u3[0] + k1 * u3[1])
            old = g[q + i]
            new = jnp.where(pair, 0.0, old) - ((k0 * clear_0 + k1 * clear_1) + (k2 * w2 + k3 * w3))
            if i == 0:
                new = jnp.where(sub > s + 3, new, old)
                new = jnp.where(sub == s + 2, third, jnp.where(sub == s + 3, fourth, new))
            g[q + i] = new
    odd = sub % 2 == 1
    done = []
    for q, v in enumerate(g):
        row = sub + 8 * q
        above = pltpu.roll(v, 1, 0)
        at = lane == row - 1
        b = jnp.sum(jnp.where(at, v, 0.0), axis=1, keepdims=True)
        a = jnp.sum(jnp.where(at, above, 0.0), axis=1, keepdims=True)
        above = jnp.where(at, 1.0, above)
        split = jnp.where(at, 0.0, v) - (b / jnp.where(odd, a, 1.0)) * above
        v = jnp.where(odd, split, v)
        pivot = jnp.sum(jnp.where(lane == row, v, 0.0), axis=1, keepdims=True)
        done.append(v * lax.rsqrt(pivot))
    return done


def links_kernel(n_inner, place, bins, pairs, hots, links):
    column, group = place[0], place[1]
    odd = column % 2
    step = 2 * odd - 1
    others = (column, column - step, column + step)
    bin_of = lax.broadcasted_iota(jnp.int32, (BINS_COL, 1), 0)

    def hot(values, base):
        return jnp.where(values == bin_of + base, 1.0, 0.0)

    def bins_at(l, c):
        return bins[pl.ds(l * n_inner + c, 1), :]

    rows = jnp.concatenate(
        [hot(bins_at(group ^ r, column), column * BINS_COL) for r in range(4)], axis=1
    )
    left, right = pairs[0:1, :], pairs[1:2, :]
    base = column * BINS_COL
    left_mine, right_mine = hot(left, base), hot(right, base)
    for i, other in enumerate(others):
        base = other * BINS_COL
        count = nt(hot(left, base), right_mine, None) + nt(hot(right, base), left_mine, None)
        linked = jnp.where(count > 0.5, 1.0, 0.0)
        links[i] = nn(linked, rows, None)
        theirs = bins_at(group, jnp.clip(other, 0, n_inner - 1))
        hots[i] = hot(theirs, base)


def turn_kernel(weights, r0, r1, turned, norms, start):
    span = r0.shape[0]
    for i, rows in enumerate((r0, r1)):
        at = slice(i * span, (i + 1) * span)
        value = rows[...].T
        turned[:, at] = value
        wide = value.astype(F32)
        norms[:, at] = jnp.sum(wide * wide, axis=0, keepdims=True)
        start[:, at] = nn(weights[...], value, None)


def tile_kernel(scale, places, hots, all_links, *refs):
    count = len(places)
    groups, others, outs = refs[:4], refs[4:4 + count], refs[-2 * count - 1:]
    degree = refs[4 + count:-2 * count - 1]
    span = groups[0].shape[1]
    totals = [degree[0][:, span * i:span * (i + 1)] if degree else 0.0 for i in range(2)]
    for k, (kind, part) in enumerate(places):
        x = others[k][...]
        wide = x.astype(F32)
        own = scale * jnp.sum(wide * wide, axis=1, keepdims=True)
        size = x.shape[0]
        hot = hots[kind, :, part:part + size].T
        high, low = outs[2 * k:2 * k + 2]
        for i in range(2):
            turned, norms = groups[2 * i:2 * i + 2]
            at = slice(i * span, (i + 1) * span)
            mask = nn(hot, all_links[kind, :, at], None)
            power = own + scale * norms[...] - (2.0 * scale) * nn(x, turned[...], None)
            value = mask * jnp.exp(power)
            top = value.astype(BF16)
            high[:, at] = top
            low[:, at] = (value - top.astype(F32)).astype(BF16)
            totals[i] = totals[i] + jnp.sum(value, axis=0, keepdims=True)
    outs[-1][...] = jnp.concatenate(totals, axis=1)


def send_back_kernel(degree, got, start_a, start_b, *refs):
    tiles, (inv_root, own, near, far) = refs[:-4], refs[-4:]
    width, size = own.shape
    other = jnp.concatenate([got[:, size * i:size * (i + 1)] for i in (2, 3, 0, 1)], axis=1)
    scale = lax.rsqrt(degree[...] + other)
    inv_root[...] = scale[:, :size]
    vectors = (jnp.concatenate([start_a[...], start_b[...]], axis=1) * scale)
    top = vectors.astype(BF16)
    low = (vectors - top.astype(F32)).astype(BF16)
    both = jnp.concatenate([top, low], axis=0)
    pieces = []
    for i in range(len(tiles) // 2):
        high = tiles[2 * i][...]
        piece = nt(both, high, None)
        pieces.append(piece[:width] + piece[width:] + nt(top, tiles[2 * i + 1][...], None))
    own[...] = pieces[0]
    cut = (len(pieces) + 1) // 2
    near[...] = jnp.concatenate(pieces[1:cut], axis=1)
    far[...] = jnp.concatenate(pieces[cut:], axis=1)


def apply_kernel(*refs):
    vectors, tiles, (keep, send) = refs[:3], refs[3:-2], refs[-2:]
    width = vectors[0].shape[0]
    half = keep.shape[1]
    total = None
    count = len(tiles) // 2
    strip = jnp.concatenate([v[...] for v in vectors], axis=1)
    top = strip.astype(BF16)
    low = (strip - top.astype(F32)).astype(BF16)
    both = jnp.concatenate([top, low], axis=0)
    at = 0
    for i in range(count):
        high_tile, low_tile = tiles[2 * i][...], tiles[2 * i + 1][...]
        size = high_tile.shape[0]
        piece = nn(both[:, at:at + size], high_tile, None)
        piece = piece[:width] + piece[width:] + nn(top[:, at:at + size], low_tile, None)
        total = piece if total is None else total + piece
        at += size
    size = half // 2
    keep[:, :size], keep[:, size:] = total[:, :size], total[:, half:half + size]
    send[:, :size], send[:, size:] = total[:, size:half], total[:, half + size:]


def fold(upper, lower):
    width = upper.shape[0]
    row = lax.broadcasted_iota(jnp.int32, upper.shape, 0)
    col = lax.broadcasted_iota(jnp.int32, upper.shape, 1)
    both = jnp.where(col >= row, upper, lower)
    flat = jnp.concatenate([both[8 * i:8 * i + 8, :] for i in range(width // 8)], axis=1)
    return flat, jnp.sum(jnp.where(col == row, lower, 0.0), axis=0, keepdims=True)


def unfold(flat, diagonal):
    width = diagonal.shape[1]
    both = jnp.concatenate([flat[:, width * i:width * (i + 1)] for i in range(width // 8)], axis=0)
    turned = both.T
    row = lax.broadcasted_iota(jnp.int32, both.shape, 0)
    col = lax.broadcasted_iota(jnp.int32, both.shape, 1)
    upper = jnp.where(col >= row, both, turned)
    return upper, jnp.where(col < row, both, jnp.where(col == row, diagonal, turned))


def gram_kernel(mine, got, inv_root, start, image, image_next, packed):
    value = inv_root[...] * (mine[...] + got[...])
    image_next[...] = value
    first, begin = image[...], start[...]
    width = first.shape[0]
    half = width // 2
    packed[:8, :], row_a = fold(nt(begin, begin), nt(begin, first))
    packed[8:16, :], row_b = fold(nt(first, first), nt(first, value))
    last = nt(value, value)
    block = jnp.concatenate([last[:half, :], last[half:, half:]], axis=1)
    rows = jnp.concatenate([row_a, row_b, jnp.zeros((6, width), F32)], axis=0)
    packed[16:, :] = jnp.concatenate([block[:8, :], block[8:, :], rows], axis=1)


def spread_kernel(mine, got, copies):
    copies[...] = jnp.broadcast_to((mine[...] + got[...])[None], copies.shape)


def last_kernel(parts, v0, v1, v2, basis, coefficients):
    packed = jnp.sum(parts[...], axis=0)
    width = v0.shape[0]
    half = width // 2
    span = width + half
    rows = packed[16:, 2 * span:2 * span + width]
    m_00, m_01 = unfold(packed[:8, :], rows[0:1, :])
    m_11, m_12 = unfold(packed[8:16, :], rows[1:2, :])
    block = jnp.concatenate([packed[16:, :span], packed[16:, span:2 * span]], axis=0)
    corner = block[:, half:width].T
    m_22 = jnp.concatenate(
        [block[:, :width], jnp.concatenate([corner, block[:, width:]], axis=1)], axis=0
    )
    blank = jnp.zeros((width, LANES - 3 * width), F32)
    gram = jnp.concatenate(
        [
            jnp.concatenate([m_00, m_01, m_11, blank], axis=1),
            jnp.concatenate([m_01, m_11, m_12, blank], axis=1),
            jnp.concatenate([m_11, m_12, m_22, blank], axis=1),
        ],
        axis=0,
    )
    rows = 3 * width
    row = lax.broadcasted_iota(jnp.int32, gram.shape, 0)
    col = lax.broadcasted_iota(jnp.int32, gram.shape, 1)
    diagonal = jnp.where(row == col, gram, 0.0)
    across = jnp.sum(diagonal, axis=0, keepdims=True)
    root = lax.rsqrt(jnp.where(col[:1, :] < rows, across, 1.0))
    gram = gram * lax.rsqrt(jnp.sum(diagonal, axis=1, keepdims=True)) * root
    groups = [gram[8 * i:8 * i + 8, :] for i in range(rows // 8)]
    whole = jnp.concatenate(eliminate(groups), axis=0)[:, :rows]
    row = lax.broadcasted_iota(jnp.int32, (rows, rows), 0)
    col = lax.broadcasted_iota(jnp.int32, (rows, rows), 1)
    root = root[:, :rows]
    upper = jnp.where(col >= row, whole, 0.0) / root
    pivot = jnp.sum(jnp.where(col == row, whole, 0.0), axis=1, keepdims=True)
    inverse = jnp.where(col < row, whole, jnp.where(col == row, 1.0 / pivot, 0.0)) * root
    basis[...] = nn(inverse, jnp.concatenate([v0[...], v1[...], v2[...]], axis=0))

    def block(value, i, j):
        return value[width * i:width * (i + 1), width * j:width * (j + 1)]

    z_00, z_11 = block(inverse, 0, 0), block(inverse, 1, 1)
    r_01, r_11 = block(upper, 0, 1), block(upper, 1, 1)
    first = nt(jnp.concatenate([r_01, r_11], axis=0), z_00)
    mixed = block(upper, 1, 2) - nn(r_11, tn(z_00, r_01))
    second = nt(jnp.concatenate([mixed, block(upper, 2, 2)], axis=0), z_11)
    coefficients[0] = first[:width]
    coefficients[1] = first[width:]
    coefficients[2] = second[:width]
    coefficients[3] = second[width:]


def routes(n_loop, n_inner):
    def build(target):
        pairs = []
        for l in range(n_loop):
            for c in range(n_inner):
                m, d = target(l, c)
                if 0 <= d < n_inner:
                    pairs.append((l * n_inner + c, m * n_inner + d))
        return pairs

    def far(l, c):
        d = c + 1 if c % 2 else c - 1
        return (l, d) if 0 <= d < n_inner else (l ^ 1, c)

    return {
        "core": build(lambda l, c: (l ^ 1, c)),
        "row": build(lambda l, c: (l ^ 2, c)),
        "near": build(lambda l, c: (l, c ^ 1)),
        "far": build(far),
        "relay": build(lambda l, c: (l, c - 2 if c % 2 else c + 2)),
    }


def steps(snapshots, bins, pairs, start_weights):
    row_count, features = snapshots.shape
    width = start_weights.shape[1]
    n_row = lax.axis_size("row")
    n_loop = n_row * lax.axis_size("core")
    n_inner = lax.axis_size("inner")
    column = lax.axis_index("inner")
    group = lax.axis_index(("row", "core"))
    route = routes(n_loop, n_inner)

    def move(value, name):
        return lax.ppermute(value, ALL, route[name])

    half = row_count // 2
    across = move(snapshots, "row")
    first_half, later = lax.optimization_barrier((snapshots[:half], snapshots))
    near_a = move(first_half, "near")
    mate = move(snapshots, "core")
    far_b = move(later[half:], "far")
    near_b = move(later[half:], "near")
    far_a = move(near_a, "relay")
    across_mate = move(across, "core")

    place = jnp.where(jnp.arange(2) == 0, column, group).astype(jnp.int32)
    hots, links = call(
        functools.partial(links_kernel, n_inner),
        [((3, BINS_COL, row_count), F32), ((3, BINS_COL, n_loop * row_count), F32)],
        place, bins.reshape(n_loop * n_inner, row_count), pairs.T,
        scalars=1,
    )

    span = n_loop * row_count
    turn_outs = [((features, span // 2), BF16), ((1, span // 2), F32), ((width, span // 2), F32)]
    turned_a, norms_a, start_a = call(
        turn_kernel, turn_outs, start_weights.T, snapshots, mate
    )
    turned_b, norms_b, start_b = call(turn_kernel, turn_outs, start_weights.T, across, across_mate)
    made = {}
    degree = ()
    for blocks in (
        (((0, 0), snapshots), ((1, 0), near_a)),
        (((2, 0), far_a),),
        (((1, half), near_b), ((2, half), far_b)),
    ):
        places = tuple(place for place, rows in blocks)
        outs = [((rows.shape[0], span), BF16) for place, rows in blocks for _ in range(2)]
        *out, total = call(
            functools.partial(tile_kernel, -3.0 / features, places),
            outs + [((1, span), F32)],
            hots, links, turned_a, norms_a, turned_b, norms_b,
            *(rows for place, rows in blocks), *degree,
        )
        degree = (total,)
        made.update((place, out[2 * i:2 * i + 2]) for i, place in enumerate(places))
    (degree,) = degree
    tiles = sum((made[place] for place in sorted(made)), [])

    got = move(degree, "core")
    degree = degree + jnp.concatenate(
        [got[:, row_count * i:row_count * (i + 1)] for i in (1, 0, 3, 2)], axis=1
    )
    block = ((width, row_count), F32)
    inv_root, own, near, far = call(
        send_back_kernel,
        [((1, row_count), F32), block, block, block],
        degree, move(degree, "row"), start_a, start_b, *tiles,
    )
    start = start_a[:, :row_count]
    near = move(near, "near")
    far = move(far, "far")
    image_1 = inv_root * (own + near + far)

    scaled = inv_root * image_1
    near = move(scaled, "near")
    far = move(scaled, "far")
    keep, send = call(
        apply_kernel,
        [((width, span // 2), F32)] * 2,
        scaled, near, far, *tiles,
    )
    keep = keep + move(send, "core")
    mine, got = keep[:, :row_count], move(keep[:, row_count:], "row")
    image_2, packed = call(
        gram_kernel,
        [((width, row_count), F32), ((24, LANES), F32)],
        mine, got, inv_root, start, image_1,
    )
    (copies,) = call(
        spread_kernel,
        [((n_row * n_inner,) + packed.shape, F32)],
        packed, move(packed, "core"),
    )
    parts = lax.all_to_all(copies, ("row", "inner"), 0, 0)
    basis, coefficients = call(
        last_kernel,
        [((3 * width, row_count), F32), ((4, width, width), F32)],
        parts, start, image_1, image_2,
        final=True,
    )
    return basis.T, coefficients


def solution(mesh):
    n_loop, n_inner = mesh.shape["loop"], mesh.shape["inner"]
    fine = Mesh(mesh.devices.reshape(n_loop // 2, 2, n_inner), ALL)
    in_specs = (P(ALL, None), P(), P(), P())
    out_specs = (P(ALL, None), P())
    return jax.shard_map(steps, mesh=fine, in_specs=in_specs, out_specs=out_specs, check_vma=False)
```
